32 devices in a mesh: ctx: 16 (over z, x, core), head: 2 (over y).
Axes of the slice: x: 2, y: 2, z: 4, core: 2. Of those that a mesh axis runs over, the one named last changes fastest.
Arguments:
- inputs: bfloat16 [2048, 4096], P('ctx', 'head'), may hold values from -60 to 60
- out_grad: bfloat16 [2048, 4096], P('ctx', 'head'), may hold values from -6 to 6
- norm_gain: float32 [4096], replicated, may hold values from 0.5 to 1.5
- w_query: bfloat16 [4096, 4096], P(None, 'head'), may hold values from -2 to 2
- w_key: bfloat16 [4096, 1024], P(None, 'head'), may hold values from -2 to 2
- w_value: bfloat16 [4096, 1024], P(None, 'head'), may hold values from -0.09375 to 0.09375
- w_out: bfloat16 [4096, 4096], P('head'), may hold values from -0.09375 to 0.09375
- record_lengths: int32 [8], replicated, may hold values from 1 to 1024, 2048 in all
- block_order: int32 [32], replicated, may hold values from 0 to 31, each once
Outputs:
- input_grad: bfloat16 [2048, 4096], P('ctx', 'head')
- saliency: float32 [2048], P('ctx')
The draws below stay inside these ranges and needn't reach their ends.
Inputs may be any that keep to these rules, and one draw needn't show every extreme that they name: `record_lengths`: record lengths sum to 2048. `block_order`: each number once.
All inputs are finite; a program needn't handle non-finite values.
Results may differ from the reference program's by a relative error of at most 0.007.
Values may be sent and summed in bfloat16 or wider, within the bound.
A program may use at most 128 MiB of HBM per device.

```python
import math
import jax
import jax.numpy as jnp
import numpy as np
from jax import lax

D = 4096
HEADS = 32
KV_HEADS = 8
HEAD_DIM = 128
BLOCK = 64
RECORDS = 8
BLOCKS = 32
SEQ = 2048
MOST_REC = 1024


def shared_projections(key):
    base = jax.random.fold_in(key, 7)
    key_weights = jax.random.normal(jax.random.fold_in(base, 1), (D, KV_HEADS * HEAD_DIM), jnp.float32) * D ** (-0.5)
    fresh = jax.random.normal(jax.random.fold_in(base, 2), (D, HEADS * HEAD_DIM), jnp.float32) * D ** (-0.5)
    query_weights = fresh
    return (jnp.clip(query_weights, -2.0, 2.0), jnp.clip(key_weights, -2.0, 2.0))


def draw_w_query(key, part):
    return shared_projections(key)[0].astype(jnp.bfloat16)


def draw_w_key(key, part):
    return shared_projections(key)[1].astype(jnp.bfloat16)


def draw_inputs(key, part):
    base = jax.random.fold_in(key, 31)
    row_scale = jnp.exp(jax.random.uniform(jax.random.fold_in(base, 1), (SEQ, 1), jnp.float32, 0.0, math.log(10.0)))
    column_scale = jnp.exp(jax.random.uniform(jax.random.fold_in(base, 2), (1, D), jnp.float32, -0.7, 0.7))
    noise = jax.random.normal(jax.random.fold_in(base, 3), (SEQ, D), jnp.float32)
    return jnp.clip(noise * row_scale * column_scale, -60.0, 60.0).astype(jnp.bfloat16)


def shard_levels(own_key, shape, cuts, low, largest):
    loudness = 1.0
    for axis_at, parts in cuts:
        heights = jax.random.uniform(jax.random.fold_in(jax.random.fold_in(own_key, 6), axis_at), (parts,), jnp.float32, low / len(cuts), largest / len(cuts))
        loudness = loudness * jnp.repeat(jnp.exp(heights), shape[axis_at] // parts).reshape((-1,) + (1,) * (len(shape) - 1 - axis_at))
    return loudness


def split_up(number_of, total, limit, skew):
    portions = [(1 << 20) // math.isqrt(rank ** skew) + 1 for rank in range(2, number_of + 1)]
    spare, given = total - limit - (number_of - 1), [1] * (number_of - 1)
    while spare > 0:
        candidates = [i for i in range(number_of - 1) if given[i] < limit]
        whole, remaining = sum([portions[i] for i in candidates]), spare
        for i in candidates:
            more = min(limit - given[i], max(1, remaining * portions[i] // whole), spare)
            given[i] = given[i] + more
            spare = spare - more
    return np.array([limit] + given)


def ragged_sizes(key, count, total, limit, skew):
    if count == 2:
        one = jax.random.randint(key, (), max(1, total - limit), min(limit, total - 1) + 1)
        return jnp.stack([one, total - one])
    sizes = jnp.asarray(split_up(count, total, limit, skew), jnp.int32)
    couples = (count - 1) // 2
    giver, receiver = sizes[1:1 + 2 * couples:2], sizes[2:2 + 2 * couples:2]
    room = jnp.minimum(giver - 1, limit - receiver)
    shifted = jax.random.randint(jax.random.fold_in(key, 1), (couples,), 0, 1 << 20) % (room + 1)
    sizes = sizes.at[1:1 + 2 * couples:2].set(giver - shifted).at[2:2 + 2 * couples:2].set(receiver + shifted)
    return sizes[jax.random.permutation(jax.random.fold_in(key, 2), count)]


def gaussian(own_key, dims, width, reach, shards=(), kind=jnp.bfloat16):
    array = width * jax.random.normal(own_key, dims, jnp.float32)
    if shards:
        array = array * shard_levels(own_key, dims, shards, -0.22, 0.18)
    return jnp.clip(array, -reach, reach).astype(kind)


def setup_inputs(seed: int = 0) -> dict:
    streams_of = jax.random.split(jax.random.key(seed), 10)
    inputs = draw_inputs(jax.random.fold_in(streams_of[9], 71), 0)
    out_grad = gaussian(streams_of[1], (SEQ, D), 1.0, 6.0, ((0, 16), (1, 2)))
    norm_gain = jnp.clip(1.0 + 0.1 * jax.random.normal(streams_of[2], (D,), jnp.float32), 0.5, 1.5)
    w_query = draw_w_query(jax.random.fold_in(streams_of[9], 71), 0)
    w_key = draw_w_key(jax.random.fold_in(streams_of[9], 71), 0)
    w_value = gaussian(streams_of[5], (D, KV_HEADS * HEAD_DIM), D ** -0.5, 0.09375, ((1, 2),))
    w_out = gaussian(streams_of[6], (HEADS * HEAD_DIM, D), (HEADS * HEAD_DIM) ** -0.5, 0.09375, ((0, 2),))
    record_lengths = ragged_sizes(streams_of[7], RECORDS, SEQ, MOST_REC, 2).astype(jnp.int32)
    block_order = jax.random.permutation(streams_of[8], BLOCKS).astype(jnp.int32)
    return dict(inputs=inputs, out_grad=out_grad, norm_gain=norm_gain, w_query=w_query, w_key=w_key, w_value=w_value, w_out=w_out, record_lengths=record_lengths, block_order=block_order)


def timeline_place(order, lengths):
    stored = jnp.arange(SEQ, dtype=jnp.int32)
    matches = (stored // BLOCK)[:, None] == jnp.arange(BLOCKS, dtype=jnp.int32)[None, :]
    position = (lax.optimization_barrier(jnp.sum(jnp.where(matches, order[None, :], 0), axis=1)).astype(jnp.int32) * BLOCK + stored % BLOCK).astype(jnp.int32)
    starts = (jnp.cumsum(lengths) - lengths).astype(jnp.int32)
    record = lax.optimization_barrier(jnp.sum((starts[None, :] <= position[:, None]).astype(jnp.int32), axis=1)).astype(jnp.int32)
    return (position, record)

def reference(inputs, out_grad, norm_gain, w_query, w_key, w_value, w_out, record_lengths, block_order):
    per_group = HEADS // KV_HEADS
    score_scale = HEAD_DIM ** (-0.5)
    position, record = timeline_place(block_order, record_lengths)
    allowed = (record[:, None] == record[None, :]) & (position[None, :] <= position[:, None])
    x_full = inputs.astype(jnp.float32)
    root_mean = jnp.sqrt(lax.optimization_barrier(jnp.mean(x_full * x_full, axis=1)) + 1e-05)
    unit_rows = x_full / root_mean[:, None]
    normed = (unit_rows * norm_gain[None, :]).astype(jnp.bfloat16)
    query = jnp.dot(normed, w_query, preferred_element_type=jnp.float32).astype(jnp.bfloat16)
    keys = jnp.dot(normed, w_key, preferred_element_type=jnp.float32).astype(jnp.bfloat16)
    values = jnp.dot(normed, w_value, preferred_element_type=jnp.float32).astype(jnp.bfloat16)
    contract = (((1,), (1,)), ((), ()))
    out_dir = lax.dot_general(out_grad, w_out, contract, preferred_element_type=jnp.float32).astype(jnp.bfloat16)
    query_groups = jnp.transpose(query.reshape(SEQ, KV_HEADS, per_group, HEAD_DIM), (1, 0, 2, 3))
    dir_groups = jnp.transpose(out_dir.reshape(SEQ, KV_HEADS, per_group, HEAD_DIM), (1, 0, 2, 3))
    key_groups = jnp.transpose(keys.reshape(SEQ, KV_HEADS, HEAD_DIM), (1, 0, 2))
    value_groups = jnp.transpose(values.reshape(SEQ, KV_HEADS, HEAD_DIM), (1, 0, 2))

    def one_group(operands):
        query_g, dir_g, key_g, value_g = operands
        query_f = query_g.astype(jnp.float32)
        dir_f = dir_g.astype(jnp.float32)
        key_f = key_g.astype(jnp.float32)
        value_f = value_g.astype(jnp.float32)
        scores = jnp.einsum('igd,jd->gij', query_f, key_f) * score_scale
        scores = jnp.where(allowed[None, :, :], scores, -1e+30)
        row_max = lax.optimization_barrier(jnp.max(scores, axis=-1))
        log_total = row_max + jnp.log(lax.optimization_barrier(jnp.sum(jnp.exp(scores - row_max[..., None]), axis=-1)))
        probs = jnp.exp(scores - log_total[..., None])
        prob_half = probs.astype(jnp.bfloat16)
        attended = jnp.einsum('gij,jd->igd', prob_half.astype(jnp.float32), value_f).astype(jnp.bfloat16)
        delta = jnp.transpose(lax.optimization_barrier(jnp.sum(dir_f * attended.astype(jnp.float32), axis=-1)), (1, 0))
        prob_grad = jnp.einsum('igd,jd->gij', dir_f, value_f)
        score_grad = (probs * (prob_grad - delta[:, :, None]) * score_scale).astype(jnp.bfloat16)
        query_grad = jnp.einsum('gij,jd->igd', score_grad.astype(jnp.float32), key_f).astype(jnp.bfloat16)
        key_grad = jnp.einsum('gij,igd->jd', score_grad.astype(jnp.float32), query_f).astype(jnp.bfloat16)
        value_grad = jnp.einsum('gij,igd->jd', prob_half.astype(jnp.float32), dir_f).astype(jnp.bfloat16)
        return (query_grad, key_grad, value_grad)
    query_grad, key_grad, value_grad = lax.map(one_group, (query_groups, dir_groups, key_groups, value_groups))
    query_grad = jnp.transpose(query_grad, (1, 0, 2, 3)).reshape(SEQ, HEADS * HEAD_DIM)
    key_grad = jnp.transpose(key_grad, (1, 0, 2)).reshape(SEQ, KV_HEADS * HEAD_DIM)
    value_grad = jnp.transpose(value_grad, (1, 0, 2)).reshape(SEQ, KV_HEADS * HEAD_DIM)
    hidden_grad = lax.dot_general(query_grad, w_query, contract, preferred_element_type=jnp.float32)
    hidden_grad = hidden_grad + lax.dot_general(key_grad, w_key, contract, preferred_element_type=jnp.float32)
    hidden_grad = hidden_grad + lax.dot_general(value_grad, w_value, contract, preferred_element_type=jnp.float32)
    scaled = hidden_grad * norm_gain[None, :]
    inner = lax.optimization_barrier(jnp.mean(scaled * unit_rows, axis=1))
    input_grad = out_grad.astype(jnp.float32) + (scaled - unit_rows * inner[:, None]) / root_mean[:, None]
    saliency = lax.optimization_barrier(jnp.sum(x_full * input_grad, axis=1))
    return (input_grad.astype(jnp.bfloat16), saliency)
```

```python
import functools

import jax
import jax.numpy as jnp
from jax import lax
from jax.experimental import pallas as pl
from jax.experimental.pallas import tpu as pltpu
from jax.sharding import PartitionSpec as P

HEAD_DIM = 128
BLOCK = 64
SLAB = 4
HALVES = 2
LOG2E = 1.4426950408889634
LN2 = 0.6931471805599453
NT = (((1,), (1,)), ((), ()))
TN = (((0,), (0,)), ((), ()))
F32 = jnp.float32
BF16 = jnp.bfloat16
MESH = pl.DeviceIdType.MESH
VM = pl.BlockSpec(memory_space=pltpu.VMEM)
ANY = pl.BlockSpec(memory_space=pl.ANY)
SM = pl.BlockSpec(memory_space=pltpu.SMEM)
VMEM_LIMIT = 64 * 1024 * 1024 - 128 * 1024


def timeline_place(stored, order_ref, lengths_ref):
    block = jnp.right_shift(stored, 6)
    position = jnp.zeros(stored.shape, jnp.int32)
    for b in range(order_ref.shape[0]):
        position = jnp.where(block == b, order_ref[b], position)
    position = position * BLOCK + (stored & (BLOCK - 1))
    record = jnp.zeros(stored.shape, jnp.int32)
    start = 0
    for r in range(lengths_ref.shape[0]):
        record = record + jnp.where(position >= start, 1, 0)
        start = start + lengths_ref[r]
    return position, record


def coords():
    me = lax.axis_index("ctx")
    return me, me // 4, lax.rem(me // 2, 2), lax.rem(me, 2)


def slot_of(z, x, c):
    return (z * 2 + x) * 2 + c


def enter(nz, nh):
    _, z, x, c = coords()
    head = lax.axis_index("head")
    barrier = pltpu.get_barrier_semaphore()

    def greet(target):
        pl.semaphore_signal(barrier, inc=1, device_id=target, device_id_type=MESH)

    for p in range(1, nh):
        greet({"head": lax.rem(head + p, nh)})
    greet({"ctx": slot_of(z, 1 - x, c)})
    greet({"ctx": slot_of(z, x, 1 - c)})

    @pl.when(z > 0)
    def _():
        greet({"ctx": slot_of(z - 1, x, c)})

    @pl.when(z < nz - 1)
    def _():
        greet({"ctx": slot_of(z + 1, x, c)})

    @pl.when((z > 0) & (z < nz - 1))
    def _():
        pl.semaphore_wait(barrier, nh + 3)

    @pl.when((z == 0) | (z == nz - 1))
    def _():
        pl.semaphore_wait(barrier, nh + 2)


def front_kernel(nz, nh, order_ref, lengths_ref, x_ref, dy_ref, gain_ref,
                 wq_ref, wk_ref, wv_ref, wo_ref,
                 q_out, do_out, kv_out, stat_ref, pq_ref, pk_ref,
                 q_ref, do_ref, kv_ref, wq, wk, wv, wo, xall, dyall, normed,
                 wsem, lsem, osem, ssem, xs, xr, dys, dyr, ks, kr):
    me, z, x, c = coords()
    head = lax.axis_index("head")
    rows, share = x_ref.shape
    dim = nh * share
    hq = q_ref.shape[1]
    width = wk_ref.shape[1]
    loads = [
        pltpu.make_async_copy(a, b, wsem.at[i])
        for i, (a, b) in enumerate(((wk_ref, wk), (wv_ref, wv), (wq_ref, wq), (wo_ref, wo)))
    ]
    for load in loads:
        load.start()
    own = [
        pltpu.make_async_copy(x_ref, xall.at[head], lsem.at[0]),
        pltpu.make_async_copy(dy_ref, dyall.at[head], lsem.at[1]),
    ]
    for copy in own:
        copy.start()
    enter(nz, nh)

    def head_copies(src, dst, send, recv):
        return [
            pltpu.make_async_remote_copy(
                src_ref=src, dst_ref=dst.at[head], send_sem=send.at[p - 1], recv_sem=recv.at[p - 1],
                device_id={"head": lax.rem(head + p, nh)}, device_id_type=MESH)
            for p in range(1, nh)
        ]

    xc = head_copies(x_ref, xall, xs, xr)
    dyc = head_copies(dy_ref, dyall, dys, dyr)
    for copy in xc + dyc:
        copy.start()
    length = kv_ref.shape[0]
    pk_ref[0:1, :], pk_ref[1:2, :] = timeline_place(
        lax.broadcasted_iota(jnp.int32, (1, length), 1), order_ref, lengths_ref)
    pq_ref[:, 0:1], pq_ref[:, 1:2] = timeline_place(
        lax.broadcasted_iota(jnp.int32, (rows, 1), 0) + me * rows, order_ref, lengths_ref)
    own[0].wait()
    for copy in xc:
        copy.wait()
    total = jnp.zeros((rows, 1), F32)
    for j in range(nh):
        v = xall[j].astype(F32)
        total = total + jnp.sum(v * v, axis=1, keepdims=True)
    root = jnp.sqrt(total / dim + 1e-05)
    inv = 1.0 / root
    for j in range(nh):
        cols = slice(j * share, (j + 1) * share)
        normed[:, cols] = (xall[j].astype(F32) * inv * gain_ref[:, cols]).astype(BF16)

    def block(slot):
        return kv_ref.at[pl.ds(pl.multiple_of(slot * rows, rows), rows), :]

    def send(direction, slot, target):
        return pltpu.make_async_remote_copy(
            src_ref=block(slot), dst_ref=block(slot), send_sem=ks.at[direction, slot],
            recv_sem=kr.at[slot], device_id={"ctx": target}, device_id_type=MESH)

    def store(slot):
        return pltpu.make_async_copy(
            block(slot), kv_out.at[pl.ds(pl.multiple_of(slot * rows, rows), rows), :],
            ssem.at[slot])

    def arrived(slot):
        send(0, slot, me).wait_recv()
        store(slot).start()

    mine = pl.ds(pl.multiple_of(me * rows, rows), rows)
    loads[0].wait()
    kv_ref[mine, :width] = jnp.dot(normed[...], wk[...], preferred_element_type=F32).astype(BF16)
    loads[1].wait()
    kv_ref[mine, width:] = jnp.dot(normed[...], wv[...], preferred_element_type=F32).astype(BF16)

    right = slot_of(z + 1, x, c)
    left = slot_of(z - 1, x, c)
    across = slot_of(z, 1 - x, c)
    beside = slot_of(z, x, 1 - c)

    def spread(s, act):
        if s == 0:
            pl.when(z < nz - 1)(lambda: act(send(0, me, right)))
            pl.when(z > 0)(lambda: act(send(1, me, left)))
            act(send(2, me, across))
            act(send(3, me, beside))
            return
        low, high = slot_of(z - s, x, c), slot_of(z + s, x, c)

        @pl.when(z - s >= 0)
        def _():
            if act is start:
                arrived(low)
            pl.when(z < nz - 1)(lambda: act(send(0, low, right)))
            act(send(2, low, across))
            act(send(3, low, beside))

        @pl.when(z + s < nz)
        def _():
            if act is start:
                arrived(high)
            pl.when(z > 0)(lambda: act(send(1, high, left)))
            act(send(2, high, across))
            act(send(3, high, beside))

    def hand_over(s, act):
        def one(slot):
            if act is start:
                arrived(slot)
            act(send(3, slot, beside))

        if s == 0:
            one(slot_of(z, 1 - x, c))
            return
        pl.when(z - s >= 0)(lambda: one(slot_of(z - s, 1 - x, c)))
        pl.when(z + s < nz)(lambda: one(slot_of(z + s, 1 - x, c)))

    def start(copy):
        copy.start()

    def sent(copy):
        copy.wait_send()

    spread(0, start)
    store(me).start()

    loads[2].wait()
    tq = min(512, hq)

    def q_tile(t, carry):
        cols = pl.ds(pl.multiple_of(t * tq, tq), tq)
        q_ref[:, cols] = jnp.dot(normed[...], wq[:, cols], preferred_element_type=F32).astype(BF16)
        return carry

    lax.fori_loop(0, hq // tq, q_tile, 0)
    q_store = pltpu.make_async_copy(q_ref, q_out, osem.at[0])
    q_store.start()
    spread(1, start)

    own[1].wait()
    for copy in dyc:
        copy.wait()
    loads[3].wait()

    def do_tile(t, carry):
        cols = pl.ds(pl.multiple_of(t * tq, tq), tq)
        acc = jnp.zeros((rows, tq), F32)
        for j in range(nh):
            acc = acc + lax.dot_general(
                dyall[j], wo[cols, j * share:(j + 1) * share], NT, preferred_element_type=F32)
        do_ref[:, cols] = acc.astype(BF16)
        return carry

    tiles = hq // tq
    gaps = nz - 2
    for s in range(2, nz):
        lax.fori_loop(tiles * (s - 2) // gaps, tiles * (s - 1) // gaps, do_tile, 0)
        if s == nz - 1:
            do_store = pltpu.make_async_copy(do_ref, do_out, osem.at[1])
            do_store.start()
        spread(s, start)
        hand_over(s - 2, start)

    product = jnp.zeros((rows, 1), F32)
    for j in range(nh):
        product = product + jnp.sum(
            xall[j].astype(F32) * dyall[j].astype(F32), axis=1, keepdims=True)
    stat_ref[:, 0:128] = jnp.broadcast_to(inv, (rows, 128))
    stat_ref[:, 128:256] = jnp.broadcast_to(product, (rows, 128))
    stat_ref[:, 256:384] = jnp.broadcast_to(total * inv * inv, (rows, 128))

    for s in range(nz - 2, nz):
        hand_over(s, start)
    for zz in range(nz):
        for xx in range(2):
            arrived(slot_of(zz, xx, 1 - c))
    for s in range(nz):
        spread(s, sent)
        hand_over(s, sent)
    for slot in range(4 * nz):
        store(slot).wait()
    q_store.wait()
    do_store.wait()


def front(nz, nh, order, lengths, x, dy, gain, wq, wk, wv, wo):
    rows, share = x.shape
    hq, width = wq.shape[1], wk.shape[1]
    n = 4 * nz
    dma = pltpu.SemaphoreType.DMA
    return pl.pallas_call(
        functools.partial(front_kernel, nz, nh),
        out_shape=(
            jax.ShapeDtypeStruct((rows, hq), BF16),
            jax.ShapeDtypeStruct((rows, hq), BF16),
            jax.ShapeDtypeStruct((n * rows, 2 * width), BF16),
            jax.ShapeDtypeStruct((rows, 384), F32),
            jax.ShapeDtypeStruct((rows, 2), jnp.int32),
            jax.ShapeDtypeStruct((2, n * rows), jnp.int32),
        ),
        in_specs=[SM, SM, VM, VM, VM, ANY, ANY, ANY, ANY],
        out_specs=(ANY, ANY, ANY, VM, VM, VM),
        scratch_shapes=[
            pltpu.VMEM((rows, hq), BF16), pltpu.VMEM((rows, hq), BF16),
            pltpu.VMEM((n * rows, 2 * width), BF16),
            pltpu.VMEM(wq.shape, BF16), pltpu.VMEM(wk.shape, BF16),
            pltpu.VMEM(wv.shape, BF16), pltpu.VMEM(wo.shape, BF16),
            pltpu.VMEM((nh, rows, share), BF16), pltpu.VMEM((nh, rows, share), BF16),
            pltpu.VMEM((rows, nh * share), BF16),
            dma((4,)), dma((2,)), dma((2,)), dma((n,)), dma((nh,)), dma((nh,)), dma((nh,)), dma((nh,)),
            dma((4, n)), dma((n,)),
        ],
        compiler_params=pltpu.CompilerParams(
            collective_id=0, has_side_effects=True, vmem_limit_bytes=VMEM_LIMIT),
        name="front",
    )(order, lengths, x, dy, gain, wq, wk, wv, wo)


def back_kernel(nz, nh, chunk, pq_ref, pk_ref, q_ref, do_ref, kv_hbm, x_ref, dy_ref, gain_ref,
                stat_ref, wq_ref, wk_ref, wv_ref, out_ref, sal_ref,
                kv_ref, wq, wk, wv, bias, ds_all, p_all, dq, dkv, hidden,
                core_in, x_out, x_in, low_out, low_in, high_out, high_in,
                grads, h_out, h_in, part_out, part_in,
                gsem, wsem, cs, cr, xs, xr, ls, lr, us, ur, hs, hr, ps, pr):
    me, z, x, c = coords()
    head = lax.axis_index("head")
    rows, share = x_ref.shape
    dim = nh * share
    hq = q_ref.shape[1]
    width = wk_ref.shape[1]
    kvh = width // HEAD_DIM
    per_group = hq // width
    scale = HEAD_DIM ** (-0.5)

    def kv_load(g, kind):
        at = pl.ds(pl.multiple_of(kind * width + g * HEAD_DIM, HEAD_DIM), HEAD_DIM)
        return pltpu.make_async_copy(kv_hbm.at[:, at], kv_ref.at[:, at], gsem.at[kind, g])

    for g in range(kvh):
        kv_load(g, 0).start()
        kv_load(g, 1).start()
    loads = [
        pltpu.make_async_copy(a, b, wsem.at[i])
        for i, (a, b) in enumerate(((wq_ref, wq), (wk_ref, wk), (wv_ref, wv)))
    ]
    for load in loads:
        load.start()
    enter(nz, nh)
    place, owner = pq_ref[:, 0:1], pq_ref[:, 1:2]
    allowed = (owner == pk_ref[1:2, :]) & (pk_ref[0:1, :] <= place)
    bias[...] = jnp.where(allowed, 0.0, -1e30)

    def lanes(start, size):
        return pl.ds(pl.multiple_of(start, HEAD_DIM), size)

    def part(g, slot):
        return (g, slice(None), pl.ds(pl.multiple_of(slot * rows, rows), rows), slice(None))

    def remote(src, dst, ss, rs, target):
        return pltpu.make_async_remote_copy(
            src_ref=src, dst_ref=dst, send_sem=ss, recv_sem=rs, device_id=target,
            device_id_type=MESH)

    beside = {"ctx": slot_of(z, x, 1 - c)}
    across = {"ctx": slot_of(z, 1 - x, c)}
    right = {"ctx": slot_of(z + 1, x, c)}
    left = {"ctx": slot_of(z - 1, x, c)}

    def core_copy(g, k, zz):
        xx = 1 - x if k == 0 else x
        return remote(dkv.at[part(g, slot_of(zz, xx, 1 - c))], core_in.at[g, k, zz],
                      cs.at[g, k, zz], cr.at[g, k, zz], beside)

    def x_copy(g, zz):
        return remote(x_out.at[g, zz], x_in.at[g, zz], xs.at[g, zz], xr.at[g, zz], across)

    def up_copy(g, zz):
        return remote(high_out.at[g, zz], high_in.at[g, zz], us.at[g, zz], ur.at[g, zz], right)

    def down_copy(g, zz):
        return remote(low_out.at[g, zz], low_in.at[g, zz], ls.at[g, zz], lr.at[g, zz], left)

    def target_of(i):
        if i == nz - 1:
            return z
        high = nz - 1 - i - jnp.where(i >= nz - 1 - z, 1, 0)
        low = i + jnp.where(i >= z, 1, 0)
        return jnp.where(z < nz // 2, high, low)

    def cross(g):
        for i in range(nz):
            zz = target_of(i)
            core_copy(g, 0, zz).wait_recv()
            x_out[g, zz] = (dkv[part(g, slot_of(zz, 1 - x, c))].astype(F32)
                            + core_in[g, 0, zz].astype(F32)).astype(BF16)
            x_copy(g, zz).start()

    def local_sum(g, zz):
        core_copy(g, 1, zz).wait_recv()
        x_copy(g, zz).wait_recv()
        return (dkv[part(g, slot_of(zz, x, c))].astype(F32) + core_in[g, 1, zz].astype(F32)
                + x_in[g, zz].astype(F32))

    def tick(g, tau):
        @pl.when(z <= tau)
        def _():
            zz = nz - 1 - tau + z
            high_out[g, zz] = local_sum(g, zz).astype(BF16)

            @pl.when(z > 0)
            def _():
                up_copy(g, zz).wait_recv()
                high_out[g, zz] = (high_out[g, zz].astype(F32)
                                   + high_in[g, zz].astype(F32)).astype(BF16)

            up_copy(g, zz).start()

        @pl.when(nz - 1 - z <= tau)
        def _():
            zz = tau - (nz - 1 - z)
            low_out[g, zz] = local_sum(g, zz).astype(BF16)

            @pl.when(z < nz - 1)
            def _():
                down_copy(g, zz).wait_recv()
                low_out[g, zz] = (low_out[g, zz].astype(F32)
                                  + low_in[g, zz].astype(F32)).astype(BF16)

            down_copy(g, zz).start()

    def settle(g):
        at = lanes(g * HEAD_DIM, HEAD_DIM)
        grads[:, :, at] = local_sum(g, z)

        @pl.when(z > 0)
        def _():
            up_copy(g, z).wait_recv()
            grads[:, :, at] = grads[:, :, at] + high_in[g, z].astype(F32)

        @pl.when(z < nz - 1)
        def _():
            down_copy(g, z).wait_recv()
            grads[:, :, at] = grads[:, :, at] + low_in[g, z].astype(F32)

    def attend(g, h):
        k = kv_ref[:, lanes(g * HEAD_DIM, HEAD_DIM)]
        v = kv_ref[:, lanes(width + g * HEAD_DIM, HEAD_DIM)]
        cols = lanes((g * per_group + h) * HEAD_DIM, HEAD_DIM)
        band = slice(h * rows, (h + 1) * rows)
        q, do = q_ref[:, cols], do_ref[:, cols]
        s = lax.dot_general(q, k, NT, preferred_element_type=F32) * scale + bias[...]
        e = jnp.exp(s - jnp.max(s, axis=1, keepdims=True))
        p = e * (1.0 / jnp.sum(e, axis=1, keepdims=True))
        half = p.astype(BF16)
        p_all[band, :] = half
        attended = jnp.dot(half, v, preferred_element_type=F32).astype(BF16)
        delta = jnp.sum(do.astype(F32) * attended.astype(F32), axis=1, keepdims=True)
        dp = lax.dot_general(do, v, NT, preferred_element_type=F32)
        ds = (p * (dp - delta) * scale).astype(BF16)
        ds_all[band, :] = ds
        dq[:, cols] = jnp.dot(ds, k, preferred_element_type=F32).astype(BF16)

    def group_grads(g):
        heads = [lanes((g * per_group + h) * HEAD_DIM, HEAD_DIM) for h in range(per_group)]
        qs = jnp.concatenate([q_ref[:, at] for at in heads], axis=0)
        dos = jnp.concatenate([do_ref[:, at] for at in heads], axis=0)
        dk = lax.dot_general(qs, ds_all[...], TN, preferred_element_type=F32)
        dkv[g, 0] = dk.astype(BF16).T
        dv = lax.dot_general(dos, p_all[...], TN, preferred_element_type=F32)
        dkv[g, 1] = dv.astype(BF16).T
        for kind in range(2):
            for i in range(nz):
                core_copy(g, kind, target_of(i)).start()

    tile = 512
    tiles = dim // tile

    def h_tile(t, carry):
        at = pl.ds(pl.multiple_of(t * tile, tile), tile)
        hidden[:, at] = lax.dot_general(dq[...], wq[at, :], NT, preferred_element_type=F32)
        return carry

    def step(t, carry):
        @pl.when(t < kvh)
        def _():
            kv_load(t, 0).wait()
            kv_load(t, 1).wait()
            for h in range(per_group // 2):
                attend(t, h)

        @pl.when(t == kvh)
        def _():
            loads[0].wait()

        @pl.when(t >= kvh)
        def _():
            e = t - kvh
            lax.fori_loop(tiles * e // (nz + 1), tiles * (e + 1) // (nz + 1), h_tile, 0)

        for stage in range(1, nz + 2):
            g = t - stage

            @pl.when((g >= 0) & (g < kvh))
            def _():
                if stage == 1:
                    cross(g)
                elif stage <= nz:
                    tick(g, stage - 2)
                else:
                    settle(g)

        @pl.when(t < kvh)
        def _():
            for h in range(per_group // 2, per_group):
                attend(t, h)
            group_grads(t)

        return carry

    lax.fori_loop(0, kvh + nz + 1, step, 0)
    loads[1].wait()
    loads[2].wait()

    def finish(start):
        at = pl.ds(pl.multiple_of(start, chunk), chunk)
        return (hidden[:, at]
                + lax.dot_general(grads[0].astype(BF16), wk[at, :], NT, preferred_element_type=F32)
                + lax.dot_general(grads[1].astype(BF16), wv[at, :], NT, preferred_element_type=F32))

    per = share // chunk

    def h_copy(p, k):
        return remote(h_out.at[p - 1, k], h_in.at[p - 1, k], hs.at[p - 1, k], hr.at[p - 1, k],
                      {"head": lax.rem(head + p, nh)})

    for p in range(1, nh):
        for k in range(per):
            h_out[p - 1, k] = finish(lax.rem(head + p, nh) * share + k * chunk).astype(BF16)
            h_copy(p, k).start()
    inv = stat_ref[:, 0:1]
    product = stat_ref[:, 128:129]
    squares = stat_ref[:, 256:257]
    for k in range(per):
        hidden[:, k * chunk:(k + 1) * chunk] = finish(head * share + k * chunk)
    inner = jnp.zeros((rows, 1), F32)
    for k in range(per):
        cols = slice(k * chunk, (k + 1) * chunk)
        grad = hidden[:, cols]
        for p in range(1, nh):
            h_copy(p, k).wait_recv()
            grad = grad + h_in[p - 1, k].astype(F32)
        scaled = grad * gain_ref[:, pl.ds(pl.multiple_of(head * share + k * chunk, chunk), chunk)]
        hidden[:, cols] = scaled
        inner = inner + jnp.sum(scaled * (x_ref[:, cols].astype(F32) * inv), axis=1, keepdims=True)
    part_out[...] = jnp.broadcast_to(inner, part_out.shape)

    def p_copy(p):
        return remote(part_out, part_in.at[p - 1], ps.at[p - 1], pr.at[p - 1],
                      {"head": lax.rem(head + p, nh)})

    for p in range(1, nh):
        p_copy(p).start()
    for p in range(1, nh):
        p_copy(p).wait_recv()
        inner = inner + part_in[p - 1][:, 0:1]
    saliency = product + inner - (inner / dim) * squares
    sal_ref[...] = jnp.broadcast_to(saliency, (rows, 128)).T[0:1, :]
    inner = inner / dim
    for k in range(per):
        cols = slice(k * chunk, (k + 1) * chunk)
        unit = x_ref[:, cols].astype(F32) * inv
        out_ref[:, cols] = (dy_ref[:, cols].astype(F32)
                            + (hidden[:, cols] - unit * inner) * inv).astype(BF16)

    def drain(g, carry):
        for zz in range(nz):
            core_copy(g, 0, zz).wait_send()
            core_copy(g, 1, zz).wait_send()
            x_copy(g, zz).wait_send()
            pl.when(z < zz)(lambda zz=zz: up_copy(g, zz).wait_send())
            pl.when(z > zz)(lambda zz=zz: down_copy(g, zz).wait_send())
        return carry

    lax.fori_loop(0, kvh, drain, 0)
    for p in range(1, nh):
        for k in range(per):
            h_copy(p, k).wait_send()
        p_copy(p).wait_send()


def back(nz, nh, pq, pk, q, do, kv, x, dy, gain, stat, wq, wk, wv):
    rows, share = x.shape
    width = wk.shape[1]
    kvh = width // HEAD_DIM
    length = kv.shape[0]
    wide = q.shape[1] // kvh
    dim = nh * share
    chunk = min(512, share)
    per = share // chunk
    piece = (kvh, nz, 2, rows, HEAD_DIM)
    dma = pltpu.SemaphoreType.DMA
    peers = max(1, nh - 1)
    hops = dma((kvh, nz))
    return pl.pallas_call(
        functools.partial(back_kernel, nz, nh, chunk),
        out_shape=(
            jax.ShapeDtypeStruct((rows, share), BF16),
            jax.ShapeDtypeStruct((1, rows), F32),
        ),
        in_specs=[VM] * 4 + [ANY] + [VM] * 4 + [ANY] * 3,
        out_specs=(VM, VM),
        scratch_shapes=[
            pltpu.VMEM(kv.shape, BF16),
            pltpu.VMEM(wq.shape, BF16), pltpu.VMEM(wk.shape, BF16), pltpu.VMEM(wv.shape, BF16),
            pltpu.VMEM((rows, length), F32),
            pltpu.VMEM((wide // HEAD_DIM * rows, length), BF16),
            pltpu.VMEM((wide // HEAD_DIM * rows, length), BF16),
            pltpu.VMEM(q.shape, BF16),
            pltpu.VMEM((kvh, 2, length, HEAD_DIM), BF16),
            pltpu.VMEM((rows, dim), F32),
            pltpu.VMEM((kvh, 2, nz, 2, rows, HEAD_DIM), BF16),
            pltpu.VMEM(piece, BF16), pltpu.VMEM(piece, BF16),
            pltpu.VMEM(piece, BF16), pltpu.VMEM(piece, BF16),
            pltpu.VMEM(piece, BF16), pltpu.VMEM(piece, BF16),
            pltpu.VMEM((2, rows, width), F32),
            pltpu.VMEM((peers, per, rows, chunk), BF16),
            pltpu.VMEM((peers, per, rows, chunk), BF16),
            pltpu.VMEM((rows, 128), F32), pltpu.VMEM((peers, rows, 128), F32),
            dma((2, kvh)), dma((3,)), dma((kvh, 2, nz)), dma((kvh, 2, nz)),
            hops, hops, hops, hops, hops, hops,
            dma((peers, per)), dma((peers, per)), dma((peers,)), dma((peers,)),
        ],
        compiler_params=pltpu.CompilerParams(
            collective_id=1, has_side_effects=True, vmem_limit_bytes=VMEM_LIMIT),
        name="back",
    )(pq, pk, q, do, kv, x, dy, gain, stat, wq, wk, wv)


def fused_kernel(nz, order_ref, lengths_ref, x_ref, dy_ref, gain_ref,
                 wq_ref, wk_ref, wv_ref, wo_ref, out_ref, sal_ref,
                 wq, wk, wv, wo, xall, dyall, xg, acc_kv, acc2, inv_ref, vx,
                 kv_own, kvs, q_out, do_out, qs, dos, qt, dot_, bias, ee, acc_o, m_run, stat,
                 dq_own, part, up_in, down_in, fin, dkvr,
                 h_out, h_in, part_out, part_in,
                 wsem, lsem, xs, xr, dys, dyr, ks, kr, zus, zds, zr, qsem, qr, dsem, dr,
                 us, ur, ls, lr, gs, gr, fs, fr, hs, hr, ps, pr):
    me, z, x, c = coords()
    head = lax.axis_index("head")
    rows, share = x_ref.shape
    dim = 2 * share
    width = wk_ref.shape[1]
    slab = SLAB * rows
    wide = wq_ref.shape[1] // SLAB
    per_group = wide // HEAD_DIM
    rc = rows // HALVES
    block = SLAB * rc
    kv = 2 * HEAD_DIM
    scale = HEAD_DIM ** (-0.5)
    j = x * 2 + c
    gg = wo.at[:, 0:block]
    dq_slab = wo.at[0:slab, block:block + wide]
    peer = 1 - head
    mine = pl.ds(pl.multiple_of(head * share, share), share)
    theirs = pl.ds(pl.multiple_of(peer * share, share), share)

    own = [
        pltpu.make_async_copy(x_ref, xall.at[head], lsem.at[0]),
        pltpu.make_async_copy(dy_ref, dyall.at[head], lsem.at[1]),
    ]
    own[0].start()
    load_k = pltpu.make_async_copy(wk_ref, wk, wsem.at[0])
    load_v = pltpu.make_async_copy(wv_ref, wv, wsem.at[1])
    load_q = [pltpu.make_async_copy(wq_ref.at[at, :], wq.at[at, :], wsem.at[2 + i])
              for i, at in enumerate((mine, theirs))]
    load_o = [pltpu.make_async_copy(wo_ref.at[:, at], wo, wsem.at[4 + i])
              for i, at in enumerate((mine, theirs))]
    load_k.start()
    load_v.start()
    load_q[0].start()
    own[1].start()
    load_o[0].start()
    load_q[1].start()

    def member(p):
        xx = x if p < 2 else 1 - x
        cc = c if p % 2 == 0 else 1 - c
        return xx, cc, xx * 2 + cc

    barrier = pltpu.get_barrier_semaphore()

    def greet(target):
        pl.semaphore_signal(barrier, inc=1, device_id=target, device_id_type=MESH)

    greet({"head": peer})
    for p in range(1, SLAB):
        greet({"ctx": slot_of(z, *member(p)[:2])})
    pl.when(z > 0)(lambda: greet({"ctx": slot_of(z - 1, x, c)}))
    pl.when(z < nz - 1)(lambda: greet({"ctx": slot_of(z + 1, x, c)}))

    @pl.when((z > 0) & (z < nz - 1))
    def _():
        pl.semaphore_wait(barrier, SLAB + 2)

    @pl.when((z == 0) | (z == nz - 1))
    def _():
        pl.semaphore_wait(barrier, SLAB + 1)

    def remote(src, dst, ss, rs, target):
        return pltpu.make_async_remote_copy(
            src_ref=src, dst_ref=dst, send_sem=ss, recv_sem=rs, device_id=target,
            device_id_type=MESH)

    def to_member(p, src, dst, ss, rs):
        xx, cc, _ = member(p)
        return remote(src, dst, ss, rs, {"ctx": slot_of(z, xx, cc)})

    right = {"ctx": slot_of(z + 1, x, c)}
    left = {"ctx": slot_of(z - 1, x, c)}

    def span(start, size):
        return pl.ds(pl.multiple_of(start, size), size)

    def x_copy(a):
        at = slice(a * rc, (a + 1) * rc)
        return remote(x_ref.at[at, :], xall.at[head, at, :], xs.at[a], xr.at[a], {"head": peer})

    tile = wide
    fd = min(1024, share)
    feats = share // fd

    def dy_copy(f):
        at = slice(f * fd, (f + 1) * fd)
        return remote(dy_ref.at[:, at], dyall.at[head, :, at], dys.at[f], dyr.at[f], {"head": peer})

    for a in range(HALVES):
        x_copy(a).start()
    for f in range(feats):
        dy_copy(f).start()

    def make_bias():
        vx[:, HEAD_DIM:kv] = jnp.ones((slab, HEAD_DIM), BF16)
        place_q, owner_q = timeline_place(
            lax.broadcasted_iota(jnp.int32, (slab, 1), 0) + z * slab, order_ref, lengths_ref)
        lane = lax.broadcasted_iota(jnp.int32, (1, nz * slab), 1)
        chunk_bits = rc.bit_length() - 1
        row_in = lane & (rc - 1)
        member_in = jnp.right_shift(lane, chunk_bits) & (SLAB - 1)
        half_in = jnp.right_shift(lane, chunk_bits + 2) & (HALVES - 1)
        slab_in = jnp.right_shift(lane, slab.bit_length() - 1)
        place_k, owner_k = timeline_place(
            slab_in * slab + member_in * rows + half_in * rc + row_in, order_ref, lengths_ref)
        for zz in range(nz):
            for a in range(HALVES):
                at = slice(zz * slab + a * block, zz * slab + (a + 1) * block)
                allowed = (owner_q == owner_k[:, at]) & (place_k[:, at] <= place_q)
                bias[zz, :, a * block:(a + 1) * block] = jnp.where(allowed, 0.0, -1e30).astype(BF16)

    def squares(v):
        return jnp.sum(v * v, axis=1, keepdims=True)

    def kv_own_half():
        own[0].wait()
        v = xall[head].astype(F32)
        inv_ref[:, 2:3] = squares(v)
        xg[head] = (v * gain_ref[:, mine]).astype(BF16)
        load_k.wait()
        acc_kv[0] = jnp.dot(xg[head], wk[mine, :], preferred_element_type=F32)
        load_v.wait()
        acc_kv[1] = jnp.dot(xg[head], wv[mine, :], preferred_element_type=F32)

    def q_half(t, carry):
        at = span(t * tile, tile)
        acc2[0, :, at] = jnp.dot(xg[head], wq[mine, at], preferred_element_type=F32)
        return carry

    def do_half(t, carry):
        at = span(t * tile, tile)
        acc2[1, :, at] = lax.dot_general(dyall[head], wo[at, :], NT, preferred_element_type=F32)
        return carry

    def q_own():
        load_q[0].wait()
        lax.fori_loop(0, SLAB, q_half, 0)

    def do_own(first, last):
        if first == 0:
            own[1].wait()
            load_o[0].wait()
        lax.fori_loop(first, last, do_half, 0)
        if last == SLAB:
            load_o[1].start()

    def kv_copy(p, a):
        jt = member(p)[2]
        dst = kvs.at[z, a, span(j * rc, rc), :]
        return to_member(p, kv_own.at[a, jt], dst, ks.at[a, p], kr.at[a, j])

    def kv_arrived(p, a):
        jt = member(p)[2]
        to_member(p, kv_own.at[a, jt], kvs.at[z, a, span(jt * rc, rc), :],
                  ks.at[a, p], kr.at[a, jt]).wait_recv()

    def make_kv(a):
        x_copy(a).wait_recv()
        at = slice(a * rc, (a + 1) * rc)
        v = xall[peer, at, :].astype(F32)
        total = inv_ref[at, 2:3] + squares(v)
        inv = 1.0 / jnp.sqrt(total / dim + 1e-05)
        inv_ref[at, 0:1] = inv
        inv_ref[at, 1:2] = total * inv * inv
        xg[peer, at, :] = (v * gain_ref[:, theirs]).astype(BF16)
        lhs = xg[peer, at, :]
        for i, w in enumerate((wk, wv)):
            got = (acc_kv[i, at, :] + jnp.dot(lhs, w[theirs, :], preferred_element_type=F32)) * inv
            got = got.astype(BF16)
            for jj in range(SLAB):
                kv_own[a, jj, :, i * HEAD_DIM:(i + 1) * HEAD_DIM] = (
                    got[:, jj * HEAD_DIM:(jj + 1) * HEAD_DIM])
        for p in (2, 3, 1):
            kv_copy(p, a).start()
        kvs[z, a, span(j * rc, rc), :] = kv_own[a, j]

    def piece(zz, a, s):
        return kvs.at[zz, a, span(s * 2 * rc, 2 * rc), :]

    def z_up(zz, a, s):
        return remote(piece(zz, a, s), piece(zz, a, s), zus.at[zz, a, s], zr.at[zz, a, s], right)

    def z_down(zz, a, s):
        return remote(piece(zz, a, s), piece(zz, a, s), zds.at[zz, a, s], zr.at[zz, a, s], left)

    def gather_own(a):
        kv_arrived(1, a)
        for s, peers in ((x, ()), (1 - x, (2, 3))):
            for p in peers:
                kv_arrived(p, a)
            pl.when(z < nz - 1)(lambda s=s: z_up(z, a, s).start())
            pl.when(z > 0)(lambda s=s: z_down(z, a, s).start())

    def order(t):
        near = jnp.where(z < nz // 2, z, nz - 1 - z)
        d = (t + 1) // 2
        o = jnp.where(t <= 2 * near, near + d if t % 2 else near - d, t)
        return jnp.where(z < nz // 2, o, nz - 1 - o)

    def take(t, a):
        zz = order(t)
        for s in range(2):
            z_up(zz, a, s).wait_recv()
            pl.when((zz < z) & (z < nz - 1))(lambda s=s: z_up(zz, a, s).start())
            pl.when((zz > z) & (z > 0))(lambda s=s: z_down(zz, a, s).start())

    def shared(p, src, dst, ss, rs):
        jt = member(p)[2]
        return to_member(p, src.at[jt], dst.at[span(j * rows, rows), :], ss.at[p], rs.at[j])

    def shared_arrived(p, src, dst, ss, rs):
        jt = member(p)[2]
        to_member(p, src.at[jt], dst.at[span(jt * rows, rows), :], ss.at[p], rs.at[jt]).wait_recv()

    def q_tile(p):
        jt = member(p)[2]
        at = span(jt * tile, tile)
        got = acc2[0, :, at] + jnp.dot(
            xg[peer], wq[theirs, at], preferred_element_type=F32)
        q_out[jt] = (got * (inv_ref[:, 0:1] * (scale * LOG2E))).astype(BF16)
        if p:
            shared(p, q_out, qs, qsem, qr).start()
        else:
            qs[span(j * rows, rows), :] = q_out[jt]

    def do_part(f, first=0, last=SLAB):
        if f == 0 and first == 0:
            load_o[1].wait()
        if first == 0:
            dy_copy(f).wait_recv()
        at = slice(f * fd, (f + 1) * fd)
        if f < feats - 1:
            def body(t, carry):
                cols = span(t * tile, tile)
                acc2[1, :, cols] = acc2[1, :, cols] + lax.dot_general(
                    dyall[peer, :, at], wo[cols, at], NT, preferred_element_type=F32)
                return carry

            lax.fori_loop(first, last, body, 0)
            return
        for p in (3, 2, 1, 0):
            jt = member(p)[2]
            cols = span(jt * tile, tile)
            do_out[jt] = (acc2[1, :, cols] + lax.dot_general(
                dyall[peer, :, at], wo[cols, at], NT, preferred_element_type=F32)).astype(BF16)
            if p:
                shared(p, do_out, dos, dsem, dr).start()
            else:
                dos[span(j * rows, rows), :] = do_out[jt]

    lane_at = lax.broadcasted_iota(jnp.int32, (slab, HEAD_DIM), 1)

    def forward(t, hook=None):
        zz = order(t)
        vx[:, 0:HEAD_DIM] = kvs[zz, :, :, HEAD_DIM:kv].reshape(slab, HEAD_DIM)
        def one(hh):
            cols = span(hh * HEAD_DIM, HEAD_DIM)
            k = kvs[zz, :, :, 0:HEAD_DIM].reshape(slab, HEAD_DIM)
            s = lax.dot_general(qs[:, cols], k, NT, preferred_element_type=F32)
            s = s + bias[zz].astype(F32)
            m = jnp.broadcast_to(jnp.max(s, axis=1, keepdims=True), (slab, HEAD_DIM))
            if t:
                old = m_run[hh]
                m = jnp.maximum(m, old)
            half = jnp.exp2(s - jnp.concatenate([m] * SLAB, axis=1)).astype(BF16)
            ee[t, span(hh * slab, slab), :] = half
            o = jnp.dot(half, vx[...], preferred_element_type=F32)
            if t:
                alpha = jnp.exp2(old - m)
                o = o + acc_o[hh] * jnp.concatenate([alpha, alpha], axis=1)
            stat[hh] = jnp.where(lane_at == t, m, stat[hh]) if t else m
            m_run[hh] = m
            acc_o[hh] = o

        def pair(i, carry):
            one(2 * i)
            one(2 * i + 1)
            if hook is not None:
                pl.when(i == 0)(hook)
            return carry

        lax.fori_loop(0, per_group // 2, pair, 0)

    def settle():
        def one(hh, carry):
            cols = span(hh * HEAD_DIM, HEAD_DIM)
            do = dos[:, cols]
            inv_l = 1.0 / acc_o[hh, :, HEAD_DIM:kv]
            attended = (acc_o[hh, :, 0:HEAD_DIM] * inv_l).astype(BF16)
            delta = jnp.sum(do.astype(F32) * attended.astype(F32), axis=1, keepdims=True)
            stat[hh] = jnp.where(lane_at == HEAD_DIM - 1, delta, jnp.exp2(stat[hh] - m_run[hh]) * inv_l)
            acc_o[hh, :, 0:HEAD_DIM] = jnp.zeros((slab, HEAD_DIM), F32)
            dot_[:, span(hh * slab, slab)] = do.T
            return carry

        lax.fori_loop(0, per_group, one, 0)

    def turn_q():
        def one(hh, carry):
            qt[:, span(hh * slab, slab)] = qs[:, span(hh * HEAD_DIM, HEAD_DIM)].T
            return carry

        lax.fori_loop(0, per_group, one, 0)

    def backward(t, a):
        zz = order(t)
        half = slice(a * block, (a + 1) * block)

        def one(hh):
            k = kvs[zz, a, :, 0:HEAD_DIM]
            v = kvs[zz, a, :, HEAD_DIM:kv]
            cols = span(hh * HEAD_DIM, HEAD_DIM)
            at = span(hh * slab, slab)
            dp = lax.dot_general(dos[:, cols], v, NT, preferred_element_type=F32)
            p = ee[t, at, half].astype(F32) * stat[hh, :, t:t + 1]
            ee[t, at, half] = p.astype(BF16)
            g = (p * (dp - stat[hh, :, 127:128])).astype(BF16)
            gg[at, :] = g
            acc_o[hh, :, 0:HEAD_DIM] = (acc_o[hh, :, 0:HEAD_DIM]
                                        + jnp.dot(g, k, preferred_element_type=F32))

        def pair(i, carry):
            one(2 * i)
            one(2 * i + 1)
            return carry

        lax.fori_loop(0, per_group // 2, pair, 0)
        dk = jnp.dot(qt[...], gg[...], preferred_element_type=F32) * LN2
        dv = jnp.dot(dot_[...], ee[t, :, half], preferred_element_type=F32)
        part[zz, a, :, 0:HEAD_DIM] = dk.astype(BF16).T
        part[zz, a, :, HEAD_DIM:kv] = dv.astype(BF16).T

    def up_copy(zz, a):
        return remote(part.at[zz, a], up_in.at[zz, a], us.at[zz, a], ur.at[zz, a], right)

    def down_copy(zz, a):
        return remote(part.at[zz, a], down_in.at[zz, a], ls.at[zz, a], lr.at[zz, a], left)

    def send_part(t, a):
        zz = order(t)
        pl.when((zz > z) & (z == 0))(lambda: up_copy(zz, a).start())
        pl.when((zz < z) & (z == nz - 1))(lambda: down_copy(zz, a).start())

    def pass_part(t, a):
        zz = order(t)

        @pl.when((zz > z) & (z > 0))
        def _():
            up_copy(zz, a).wait_recv()
            part[zz, a] = (part[zz, a].astype(F32) + up_in[zz, a].astype(F32)).astype(BF16)
            up_copy(zz, a).start()

        @pl.when((zz < z) & (z < nz - 1))
        def _():
            down_copy(zz, a).wait_recv()
            part[zz, a] = (part[zz, a].astype(F32) + down_in[zz, a].astype(F32)).astype(BF16)
            down_copy(zz, a).start()

    def fin_copy(p, a):
        jt = member(p)[2]
        return to_member(p, fin.at[a, span(jt * rc, rc), :], dkvr.at[a, j], fs.at[a, p], fr.at[a, j])

    def fin_arrived(p, a):
        jt = member(p)[2]
        to_member(p, fin.at[a, span(jt * rc, rc), :], dkvr.at[a, jt], fs.at[a, p],
                  fr.at[a, jt]).wait_recv()

    def finish_part(a):
        fin[a] = part[z, a]

        @pl.when(z > 0)
        def _():
            up_copy(z, a).wait_recv()
            fin[a] = (fin[a].astype(F32) + up_in[z, a].astype(F32)).astype(BF16)

        @pl.when(z < nz - 1)
        def _():
            down_copy(z, a).wait_recv()
            fin[a] = (fin[a].astype(F32) + down_in[z, a].astype(F32)).astype(BF16)

        for p in (3, 2, 1):
            fin_copy(p, a).start()
        dkvr[a, j] = fin[a, span(j * rc, rc), :]

    def dq_copy(p):
        jt = member(p)[2]
        return to_member(p, wo.at[span(jt * rows, rows), block:block + wide], dq_own.at[:, span(j * tile, tile)],
                         gs.at[p], gr.at[j])

    def dq_arrived(p):
        jt = member(p)[2]
        to_member(p, wo.at[span(jt * rows, rows), block:block + wide], dq_own.at[:, span(jt * tile, tile)],
                  gs.at[p], gr.at[jt]).wait_recv()

    make_bias()
    kv_own_half()
    q_own()
    make_kv(0)
    do_own(0, 2)
    gather_own(0)
    do_own(2, SLAB)
    make_kv(1)
    load_q[1].wait()
    q_tile(3)
    q_tile(2)
    q_tile(1)
    q_tile(0)
    take(1, 0)
    gather_own(1)
    do_part(0, 0, 2)
    for t in range(2, min(3, nz)):
        take(t, 0)
    do_part(0, 2, SLAB)
    take(1, 1)
    for p in (1, 2, 3):
        shared_arrived(p, q_out, qs, qsem, qr)

    def far():
        for t in range(3, nz):
            take(t, 0)

    forward(0, far)
    for t in range(2, min(3, nz)):
        take(t, 1)
    for f in range(1, feats):
        do_part(f)
    forward(1)
    for t in range(3, nz):
        take(t, 1)
    turn_q()
    for t in range(2, nz):
        forward(t)
    for p in (1, 2, 3):
        shared_arrived(p, do_out, dos, dsem, dr)
    settle()
    steps = [(nz - 1, a) for a in range(HALVES)]
    steps += [(t, a) for a in range(HALVES) for t in range(nz - 2, 0, -1)]
    steps += [(0, a) for a in range(HALVES)]
    lag = 3
    for i, (t, a) in enumerate(steps):
        backward(t, a)
        if t:
            send_part(t, a)
        if i >= lag and steps[i - lag][0]:
            pass_part(*steps[i - lag])
    for hh in range(per_group):
        dq_slab[:, hh * HEAD_DIM:(hh + 1) * HEAD_DIM] = (acc_o[hh, :, 0:HEAD_DIM] * scale).astype(BF16)
    for p in (3, 2, 1):
        dq_copy(p).start()
    dq_own[:, span(j * tile, tile)] = dq_slab[span(j * rows, rows), :]
    for step in steps[len(steps) - lag:]:
        if step[0]:
            pass_part(*step)
    product = jnp.zeros((rows, 1), F32)
    for h in range(2):
        product = product + jnp.sum(
            xall[h].astype(F32) * dyall[h].astype(F32), axis=1, keepdims=True)
    dq_arrived(1)
    hidden = acc2
    chunk = min(512, share)
    per = share // chunk

    def h_tile(half, xx, add):
        heads_at = span(xx * 2 * tile, 2 * tile)

        def body(k, carry):
            at = span(half * share + k * chunk, chunk)
            cols = span(k * chunk, chunk)
            got = lax.dot_general(dq_own[:, heads_at], wq[at, heads_at], NT,
                                  preferred_element_type=F32)
            hidden[half, :, cols] = hidden[half, :, cols] + got if add else got
            return carry

        lax.fori_loop(0, per, body, 0)

    h_tile(peer, x, False)
    finish_part(0)
    h_tile(head, x, False)
    dq_arrived(3)
    dq_arrived(2)
    h_tile(peer, 1 - x, True)
    finish_part(1)
    h_tile(head, 1 - x, True)
    for a in range(HALVES):
        for p in (1, 2, 3):
            fin_arrived(p, a)
    grads = [
        jnp.concatenate(
            [jnp.concatenate([dkvr[a, jj, :, i * HEAD_DIM:(i + 1) * HEAD_DIM] for jj in range(SLAB)],
                             axis=1) for a in range(HALVES)], axis=0)
        for i in range(2)
    ]

    def finish(half, k):
        at = span(half * share + k * chunk, chunk)
        return (hidden[half, :, k * chunk:(k + 1) * chunk]
                + lax.dot_general(grads[0], wk[at, :], NT, preferred_element_type=F32)
                + lax.dot_general(grads[1], wv[at, :], NT, preferred_element_type=F32))

    def h_copy(k):
        return remote(h_out.at[k], h_in.at[k], hs.at[k], hr.at[k], {"head": peer})

    inv = inv_ref[:, 0:1]
    inner = jnp.zeros((rows, 1), F32)

    def weighed(half, k, grad):
        scaled = grad * gain_ref[:, span(half * share + k * chunk, chunk)]
        unit = xall[half, :, k * chunk:(k + 1) * chunk].astype(F32) * inv
        return jnp.sum(scaled * unit, axis=1, keepdims=True)

    for k in range(per):
        grad = finish(peer, k)
        h_out[k] = grad.astype(BF16)
        h_copy(k).start()
        inner = inner + weighed(peer, k, grad)
    for k in range(per):
        grad = finish(head, k)
        hidden[head, :, k * chunk:(k + 1) * chunk] = grad
        inner = inner + weighed(head, k, grad)
    part_out[...] = jnp.broadcast_to(inner, part_out.shape)
    p_copy = remote(part_out, part_in, ps, pr, {"head": peer})
    p_copy.start()
    p_copy.wait_recv()
    inner = inner + part_in[:, 0:1]
    saliency = product + inner - (inner / dim) * inv_ref[:, 1:2]
    sal_ref[...] = jnp.broadcast_to(saliency, (rows, 128)).T[0:1, :]
    inner = inner / dim
    for k in range(per):
        cols = slice(k * chunk, (k + 1) * chunk)
        unit = xall[head, :, cols].astype(F32) * inv
        h_copy(k).wait_recv()
        grad = hidden[head, :, cols] + h_in[k].astype(F32)
        scaled = grad * gain_ref[:, span(head * share + k * chunk, chunk)]
        out_ref[:, cols] = (dyall[head, :, cols].astype(F32)
                            + (scaled - unit * inner) * inv).astype(BF16)

    for a in range(HALVES):
        x_copy(a).wait_send()
        for p in (1, 2, 3):
            kv_copy(p, a).wait_send()
            fin_copy(p, a).wait_send()
        for zz in range(nz):
            pl.when(z < zz)(lambda zz=zz, a=a: up_copy(zz, a).wait_send())
            pl.when(z > zz)(lambda zz=zz, a=a: down_copy(zz, a).wait_send())
            for s in range(2):
                pl.when((zz <= z) & (z < nz - 1))(lambda zz=zz, a=a, s=s: z_up(zz, a, s).wait_send())
                pl.when((zz >= z) & (z > 0))(lambda zz=zz, a=a, s=s: z_down(zz, a, s).wait_send())
    for f in range(feats):
        dy_copy(f).wait_send()
    for p in (1, 2, 3):
        shared(p, q_out, qs, qsem, qr).wait_send()
        shared(p, do_out, dos, dsem, dr).wait_send()
        dq_copy(p).wait_send()
    for k in range(per):
        h_copy(k).wait_send()
    p_copy.wait_send()


def fused(nz, order, lengths, x, dy, gain, wq, wk, wv, wo):
    rows, share = x.shape
    dim = 2 * share
    hq, width = wq.shape[1], wk.shape[1]
    wide = hq // SLAB
    heads = wide // HEAD_DIM
    rc = rows // HALVES
    slab = SLAB * rows
    block = SLAB * rc
    kv = 2 * HEAD_DIM
    fd = min(1024, share)
    chunk = min(512, share)
    per = share // chunk
    feats = share // fd
    dma = pltpu.SemaphoreType.DMA
    vm = pltpu.VMEM
    return pl.pallas_call(
        functools.partial(fused_kernel, nz),
        out_shape=(
            jax.ShapeDtypeStruct((rows, share), BF16),
            jax.ShapeDtypeStruct((1, rows), F32),
        ),
        in_specs=[SM, SM, ANY, ANY, VM, ANY, ANY, ANY, ANY],
        out_specs=(VM, VM),
        scratch_shapes=[
            vm(wq.shape, BF16), vm(wk.shape, BF16), vm(wv.shape, BF16), vm((hq, share), BF16),
            vm((2, rows, share), BF16), vm((2, rows, share), BF16), vm((2, rows, share), BF16),
            vm((2, rows, width), F32), vm((2, rows, share), F32), vm((rows, 128), F32),
            vm((slab, kv), BF16),
            vm((HALVES, SLAB, rc, kv), BF16), vm((nz, HALVES, block, kv), BF16),
            vm((SLAB, rows, wide), BF16), vm((SLAB, rows, wide), BF16),
            vm((slab, wide), BF16), vm((slab, wide), BF16),
            vm((HEAD_DIM, heads * slab), BF16), vm((HEAD_DIM, heads * slab), BF16),
            vm((nz, slab, slab), BF16),
            vm((nz, heads * slab, slab), BF16),
            vm((heads, slab, kv), F32), vm((heads, slab, HEAD_DIM), F32), vm((heads, slab, 128), F32),
            vm((rows, hq), BF16),
            vm((nz, HALVES, block, kv), BF16), vm((nz, HALVES, block, kv), BF16),
            vm((nz, HALVES, block, kv), BF16),
            vm((HALVES, block, kv), BF16), vm((HALVES, SLAB, rc, kv), BF16),
            vm((per, rows, chunk), BF16), vm((per, rows, chunk), BF16),
            vm((rows, 128), F32), vm((rows, 128), F32),
            dma((6,)), dma((2,)), dma((HALVES,)), dma((HALVES,)), dma((feats,)), dma((feats,)),
            dma((HALVES, SLAB)), dma((HALVES, SLAB)),
            dma((nz, HALVES, 2)), dma((nz, HALVES, 2)), dma((nz, HALVES, 2)),
            dma((SLAB,)), dma((SLAB,)), dma((SLAB,)), dma((SLAB,)),
            dma((nz, HALVES)), dma((nz, HALVES)), dma((nz, HALVES)), dma((nz, HALVES)),
            dma((SLAB,)), dma((SLAB,)), dma((HALVES, SLAB)), dma((HALVES, SLAB)),
            dma((per,)), dma((per,)), dma(()), dma(()),
        ],
        compiler_params=pltpu.CompilerParams(
            collective_id=2, has_side_effects=True, vmem_limit_bytes=VMEM_LIMIT),
        name="fused",
    )(order, lengths, x, dy, gain, wq, wk, wv, wo)


def local(inputs, out_grad, norm_gain, w_query, w_key, w_value, w_out, record_lengths, block_order):
    rows, share = inputs.shape
    n = lax.axis_size("ctx")
    nh = lax.axis_size("head")
    nz = n // 4
    gain = norm_gain[None, :]
    if nh == 2 and w_key.shape[1] == SLAB * HEAD_DIM:
        input_grad, saliency = fused(
            nz, block_order, record_lengths, inputs, out_grad, gain, w_query, w_key, w_value, w_out)
        return (input_grad, saliency.reshape(rows))
    q, do, kv, stat, pq, pk = front(
        nz, nh, block_order, record_lengths, inputs, out_grad, gain,
        w_query, w_key, w_value, w_out)
    input_grad, saliency = back(
        nz, nh, pq, pk, q, do, kv, inputs, out_grad, gain, stat, w_query, w_key, w_value)
    return (input_grad, saliency.reshape(rows))


def solution(mesh):
    placed = (
        P("ctx", "head"),
        P("ctx", "head"),
        P(),
        P(None, "head"),
        P(None, "head"),
        P(None, "head"),
        P("head", None),
        P(),
        P(),
    )
    return jax.shard_map(
        local, mesh=mesh, in_specs=placed, out_specs=(P("ctx", "head"), P("ctx")), check_vma=False
    )
```

```python
import functools

import jax
import jax.numpy as jnp
from jax import lax
from jax.experimental import pallas as pl
from jax.experimental.pallas import tpu as pltpu
from jax.sharding import PartitionSpec as P

HEAD_DIM = 128
BLOCK = 64
SLAB = 4
HALVES = 2
LOG2E = 1.4426950408889634
LN2 = 0.6931471805599453
NT = (((1,), (1,)), ((), ()))
TN = (((0,), (0,)), ((), ()))
F32 = jnp.float32
BF16 = jnp.bfloat16
MESH = pl.DeviceIdType.MESH
VM = pl.BlockSpec(memory_space=pltpu.VMEM)
ANY = pl.BlockSpec(memory_space=pl.ANY)
SM = pl.BlockSpec(memory_space=pltpu.SMEM)
VMEM_LIMIT = 64 * 1024 * 1024 - 128 * 1024


def timeline_place(stored, order_ref, lengths_ref):
    block = jnp.right_shift(stored, 6)
    position = jnp.zeros(stored.shape, jnp.int32)
    for b in range(order_ref.shape[0]):
        position = jnp.where(block == b, order_ref[b], position)
    position = position * BLOCK + (stored & (BLOCK - 1))
    record = jnp.zeros(stored.shape, jnp.int32)
    start = 0
    for r in range(lengths_ref.shape[0]):
        record = record + jnp.where(position >= start, 1, 0)
        start = start + lengths_ref[r]
    return position, record


def coords():
    me = lax.axis_index("ctx")
    return me, me // 4, lax.rem(me // 2, 2), lax.rem(me, 2)


def slot_of(z, x, c):
    return (z * 2 + x) * 2 + c


def enter(nz, nh):
    _, z, x, c = coords()
    head = lax.axis_index("head")
    barrier = pltpu.get_barrier_semaphore()

    def greet(target):
        pl.semaphore_signal(barrier, inc=1, device_id=target, device_id_type=MESH)

    for p in range(1, nh):
        greet({"head": lax.rem(head + p, nh)})
    greet({"ctx": slot_of(z, 1 - x, c)})
    greet({"ctx": slot_of(z, x, 1 - c)})

    @pl.when(z > 0)
    def _():
        greet({"ctx": slot_of(z - 1, x, c)})

    @pl.when(z < nz - 1)
    def _():
        greet({"ctx": slot_of(z + 1, x, c)})

    @pl.when((z > 0) & (z < nz - 1))
    def _():
        pl.semaphore_wait(barrier, nh + 3)

    @pl.when((z == 0) | (z == nz - 1))
    def _():
        pl.semaphore_wait(barrier, nh + 2)


def front_kernel(nz, nh, order_ref, lengths_ref, x_ref, dy_ref, gain_ref,
                 wq_ref, wk_ref, wv_ref, wo_ref,
                 q_out, do_out, kv_out, stat_ref, pq_ref, pk_ref,
                 q_ref, do_ref, kv_ref, wq, wk, wv, wo, xall, dyall, normed,
                 wsem, lsem, osem, ssem, xs, xr, dys, dyr, ks, kr):
    me, z, x, c = coords()
    head = lax.axis_index("head")
    rows, share = x_ref.shape
    dim = nh * share
    hq = q_ref.shape[1]
    width = wk_ref.shape[1]
    loads = [
        pltpu.make_async_copy(a, b, wsem.at[i])
        for i, (a, b) in enumerate(((wk_ref, wk), (wv_ref, wv), (wq_ref, wq), (wo_ref, wo)))
    ]
    for load in loads:
        load.start()
    own = [
        pltpu.make_async_copy(x_ref, xall.at[head], lsem.at[0]),
        pltpu.make_async_copy(dy_ref, dyall.at[head], lsem.at[1]),
    ]
    for copy in own:
        copy.start()
    enter(nz, nh)

    def head_copies(src, dst, send, recv):
        return [
            pltpu.make_async_remote_copy(
                src_ref=src, dst_ref=dst.at[head], send_sem=send.at[p - 1], recv_sem=recv.at[p - 1],
                device_id={"head": lax.rem(head + p, nh)}, device_id_type=MESH)
            for p in range(1, nh)
        ]

    xc = head_copies(x_ref, xall, xs, xr)
    dyc = head_copies(dy_ref, dyall, dys, dyr)
    for copy in xc + dyc:
        copy.start()
    length = kv_ref.shape[0]
    pk_ref[0:1, :], pk_ref[1:2, :] = timeline_place(
        lax.broadcasted_iota(jnp.int32, (1, length), 1), order_ref, lengths_ref)
    pq_ref[:, 0:1], pq_ref[:, 1:2] = timeline_place(
        lax.broadcasted_iota(jnp.int32, (rows, 1), 0) + me * rows, order_ref, lengths_ref)
    own[0].wait()
    for copy in xc:
        copy.wait()
    total = jnp.zeros((rows, 1), F32)
    for j in range(nh):
        v = xall[j].astype(F32)
        total = total + jnp.sum(v * v, axis=1, keepdims=True)
    root = jnp.sqrt(total / dim + 1e-05)
    inv = 1.0 / root
    for j in range(nh):
        cols = slice(j * share, (j + 1) * share)
        normed[:, cols] = (xall[j].astype(F32) * inv * gain_ref[:, cols]).astype(BF16)

    def block(slot):
        return kv_ref.at[pl.ds(pl.multiple_of(slot * rows, rows), rows), :]

    def send(direction, slot, target):
        return pltpu.make_async_remote_copy(
            src_ref=block(slot), dst_ref=block(slot), send_sem=ks.at[direction, slot],
            recv_sem=kr.at[slot], device_id={"ctx": target}, device_id_type=MESH)

    def store(slot):
        return pltpu.make_async_copy(
            block(slot), kv_out.at[pl.ds(pl.multiple_of(slot * rows, rows), rows), :],
            ssem.at[slot])

    def arrived(slot):
        send(0, slot, me).wait_recv()
        store(slot).start()

    mine = pl.ds(pl.multiple_of(me * rows, rows), rows)
    loads[0].wait()
    kv_ref[mine, :width] = jnp.dot(normed[...], wk[...], preferred_element_type=F32).astype(BF16)
    loads[1].wait()
    kv_ref[mine, width:] = jnp.dot(normed[...], wv[...], preferred_element_type=F32).astype(BF16)

    right = slot_of(z + 1, x, c)
    left = slot_of(z - 1, x, c)
    across = slot_of(z, 1 - x, c)
    beside = slot_of(z, x, 1 - c)

    def spread(s, act):
        if s == 0:
            pl.when(z < nz - 1)(lambda: act(send(0, me, right)))
            pl.when(z > 0)(lambda: act(send(1, me, left)))
            act(send(2, me, across))
            act(send(3, me, beside))
            return
        low, high = slot_of(z - s, x, c), slot_of(z + s, x, c)

        @pl.when(z - s >= 0)
        def _():
            if act is start:
                arrived(low)
            pl.when(z < nz - 1)(lambda: act(send(0, low, right)))
            act(send(2, low, across))
            act(send(3, low, beside))

        @pl.when(z + s < nz)
        def _():
            if act is start:
                arrived(high)
            pl.when(z > 0)(lambda: act(send(1, high, left)))
            act(send(2, high, across))
            act(send(3, high, beside))

    def hand_over(s, act):
        def one(slot):
            if act is start:
                arrived(slot)
            act(send(3, slot, beside))

        if s == 0:
            one(slot_of(z, 1 - x, c))
            return
        pl.when(z - s >= 0)(lambda: one(slot_of(z - s, 1 - x, c)))
        pl.when(z + s < nz)(lambda: one(slot_of(z + s, 1 - x, c)))

    def start(copy):
        copy.start()

    def sent(copy):
        copy.wait_send()

    spread(0, start)
    store(me).start()

    loads[2].wait()
    tq = min(512, hq)

    def q_tile(t, carry):
        cols = pl.ds(pl.multiple_of(t * tq, tq), tq)
        q_ref[:, cols] = jnp.dot(normed[...], wq[:, cols], preferred_element_type=F32).astype(BF16)
        return carry

    lax.fori_loop(0, hq // tq, q_tile, 0)
    q_store = pltpu.make_async_copy(q_ref, q_out, osem.at[0])
    q_store.start()
    spread(1, start)

    own[1].wait()
    for copy in dyc:
        copy.wait()
    loads[3].wait()

    def do_tile(t, carry):
        cols = pl.ds(pl.multiple_of(t * tq, tq), tq)
        acc = jnp.zeros((rows, tq), F32)
        for j in range(nh):
            acc = acc + lax.dot_general(
                dyall[j], wo[cols, j * share:(j + 1) * share], NT, preferred_element_type=F32)
        do_ref[:, cols] = acc.astype(BF16)
        return carry

    tiles = hq // tq
    gaps = nz - 2
    for s in range(2, nz):
        lax.fori_loop(tiles * (s - 2) // gaps, tiles * (s - 1) // gaps, do_tile, 0)
        if s == nz - 1:
            do_store = pltpu.make_async_copy(do_ref, do_out, osem.at[1])
            do_store.start()
        spread(s, start)
        hand_over(s - 2, start)

    product = jnp.zeros((rows, 1), F32)
    for j in range(nh):
        product = product + jnp.sum(
            xall[j].astype(F32) * dyall[j].astype(F32), axis=1, keepdims=True)
    stat_ref[:, 0:128] = jnp.broadcast_to(inv, (rows, 128))
    stat_ref[:, 128:256] = jnp.broadcast_to(product, (rows, 128))
    stat_ref[:, 256:384] = jnp.broadcast_to(total * inv * inv, (rows, 128))

    for s in range(nz - 2, nz):
        hand_over(s, start)
    for zz in range(nz):
        for xx in range(2):
            arrived(slot_of(zz, xx, 1 - c))
    for s in range(nz):
        spread(s, sent)
        hand_over(s, sent)
    for slot in range(4 * nz):
        store(slot).wait()
    q_store.wait()
    do_store.wait()


def front(nz, nh, order, lengths, x, dy, gain, wq, wk, wv, wo):
    rows, share = x.shape
    hq, width = wq.shape[1], wk.shape[1]
    n = 4 * nz
    dma = pltpu.SemaphoreType.DMA
    return pl.pallas_call(
        functools.partial(front_kernel, nz, nh),
        out_shape=(
            jax.ShapeDtypeStruct((rows, hq), BF16),
            jax.ShapeDtypeStruct((rows, hq), BF16),
            jax.ShapeDtypeStruct((n * rows, 2 * width), BF16),
            jax.ShapeDtypeStruct((rows, 384), F32),
            jax.ShapeDtypeStruct((rows, 2), jnp.int32),
            jax.ShapeDtypeStruct((2, n * rows), jnp.int32),
        ),
        in_specs=[SM, SM, VM, VM, VM, ANY, ANY, ANY, ANY],
        out_specs=(ANY, ANY, ANY, VM, VM, VM),
        scratch_shapes=[
            pltpu.VMEM((rows, hq), BF16), pltpu.VMEM((rows, hq), BF16),
            pltpu.VMEM((n * rows, 2 * width), BF16),
            pltpu.VMEM(wq.shape, BF16), pltpu.VMEM(wk.shape, BF16),
            pltpu.VMEM(wv.shape, BF16), pltpu.VMEM(wo.shape, BF16),
            pltpu.VMEM((nh, rows, share), BF16), pltpu.VMEM((nh, rows, share), BF16),
            pltpu.VMEM((rows, nh * share), BF16),
            dma((4,)), dma((2,)), dma((2,)), dma((n,)), dma((nh,)), dma((nh,)), dma((nh,)), dma((nh,)),
            dma((4, n)), dma((n,)),
        ],
        compiler_params=pltpu.CompilerParams(
            collective_id=0, has_side_effects=True, vmem_limit_bytes=VMEM_LIMIT),
        name="front",
    )(order, lengths, x, dy, gain, wq, wk, wv, wo)


def back_kernel(nz, nh, chunk, pq_ref, pk_ref, q_ref, do_ref, kv_hbm, x_ref, dy_ref, gain_ref,
                stat_ref, wq_ref, wk_ref, wv_ref, out_ref, sal_ref,
                kv_ref, wq, wk, wv, bias, ds_all, p_all, dq, dkv, hidden,
                core_in, x_out, x_in, low_out, low_in, high_out, high_in,
                grads, h_out, h_in, part_out, part_in,
                gsem, wsem, cs, cr, xs, xr, ls, lr, us, ur, hs, hr, ps, pr):
    me, z, x, c = coords()
    head = lax.axis_index("head")
    rows, share = x_ref.shape
    dim = nh * share
    hq = q_ref.shape[1]
    width = wk_ref.shape[1]
    kvh = width // HEAD_DIM
    per_group = hq // width
    scale = HEAD_DIM ** (-0.5)

    def kv_load(g, kind):
        at = pl.ds(pl.multiple_of(kind * width + g * HEAD_DIM, HEAD_DIM), HEAD_DIM)
        return pltpu.make_async_copy(kv_hbm.at[:, at], kv_ref.at[:, at], gsem.at[kind, g])

    for g in range(kvh):
        kv_load(g, 0).start()
        kv_load(g, 1).start()
    loads = [
        pltpu.make_async_copy(a, b, wsem.at[i])
        for i, (a, b) in enumerate(((wq_ref, wq), (wk_ref, wk), (wv_ref, wv)))
    ]
    for load in loads:
        load.start()
    enter(nz, nh)
    place, owner = pq_ref[:, 0:1], pq_ref[:, 1:2]
    allowed = (owner == pk_ref[1:2, :]) & (pk_ref[0:1, :] <= place)
    bias[...] = jnp.where(allowed, 0.0, -1e30)

    def lanes(start, size):
        return pl.ds(pl.multiple_of(start, HEAD_DIM), size)

    def part(g, slot):
        return (g, slice(None), pl.ds(pl.multiple_of(slot * rows, rows), rows), slice(None))

    def remote(src, dst, ss, rs, target):
        return pltpu.make_async_remote_copy(
            src_ref=src, dst_ref=dst, send_sem=ss, recv_sem=rs, device_id=target,
            device_id_type=MESH)

    beside = {"ctx": slot_of(z, x, 1 - c)}
    across = {"ctx": slot_of(z, 1 - x, c)}
    right = {"ctx": slot_of(z + 1, x, c)}
    left = {"ctx": slot_of(z - 1, x, c)}

    def core_copy(g, k, zz):
        xx = 1 - x if k == 0 else x
        return remote(dkv.at[part(g, slot_of(zz, xx, 1 - c))], core_in.at[g, k, zz],
                      cs.at[g, k, zz], cr.at[g, k, zz], beside)

    def x_copy(g, zz):
        return remote(x_out.at[g, zz], x_in.at[g, zz], xs.at[g, zz], xr.at[g, zz], across)

    def up_copy(g, zz):
        return remote(high_out.at[g, zz], high_in.at[g, zz], us.at[g, zz], ur.at[g, zz], right)

    def down_copy(g, zz):
        return remote(low_out.at[g, zz], low_in.at[g, zz], ls.at[g, zz], lr.at[g, zz], left)

    def target_of(i):
        if i == nz - 1:
            return z
        high = nz - 1 - i - jnp.where(i >= nz - 1 - z, 1, 0)
        low = i + jnp.where(i >= z, 1, 0)
        return jnp.where(z < nz // 2, high, low)

    def cross(g):
        for i in range(nz):
            zz = target_of(i)
            core_copy(g, 0, zz).wait_recv()
            x_out[g, zz] = (dkv[part(g, slot_of(zz, 1 - x, c))].astype(F32)
                            + core_in[g, 0, zz].astype(F32)).astype(BF16)
            x_copy(g, zz).start()

    def local_sum(g, zz):
        core_copy(g, 1, zz).wait_recv()
        x_copy(g, zz).wait_recv()
        return (dkv[part(g, slot_of(zz, x, c))].astype(F32) + core_in[g, 1, zz].astype(F32)
                + x_in[g, zz].astype(F32))

    def tick(g, tau):
        @pl.when(z <= tau)
        def _():
            zz = nz - 1 - tau + z
            high_out[g, zz] = local_sum(g, zz).astype(BF16)

            @pl.when(z > 0)
            def _():
                up_copy(g, zz).wait_recv()
                high_out[g, zz] = (high_out[g, zz].astype(F32)
                                   + high_in[g, zz].astype(F32)).astype(BF16)

            up_copy(g, zz).start()

        @pl.when(nz - 1 - z <= tau)
        def _():
            zz = tau - (nz - 1 - z)
            low_out[g, zz] = local_sum(g, zz).astype(BF16)

            @pl.when(z < nz - 1)
            def _():
                down_copy(g, zz).wait_recv()
                low_out[g, zz] = (low_out[g, zz].astype(F32)
                                  + low_in[g, zz].astype(F32)).astype(BF16)

            down_copy(g, zz).start()

    def settle(g):
        at = lanes(g * HEAD_DIM, HEAD_DIM)
        grads[:, :, at] = local_sum(g, z)

        @pl.when(z > 0)
        def _():
            up_copy(g, z).wait_recv()
            grads[:, :, at] = grads[:, :, at] + high_in[g, z].astype(F32)

        @pl.when(z < nz - 1)
        def _():
            down_copy(g, z).wait_recv()
            grads[:, :, at] = grads[:, :, at] + low_in[g, z].astype(F32)

    def attend(g, h):
        k = kv_ref[:, lanes(g * HEAD_DIM, HEAD_DIM)]
        v = kv_ref[:, lanes(width + g * HEAD_DIM, HEAD_DIM)]
        cols = lanes((g * per_group + h) * HEAD_DIM, HEAD_DIM)
        band = slice(h * rows, (h + 1) * rows)
        q, do = q_ref[:, cols], do_ref[:, cols]
        s = lax.dot_general(q, k, NT, preferred_element_type=F32) * scale + bias[...]
        e = jnp.exp(s - jnp.max(s, axis=1, keepdims=True))
        p = e * (1.0 / jnp.sum(e, axis=1, keepdims=True))
        half = p.astype(BF16)
        p_all[band, :] = half
        attended = jnp.dot(half, v, preferred_element_type=F32).astype(BF16)
        delta = jnp.sum(do.astype(F32) * attended.astype(F32), axis=1, keepdims=True)
        dp = lax.dot_general(do, v, NT, preferred_element_type=F32)
        ds = (p * (dp - delta) * scale).astype(BF16)
        ds_all[band, :] = ds
        dq[:, cols] = jnp.dot(ds, k, preferred_element_type=F32).astype(BF16)

    def group_grads(g):
        heads = [lanes((g * per_group + h) * HEAD_DIM, HEAD_DIM) for h in range(per_group)]
        qs = jnp.concatenate([q_ref[:, at] for at in heads], axis=0)
        dos = jnp.concatenate([do_ref[:, at] for at in heads], axis=0)
        dk = lax.dot_general(qs, ds_all[...], TN, preferred_element_type=F32)
        dkv[g, 0] = dk.astype(BF16).T
        dv = lax.dot_general(dos, p_all[...], TN, preferred_element_type=F32)
        dkv[g, 1] = dv.astype(BF16).T
        for kind in range(2):
            for i in range(nz):
                core_copy(g, kind, target_of(i)).start()

    tile = 512
    tiles = dim // tile

    def h_tile(t, carry):
        at = pl.ds(pl.multiple_of(t * tile, tile), tile)
        hidden[:, at] = lax.dot_general(dq[...], wq[at, :], NT, preferred_element_type=F32)
        return carry

    def step(t, carry):
        @pl.when(t < kvh)
        def _():
            kv_load(t, 0).wait()
            kv_load(t, 1).wait()
            for h in range(per_group // 2):
                attend(t, h)

        @pl.when(t == kvh)
        def _():
            loads[0].wait()

        @pl.when(t >= kvh)
        def _():
            e = t - kvh
            lax.fori_loop(tiles * e // (nz + 1), tiles * (e + 1) // (nz + 1), h_tile, 0)

        for stage in range(1, nz + 2):
            g = t - stage

            @pl.when((g >= 0) & (g < kvh))
            def _():
                if stage == 1:
                    cross(g)
                elif stage <= nz:
                    tick(g, stage - 2)
                else:
                    settle(g)

        @pl.when(t < kvh)
        def _():
            for h in range(per_group // 2, per_group):
                attend(t, h)
            group_grads(t)

        return carry

    lax.fori_loop(0, kvh + nz + 1, step, 0)
    loads[1].wait()
    loads[2].wait()

    def finish(start):
        at = pl.ds(pl.multiple_of(start, chunk), chunk)
        return (hidden[:, at]
                + lax.dot_general(grads[0].astype(BF16), wk[at, :], NT, preferred_element_type=F32)
                + lax.dot_general(grads[1].astype(BF16), wv[at, :], NT, preferred_element_type=F32))

    per = share // chunk

    def h_copy(p, k):
        return remote(h_out.at[p - 1, k], h_in.at[p - 1, k], hs.at[p - 1, k], hr.at[p - 1, k],
                      {"head": lax.rem(head + p, nh)})

    for p in range(1, nh):
        for k in range(per):
            h_out[p - 1, k] = finish(lax.rem(head + p, nh) * share + k * chunk).astype(BF16)
            h_copy(p, k).start()
    inv = stat_ref[:, 0:1]
    product = stat_ref[:, 128:129]
    squares = stat_ref[:, 256:257]
    for k in range(per):
        hidden[:, k * chunk:(k + 1) * chunk] = finish(head * share + k * chunk)
    inner = jnp.zeros((rows, 1), F32)
    for k in range(per):
        cols = slice(k * chunk, (k + 1) * chunk)
        grad = hidden[:, cols]
        for p in range(1, nh):
            h_copy(p, k).wait_recv()
            grad = grad + h_in[p - 1, k].astype(F32)
        scaled = grad * gain_ref[:, pl.ds(pl.multiple_of(head * share + k * chunk, chunk), chunk)]
        hidden[:, cols] = scaled
        inner = inner + jnp.sum(scaled * (x_ref[:, cols].astype(F32) * inv), axis=1, keepdims=True)
    part_out[...] = jnp.broadcast_to(inner, part_out.shape)

    def p_copy(p):
        return remote(part_out, part_in.at[p - 1], ps.at[p - 1], pr.at[p - 1],
                      {"head": lax.rem(head + p, nh)})

    for p in range(1, nh):
        p_copy(p).start()
    for p in range(1, nh):
        p_copy(p).wait_recv()
        inner = inner + part_in[p - 1][:, 0:1]
    saliency = product + inner - (inner / dim) * squares
    sal_ref[...] = jnp.broadcast_to(saliency, (rows, 128)).T[0:1, :]
    inner = inner / dim
    for k in range(per):
        cols = slice(k * chunk, (k + 1) * chunk)
        unit = x_ref[:, cols].astype(F32) * inv
        out_ref[:, cols] = (dy_ref[:, cols].astype(F32)
                            + (hidden[:, cols] - unit * inner) * inv).astype(BF16)

    def drain(g, carry):
        for zz in range(nz):
            core_copy(g, 0, zz).wait_send()
            core_copy(g, 1, zz).wait_send()
            x_copy(g, zz).wait_send()
            pl.when(z < zz)(lambda zz=zz: up_copy(g, zz).wait_send())
            pl.when(z > zz)(lambda zz=zz: down_copy(g, zz).wait_send())
        return carry

    lax.fori_loop(0, kvh, drain, 0)
    for p in range(1, nh):
        for k in range(per):
            h_copy(p, k).wait_send()
        p_copy(p).wait_send()


def back(nz, nh, pq, pk, q, do, kv, x, dy, gain, stat, wq, wk, wv):
    rows, share = x.shape
    width = wk.shape[1]
    kvh = width // HEAD_DIM
    length = kv.shape[0]
    wide = q.shape[1] // kvh
    dim = nh * share
    chunk = min(512, share)
    per = share // chunk
    piece = (kvh, nz, 2, rows, HEAD_DIM)
    dma = pltpu.SemaphoreType.DMA
    peers = max(1, nh - 1)
    hops = dma((kvh, nz))
    return pl.pallas_call(
        functools.partial(back_kernel, nz, nh, chunk),
        out_shape=(
            jax.ShapeDtypeStruct((rows, share), BF16),
            jax.ShapeDtypeStruct((1, rows), F32),
        ),
        in_specs=[VM] * 4 + [ANY] + [VM] * 4 + [ANY] * 3,
        out_specs=(VM, VM),
        scratch_shapes=[
            pltpu.VMEM(kv.shape, BF16),
            pltpu.VMEM(wq.shape, BF16), pltpu.VMEM(wk.shape, BF16), pltpu.VMEM(wv.shape, BF16),
            pltpu.VMEM((rows, length), F32),
            pltpu.VMEM((wide // HEAD_DIM * rows, length), BF16),
            pltpu.VMEM((wide // HEAD_DIM * rows, length), BF16),
            pltpu.VMEM(q.shape, BF16),
            pltpu.VMEM((kvh, 2, length, HEAD_DIM), BF16),
            pltpu.VMEM((rows, dim), F32),
            pltpu.VMEM((kvh, 2, nz, 2, rows, HEAD_DIM), BF16),
            pltpu.VMEM(piece, BF16), pltpu.VMEM(piece, BF16),
            pltpu.VMEM(piece, BF16), pltpu.VMEM(piece, BF16),
            pltpu.VMEM(piece, BF16), pltpu.VMEM(piece, BF16),
            pltpu.VMEM((2, rows, width), F32),
            pltpu.VMEM((peers, per, rows, chunk), BF16),
            pltpu.VMEM((peers, per, rows, chunk), BF16),
            pltpu.VMEM((rows, 128), F32), pltpu.VMEM((peers, rows, 128), F32),
            dma((2, kvh)), dma((3,)), dma((kvh, 2, nz)), dma((kvh, 2, nz)),
            hops, hops, hops, hops, hops, hops,
            dma((peers, per)), dma((peers, per)), dma((peers,)), dma((peers,)),
        ],
        compiler_params=pltpu.CompilerParams(
            collective_id=1, has_side_effects=True, vmem_limit_bytes=VMEM_LIMIT),
        name="back",
    )(pq, pk, q, do, kv, x, dy, gain, stat, wq, wk, wv)


def fused_kernel(nz, order_hbm, lengths_hbm, x_ref, dy_ref, gain_hbm,
                 wq_ref, wk_ref, wv_ref, wo_ref, out_ref, sal_ref,
                 wq, wk, wv, wo, xall, dyall, xg, acc_kv, acc2, inv_ref, vx,
                 kv_own, kvs, q_out, do_out, qs, dos, qt, dot_, bias, ee, acc_o, m_run, stat,
                 dq_own, part, up_in, down_in, fin, dkvr,
                 h_out, h_in, part_out, part_in, gain_ref, order_ref, lengths_ref,
                 isem, wsem, lsem, xs, xr, dys, dyr, ks, kr, zus, zds, zr, qsem, qr, dsem, dr,
                 us, ur, ls, lr, gs, gr, fs, fr, hs, hr, ps, pr):
    me, z, x, c = coords()
    head = lax.axis_index("head")
    rows, share = x_ref.shape
    dim = 2 * share
    width = wk_ref.shape[1]
    slab = SLAB * rows
    wide = wq_ref.shape[1] // SLAB
    per_group = wide // HEAD_DIM
    rc = rows // HALVES
    block = SLAB * rc
    kv = 2 * HEAD_DIM
    scale = HEAD_DIM ** (-0.5)
    j = x * 2 + c
    gg = wo.at[:, 0:block]
    dq_slab = wo.at[0:slab, block:block + wide]
    peer = 1 - head
    mine = pl.ds(pl.multiple_of(head * share, share), share)
    theirs = pl.ds(pl.multiple_of(peer * share, share), share)

    own = [
        pltpu.make_async_copy(x_ref, xall.at[head], lsem.at[0]),
        pltpu.make_async_copy(dy_ref, dyall.at[head], lsem.at[1]),
    ]
    small = [pltpu.make_async_copy(a, b, isem.at[i]) for i, (a, b) in enumerate(
        ((order_hbm, order_ref), (lengths_hbm, lengths_ref), (gain_hbm, gain_ref)))]
    for copy in small:
        copy.start()
    own[0].start()
    load_k = pltpu.make_async_copy(wk_ref, wk, wsem.at[0])
    load_v = pltpu.make_async_copy(wv_ref, wv, wsem.at[1])
    load_q = [pltpu.make_async_copy(wq_ref.at[at, :], wq.at[at, :], wsem.at[2 + i])
              for i, at in enumerate((mine, theirs))]
    load_o = [pltpu.make_async_copy(wo_ref.at[:, at], wo, wsem.at[4 + i])
              for i, at in enumerate((mine, theirs))]
    load_k.start()
    load_v.start()
    load_q[0].start()
    own[1].start()
    load_o[0].start()
    load_q[1].start()

    def member(p):
        xx = x if p < 2 else 1 - x
        cc = c if p % 2 == 0 else 1 - c
        return xx, cc, xx * 2 + cc

    barrier = pltpu.get_barrier_semaphore()

    def greet(target):
        pl.semaphore_signal(barrier, inc=1, device_id=target, device_id_type=MESH)

    greet({"head": peer})
    for p in range(1, SLAB):
        greet({"ctx": slot_of(z, *member(p)[:2])})
    pl.when(z > 0)(lambda: greet({"ctx": slot_of(z - 1, x, c)}))
    pl.when(z < nz - 1)(lambda: greet({"ctx": slot_of(z + 1, x, c)}))

    @pl.when((z > 0) & (z < nz - 1))
    def _():
        pl.semaphore_wait(barrier, SLAB + 2)

    @pl.when((z == 0) | (z == nz - 1))
    def _():
        pl.semaphore_wait(barrier, SLAB + 1)

    def remote(src, dst, ss, rs, target):
        return pltpu.make_async_remote_copy(
            src_ref=src, dst_ref=dst, send_sem=ss, recv_sem=rs, device_id=target,
            device_id_type=MESH)

    def to_member(p, src, dst, ss, rs):
        xx, cc, _ = member(p)
        return remote(src, dst, ss, rs, {"ctx": slot_of(z, xx, cc)})

    right = {"ctx": slot_of(z + 1, x, c)}
    left = {"ctx": slot_of(z - 1, x, c)}

    def span(start, size):
        return pl.ds(pl.multiple_of(start, size), size)

    def x_copy(a):
        at = slice(a * rc, (a + 1) * rc)
        return remote(x_ref.at[at, :], xall.at[head, at, :], xs.at[a], xr.at[a], {"head": peer})

    tile = wide
    fd = min(1024, share)
    feats = share // fd

    def dy_copy(f):
        at = slice(f * fd, (f + 1) * fd)
        return remote(dy_ref.at[:, at], dyall.at[head, :, at], dys.at[f], dyr.at[f], {"head": peer})

    for a in range(HALVES):
        x_copy(a).start()
    for f in range(feats):
        dy_copy(f).start()

    def make_bias():
        vx[:, HEAD_DIM:kv] = jnp.ones((slab, HEAD_DIM), BF16)
        place_q, owner_q = timeline_place(
            lax.broadcasted_iota(jnp.int32, (slab, 1), 0) + z * slab, order_ref, lengths_ref)
        lane = lax.broadcasted_iota(jnp.int32, (1, nz * slab), 1)
        chunk_bits = rc.bit_length() - 1
        row_in = lane & (rc - 1)
        member_in = jnp.right_shift(lane, chunk_bits) & (SLAB - 1)
        half_in = jnp.right_shift(lane, chunk_bits + 2) & (HALVES - 1)
        slab_in = jnp.right_shift(lane, slab.bit_length() - 1)
        place_k, owner_k = timeline_place(
            slab_in * slab + member_in * rows + half_in * rc + row_in, order_ref, lengths_ref)
        for zz in range(nz):
            for a in range(HALVES):
                at = slice(zz * slab + a * block, zz * slab + (a + 1) * block)
                allowed = (owner_q == owner_k[:, at]) & (place_k[:, at] <= place_q)
                bias[zz, :, a * block:(a + 1) * block] = jnp.where(allowed, 0.0, -1e30).astype(BF16)

    def squares(v):
        return jnp.sum(v * v, axis=1, keepdims=True)

    def kv_own_half():
        own[0].wait()
        v = xall[head].astype(F32)
        inv_ref[:, 2:3] = squares(v)
        xg[head] = (v * gain_ref[:, mine]).astype(BF16)
        load_k.wait()
        acc_kv[0] = jnp.dot(xg[head], wk[mine, :], preferred_element_type=F32)
        load_v.wait()
        acc_kv[1] = jnp.dot(xg[head], wv[mine, :], preferred_element_type=F32)

    def q_half(t, carry):
        at = span(t * tile, tile)
        acc2[0, :, at] = jnp.dot(xg[head], wq[mine, at], preferred_element_type=F32)
        return carry

    def do_half(t, carry):
        at = span(t * tile, tile)
        acc2[1, :, at] = lax.dot_general(dyall[head], wo[at, :], NT, preferred_element_type=F32)
        return carry

    def q_own():
        load_q[0].wait()
        lax.fori_loop(0, SLAB, q_half, 0)

    def do_own(first, last):
        if first == 0:
            own[1].wait()
            load_o[0].wait()
        lax.fori_loop(first, last, do_half, 0)
        if last == SLAB:
            load_o[1].start()

    def kv_copy(p, a):
        jt = member(p)[2]
        dst = kvs.at[z, a, span(j * rc, rc), :]
        return to_member(p, kv_own.at[a, jt], dst, ks.at[a, p], kr.at[a, j])

    def kv_arrived(p, a):
        jt = member(p)[2]
        to_member(p, kv_own.at[a, jt], kvs.at[z, a, span(jt * rc, rc), :],
                  ks.at[a, p], kr.at[a, jt]).wait_recv()

    def make_kv(a):
        x_copy(a).wait_recv()
        at = slice(a * rc, (a + 1) * rc)
        v = xall[peer, at, :].astype(F32)
        total = inv_ref[at, 2:3] + squares(v)
        inv = 1.0 / jnp.sqrt(total / dim + 1e-05)
        inv_ref[at, 0:1] = inv
        inv_ref[at, 1:2] = total * inv * inv
        xg[peer, at, :] = (v * gain_ref[:, theirs]).astype(BF16)
        lhs = xg[peer, at, :]
        for i, w in enumerate((wk, wv)):
            got = (acc_kv[i, at, :] + jnp.dot(lhs, w[theirs, :], preferred_element_type=F32)) * inv
            got = got.astype(BF16)
            for jj in range(SLAB):
                kv_own[a, jj, :, i * HEAD_DIM:(i + 1) * HEAD_DIM] = (
                    got[:, jj * HEAD_DIM:(jj + 1) * HEAD_DIM])
        for p in (2, 3, 1):
            kv_copy(p, a).start()
        kvs[z, a, span(j * rc, rc), :] = kv_own[a, j]

    def piece(zz, a, s):
        return kvs.at[zz, a, span(s * 2 * rc, 2 * rc), :]

    def z_up(zz, a, s):
        return remote(piece(zz, a, s), piece(zz, a, s), zus.at[zz, a, s], zr.at[zz, a, s], right)

    def z_down(zz, a, s):
        return remote(piece(zz, a, s), piece(zz, a, s), zds.at[zz, a, s], zr.at[zz, a, s], left)

    def gather_own(a):
        kv_arrived(1, a)
        for s, peers in ((x, ()), (1 - x, (2, 3))):
            for p in peers:
                kv_arrived(p, a)
            pl.when(z < nz - 1)(lambda s=s: z_up(z, a, s).start())
            pl.when(z > 0)(lambda s=s: z_down(z, a, s).start())

    def order(t):
        near = jnp.where(z < nz // 2, z, nz - 1 - z)
        d = (t + 1) // 2
        o = jnp.where(t <= 2 * near, near + d if t % 2 else near - d, t)
        return jnp.where(z < nz // 2, o, nz - 1 - o)

    def travels(zz):
        return ((zz < z) & (z < nz - 1)) | ((zz > z) & (z > 0))

    def take(t, a):
        zz = order(t)

        @pl.when(travels(zz))
        def _():
            for s in range(2):
                z_up(zz, a, s).wait_recv()
                pl.when(zz < z)(lambda s=s: z_up(zz, a, s).start())
                pl.when(zz > z)(lambda s=s: z_down(zz, a, s).start())

    def keep(t):
        zz = order(t)

        @pl.when(jnp.logical_not(travels(zz)))
        def _():
            for a in range(HALVES):
                for s in range(2):
                    z_up(zz, a, s).wait_recv()

    def shared(p, src, dst, ss, rs):
        jt = member(p)[2]
        return to_member(p, src.at[jt], dst.at[span(j * rows, rows), :], ss.at[p], rs.at[j])

    def shared_arrived(p, src, dst, ss, rs):
        jt = member(p)[2]
        to_member(p, src.at[jt], dst.at[span(jt * rows, rows), :], ss.at[p], rs.at[jt]).wait_recv()

    def q_tile(p):
        jt = member(p)[2]
        at = span(jt * tile, tile)
        got = acc2[0, :, at] + jnp.dot(
            xg[peer], wq[theirs, at], preferred_element_type=F32)
        q_out[jt] = (got * (inv_ref[:, 0:1] * (scale * LOG2E))).astype(BF16)
        if p:
            shared(p, q_out, qs, qsem, qr).start()
        else:
            qs[span(j * rows, rows), :] = q_out[jt]

    def do_part(f, first=0, last=SLAB):
        if f == 0 and first == 0:
            load_o[1].wait()
        if first == 0:
            dy_copy(f).wait_recv()
        at = slice(f * fd, (f + 1) * fd)
        if f < feats - 1:
            def body(t, carry):
                cols = span(t * tile, tile)
                acc2[1, :, cols] = acc2[1, :, cols] + lax.dot_general(
                    dyall[peer, :, at], wo[cols, at], NT, preferred_element_type=F32)
                return carry

            lax.fori_loop(first, last, body, 0)
            return
        for p in (3, 2, 1, 0):
            jt = member(p)[2]
            cols = span(jt * tile, tile)
            do_out[jt] = (acc2[1, :, cols] + lax.dot_general(
                dyall[peer, :, at], wo[cols, at], NT, preferred_element_type=F32)).astype(BF16)
            if p:
                shared(p, do_out, dos, dsem, dr).start()
            else:
                dos[span(j * rows, rows), :] = do_out[jt]

    lane_at = lax.broadcasted_iota(jnp.int32, (slab, HEAD_DIM), 1)

    def forward(t, hook=None):
        zz = order(t)
        vx[:, 0:HEAD_DIM] = kvs[zz, :, :, HEAD_DIM:kv].reshape(slab, HEAD_DIM)
        def one(hh):
            cols = span(hh * HEAD_DIM, HEAD_DIM)
            k = kvs[zz, :, :, 0:HEAD_DIM].reshape(slab, HEAD_DIM)
            s = lax.dot_general(qs[:, cols], k, NT, preferred_element_type=F32)
            s = s + bias[zz].astype(F32)
            m = jnp.broadcast_to(jnp.max(s, axis=1, keepdims=True), (slab, HEAD_DIM))
            if t:
                old = m_run[hh]
                m = jnp.maximum(m, old)
            half = jnp.exp2(s - jnp.concatenate([m] * SLAB, axis=1)).astype(BF16)
            ee[t, span(hh * slab, slab), :] = half
            o = jnp.dot(half, vx[...], preferred_element_type=F32)
            if t:
                alpha = jnp.exp2(old - m)
                o = o + acc_o[hh] * jnp.concatenate([alpha, alpha], axis=1)
            stat[hh] = jnp.where(lane_at == t, m, stat[hh]) if t else m
            m_run[hh] = m
            acc_o[hh] = o

        def pair(i, carry):
            one(2 * i)
            one(2 * i + 1)
            if hook is not None:
                pl.when(i == 0)(hook)
            return carry

        lax.fori_loop(0, per_group // 2, pair, 0)

    def settle():
        def one(hh, carry):
            cols = span(hh * HEAD_DIM, HEAD_DIM)
            do = dos[:, cols]
            inv_l = 1.0 / acc_o[hh, :, HEAD_DIM:kv]
            attended = (acc_o[hh, :, 0:HEAD_DIM] * inv_l).astype(BF16)
            delta = jnp.sum(do.astype(F32) * attended.astype(F32), axis=1, keepdims=True)
            stat[hh] = jnp.where(lane_at == HEAD_DIM - 1, delta, jnp.exp2(stat[hh] - m_run[hh]) * inv_l)
            acc_o[hh, :, 0:HEAD_DIM] = jnp.zeros((slab, HEAD_DIM), F32)
            dot_[:, span(hh * slab, slab)] = do.T
            return carry

        lax.fori_loop(0, per_group, one, 0)

    def turn_q():
        def one(hh, carry):
            qt[:, span(hh * slab, slab)] = qs[:, span(hh * HEAD_DIM, HEAD_DIM)].T
            return carry

        lax.fori_loop(0, per_group, one, 0)

    def backward(t, a):
        zz = order(t)
        half = slice(a * block, (a + 1) * block)

        def one(hh):
            k = kvs[zz, a, :, 0:HEAD_DIM]
            v = kvs[zz, a, :, HEAD_DIM:kv]
            cols = span(hh * HEAD_DIM, HEAD_DIM)
            at = span(hh * slab, slab)
            dp = lax.dot_general(dos[:, cols], v, NT, preferred_element_type=F32)
            p = ee[t, at, half].astype(F32) * stat[hh, :, t:t + 1]
            ee[t, at, half] = p.astype(BF16)
            g = (p * (dp - stat[hh, :, 127:128])).astype(BF16)
            gg[at, :] = g
            acc_o[hh, :, 0:HEAD_DIM] = (acc_o[hh, :, 0:HEAD_DIM]
                                        + jnp.dot(g, k, preferred_element_type=F32))

        def pair(i, carry):
            one(2 * i)
            one(2 * i + 1)
            return carry

        lax.fori_loop(0, per_group // 2, pair, 0)
        dk = jnp.dot(qt[...], gg[...], preferred_element_type=F32) * LN2
        dv = jnp.dot(dot_[...], ee[t, :, half], preferred_element_type=F32)
        part[zz, a, :, 0:HEAD_DIM] = dk.astype(BF16).T
        part[zz, a, :, HEAD_DIM:kv] = dv.astype(BF16).T

    def up_copy(zz, a):
        return remote(part.at[zz, a], up_in.at[zz, a], us.at[zz, a], ur.at[zz, a], right)

    def down_copy(zz, a):
        return remote(part.at[zz, a], down_in.at[zz, a], ls.at[zz, a], lr.at[zz, a], left)

    def send_part(t, a):
        zz = order(t)
        pl.when((zz > z) & (z == 0))(lambda: up_copy(zz, a).start())
        pl.when((zz < z) & (z == nz - 1))(lambda: down_copy(zz, a).start())

    def pass_part(t, a):
        zz = order(t)

        @pl.when((zz > z) & (z > 0))
        def _():
            up_copy(zz, a).wait_recv()
            part[zz, a] = (part[zz, a].astype(F32) + up_in[zz, a].astype(F32)).astype(BF16)
            up_copy(zz, a).start()

        @pl.when((zz < z) & (z < nz - 1))
        def _():
            down_copy(zz, a).wait_recv()
            part[zz, a] = (part[zz, a].astype(F32) + down_in[zz, a].astype(F32)).astype(BF16)
            down_copy(zz, a).start()

    def fin_copy(p, a):
        jt = member(p)[2]
        return to_member(p, fin.at[a, span(jt * rc, rc), :], dkvr.at[a, j], fs.at[a, p], fr.at[a, j])

    def fin_arrived(p, a):
        jt = member(p)[2]
        to_member(p, fin.at[a, span(jt * rc, rc), :], dkvr.at[a, jt], fs.at[a, p],
                  fr.at[a, jt]).wait_recv()

    def finish_part(a):
        fin[a] = part[z, a]

        @pl.when(z > 0)
        def _():
            up_copy(z, a).wait_recv()
            fin[a] = (fin[a].astype(F32) + up_in[z, a].astype(F32)).astype(BF16)

        @pl.when(z < nz - 1)
        def _():
            down_copy(z, a).wait_recv()
            fin[a] = (fin[a].astype(F32) + down_in[z, a].astype(F32)).astype(BF16)

        for p in (3, 2, 1):
            fin_copy(p, a).start()
        dkvr[a, j] = fin[a, span(j * rc, rc), :]

    def dq_copy(p):
        jt = member(p)[2]
        return to_member(p, wo.at[span(jt * rows, rows), block:block + wide], dq_own.at[:, span(j * tile, tile)],
                         gs.at[p], gr.at[j])

    def dq_arrived(p):
        jt = member(p)[2]
        to_member(p, wo.at[span(jt * rows, rows), block:block + wide], dq_own.at[:, span(jt * tile, tile)],
                  gs.at[p], gr.at[jt]).wait_recv()

    for copy in small:
        copy.wait()
    make_bias()
    kv_own_half()
    q_own()
    make_kv(0)
    do_own(0, 2)
    gather_own(0)
    do_own(2, SLAB)
    make_kv(1)
    load_q[1].wait()
    q_tile(3)
    q_tile(2)
    q_tile(1)
    q_tile(0)
    take(1, 0)
    gather_own(1)
    do_part(0, 0, 2)
    for t in range(2, min(3, nz)):
        take(t, 0)
    do_part(0, 2, SLAB)
    take(1, 1)
    for p in (1, 2, 3):
        shared_arrived(p, q_out, qs, qsem, qr)

    def far():
        for t in range(3, nz):
            take(t, 0)

    forward(0, far)
    for t in range(2, min(3, nz)):
        take(t, 1)
    for f in range(1, feats):
        do_part(f)
    keep(1)
    forward(1)
    for t in range(3, nz):
        take(t, 1)
    turn_q()
    for t in range(2, nz):
        keep(t)
        forward(t)
    for p in (1, 2, 3):
        shared_arrived(p, do_out, dos, dsem, dr)
    settle()
    steps = [(nz - 1, a) for a in range(HALVES)]
    steps += [(t, a) for a in range(HALVES) for t in range(nz - 2, 0, -1)]
    steps += [(0, a) for a in range(HALVES)]
    lag = 3
    for i, (t, a) in enumerate(steps):
        backward(t, a)
        if t:
            send_part(t, a)
        if i >= lag and steps[i - lag][0]:
            pass_part(*steps[i - lag])
    for hh in range(per_group):
        dq_slab[:, hh * HEAD_DIM:(hh + 1) * HEAD_DIM] = (acc_o[hh, :, 0:HEAD_DIM] * scale).astype(BF16)
    for p in (3, 2, 1):
        dq_copy(p).start()
    dq_own[:, span(j * tile, tile)] = dq_slab[span(j * rows, rows), :]
    for step in steps[len(steps) - lag:]:
        if step[0]:
            pass_part(*step)
    product = jnp.zeros((rows, 1), F32)
    for h in range(2):
        product = product + jnp.sum(
            xall[h].astype(F32) * dyall[h].astype(F32), axis=1, keepdims=True)
    dq_arrived(1)
    hidden = acc2
    chunk = min(512, share)
    per = share // chunk

    def h_tile(half, xx, add):
        heads_at = span(xx * 2 * tile, 2 * tile)

        def body(k, carry):
            at = span(half * share + k * chunk, chunk)
            cols = span(k * chunk, chunk)
            got = lax.dot_general(dq_own[:, heads_at], wq[at, heads_at], NT,
                                  preferred_element_type=F32)
            hidden[half, :, cols] = hidden[half, :, cols] + got if add else got
            return carry

        lax.fori_loop(0, per, body, 0)

    h_tile(peer, x, False)
    finish_part(0)
    finish_part(1)
    dq_arrived(3)
    dq_arrived(2)
    h_tile(peer, 1 - x, True)
    for a in range(HALVES):
        for p in (1, 2, 3):
            fin_arrived(p, a)
    grads = [
        jnp.concatenate(
            [jnp.concatenate([dkvr[a, jj, :, i * HEAD_DIM:(i + 1) * HEAD_DIM] for jj in range(SLAB)],
                             axis=1) for a in range(HALVES)], axis=0)
        for i in range(2)
    ]

    def finish(half, k):
        at = span(half * share + k * chunk, chunk)
        return (hidden[half, :, k * chunk:(k + 1) * chunk]
                + lax.dot_general(grads[0], wk[at, :], NT, preferred_element_type=F32)
                + lax.dot_general(grads[1], wv[at, :], NT, preferred_element_type=F32))

    def h_copy(k):
        return remote(h_out.at[k], h_in.at[k], hs.at[k], hr.at[k], {"head": peer})

    inv = inv_ref[:, 0:1]
    inner = jnp.zeros((rows, 1), F32)

    def weighed(half, k, grad):
        scaled = grad * gain_ref[:, span(half * share + k * chunk, chunk)]
        unit = xall[half, :, k * chunk:(k + 1) * chunk].astype(F32) * inv
        return jnp.sum(scaled * unit, axis=1, keepdims=True)

    for k in range(per):
        grad = finish(peer, k)
        h_out[k] = grad.astype(BF16)
        h_copy(k).start()
        inner = inner + weighed(peer, k, grad)
    h_tile(head, x, False)
    h_tile(head, 1 - x, True)
    for k in range(per):
        grad = finish(head, k)
        hidden[head, :, k * chunk:(k + 1) * chunk] = grad
        inner = inner + weighed(head, k, grad)
    part_out[...] = jnp.broadcast_to(inner, (rows, 128)).T[0:8, :]
    p_copy = remote(part_out, part_in, ps, pr, {"head": peer})
    p_copy.start()
    p_copy.wait_recv()
    inner = inner + jnp.broadcast_to(part_in[0:1, :], (128, rows)).T[:, 0:1]
    saliency = product + inner - (inner / dim) * inv_ref[:, 1:2]
    sal_ref[...] = jnp.broadcast_to(saliency, (rows, 128)).T[0:1, :]
    inner = inner / dim
    for k in range(per):
        cols = slice(k * chunk, (k + 1) * chunk)
        unit = xall[head, :, cols].astype(F32) * inv
        h_copy(k).wait_recv()
        grad = hidden[head, :, cols] + h_in[k].astype(F32)
        scaled = grad * gain_ref[:, span(head * share + k * chunk, chunk)]
        out_ref[:, cols] = (dyall[head, :, cols].astype(F32)
                            + (scaled - unit * inner) * inv).astype(BF16)

    for a in range(HALVES):
        x_copy(a).wait_send()
        for p in (1, 2, 3):
            kv_copy(p, a).wait_send()
            fin_copy(p, a).wait_send()
        for zz in range(nz):
            pl.when(z < zz)(lambda zz=zz, a=a: up_copy(zz, a).wait_send())
            pl.when(z > zz)(lambda zz=zz, a=a: down_copy(zz, a).wait_send())
            for s in range(2):
                pl.when((zz <= z) & (z < nz - 1))(lambda zz=zz, a=a, s=s: z_up(zz, a, s).wait_send())
                pl.when((zz >= z) & (z > 0))(lambda zz=zz, a=a, s=s: z_down(zz, a, s).wait_send())
    for f in range(feats):
        dy_copy(f).wait_send()
    for p in (1, 2, 3):
        shared(p, q_out, qs, qsem, qr).wait_send()
        shared(p, do_out, dos, dsem, dr).wait_send()
        dq_copy(p).wait_send()
    for k in range(per):
        h_copy(k).wait_send()
    p_copy.wait_send()


def fused(nz, order, lengths, x, dy, gain, wq, wk, wv, wo):
    rows, share = x.shape
    dim = 2 * share
    hq, width = wq.shape[1], wk.shape[1]
    wide = hq // SLAB
    heads = wide // HEAD_DIM
    rc = rows // HALVES
    slab = SLAB * rows
    block = SLAB * rc
    kv = 2 * HEAD_DIM
    fd = min(1024, share)
    chunk = min(512, share)
    per = share // chunk
    feats = share // fd
    dma = pltpu.SemaphoreType.DMA
    vm = pltpu.VMEM
    return pl.pallas_call(
        functools.partial(fused_kernel, nz),
        out_shape=(
            jax.ShapeDtypeStruct((rows, share), BF16),
            jax.ShapeDtypeStruct((1, rows), F32),
        ),
        in_specs=[ANY] * 9,
        out_specs=(VM, VM),
        scratch_shapes=[
            vm(wq.shape, BF16), vm(wk.shape, BF16), vm(wv.shape, BF16), vm((hq, share), BF16),
            vm((2, rows, share), BF16), vm((2, rows, share), BF16), vm((2, rows, share), BF16),
            vm((2, rows, width), F32), vm((2, rows, share), F32), vm((rows, 128), F32),
            vm((slab, kv), BF16),
            vm((HALVES, SLAB, rc, kv), BF16), vm((nz, HALVES, block, kv), BF16),
            vm((SLAB, rows, wide), BF16), vm((SLAB, rows, wide), BF16),
            vm((slab, wide), BF16), vm((slab, wide), BF16),
            vm((HEAD_DIM, heads * slab), BF16), vm((HEAD_DIM, heads * slab), BF16),
            vm((nz, slab, slab), BF16),
            vm((nz, heads * slab, slab), BF16),
            vm((heads, slab, kv), F32), vm((heads, slab, HEAD_DIM), F32), vm((heads, slab, 128), F32),
            vm((rows, hq), BF16),
            vm((nz, HALVES, block, kv), BF16), vm((nz, HALVES, block, kv), BF16),
            vm((nz, HALVES, block, kv), BF16),
            vm((HALVES, block, kv), BF16), vm((HALVES, SLAB, rc, kv), BF16),
            vm((per, rows, chunk), BF16), vm((per, rows, chunk), BF16),
            vm((8, rows), F32), vm((8, rows), F32),
            vm((1, dim), F32), pltpu.SMEM(order.shape, jnp.int32), pltpu.SMEM(lengths.shape, jnp.int32),
            dma((3,)), dma((6,)), dma((2,)), dma((HALVES,)), dma((HALVES,)), dma((feats,)), dma((feats,)),
            dma((HALVES, SLAB)), dma((HALVES, SLAB)),
            dma((nz, HALVES, 2)), dma((nz, HALVES, 2)), dma((nz, HALVES, 2)),
            dma((SLAB,)), dma((SLAB,)), dma((SLAB,)), dma((SLAB,)),
            dma((nz, HALVES)), dma((nz, HALVES)), dma((nz, HALVES)), dma((nz, HALVES)),
            dma((SLAB,)), dma((SLAB,)), dma((HALVES, SLAB)), dma((HALVES, SLAB)),
            dma((per,)), dma((per,)), dma(()), dma(()),
        ],
        compiler_params=pltpu.CompilerParams(
            collective_id=2, has_side_effects=True, vmem_limit_bytes=VMEM_LIMIT),
        name="fused",
    )(order, lengths, x, dy, gain, wq, wk, wv, wo)


def local(inputs, out_grad, norm_gain, w_query, w_key, w_value, w_out, record_lengths, block_order):
    rows, share = inputs.shape
    n = lax.axis_size("ctx")
    nh = lax.axis_size("head")
    nz = n // 4
    gain = norm_gain[None, :]
    if nh == 2 and w_key.shape[1] == SLAB * HEAD_DIM:
        input_grad, saliency = fused(
            nz, block_order, record_lengths, inputs, out_grad, gain, w_query, w_key, w_value, w_out)
        return (input_grad, saliency.reshape(rows))
    q, do, kv, stat, pq, pk = front(
        nz, nh, block_order, record_lengths, inputs, out_grad, gain,
        w_query, w_key, w_value, w_out)
    input_grad, saliency = back(
        nz, nh, pq, pk, q, do, kv, inputs, out_grad, gain, stat, w_query, w_key, w_value)
    return (input_grad, saliency.reshape(rows))


def solution(mesh):
    placed = (
        P("ctx", "head"),
        P("ctx", "head"),
        P(),
        P(None, "head"),
        P(None, "head"),
        P(None, "head"),
        P("head", None),
        P(),
        P(),
    )
    return jax.shard_map(
        local, mesh=mesh, in_specs=placed, out_specs=(P("ctx", "head"), P("ctx")), check_vma=False
    )
```

```python
import functools

import jax
import jax.numpy as jnp
from jax import lax
from jax.experimental import pallas as pl
from jax.experimental.pallas import tpu as pltpu
from jax.sharding import PartitionSpec as P

HEAD_DIM = 128
BLOCK = 64
SLAB = 4
HALVES = 2
LOG2E = 1.4426950408889634
LN2 = 0.6931471805599453
NT = (((1,), (1,)), ((), ()))
TN = (((0,), (0,)), ((), ()))
F32 = jnp.float32
BF16 = jnp.bfloat16
MESH = pl.DeviceIdType.MESH
VM = pl.BlockSpec(memory_space=pltpu.VMEM)
ANY = pl.BlockSpec(memory_space=pl.ANY)
SM = pl.BlockSpec(memory_space=pltpu.SMEM)
VMEM_LIMIT = 67043328


def timeline_place(stored, order_ref, lengths_ref):
    block = jnp.right_shift(stored, 6)
    position = jnp.zeros(stored.shape, jnp.int32)
    for b in range(order_ref.shape[0]):
        position = jnp.where(block == b, order_ref[b], position)
    position = position * BLOCK + (stored & (BLOCK - 1))
    record = jnp.zeros(stored.shape, jnp.int32)
    start = 0
    for r in range(lengths_ref.shape[0]):
        record = record + jnp.where(position >= start, 1, 0)
        start = start + lengths_ref[r]
    return position, record


def coords():
    me = lax.axis_index("ctx")
    return me, me // 4, lax.rem(me // 2, 2), lax.rem(me, 2)


def slot_of(z, x, c):
    return (z * 2 + x) * 2 + c


def enter(nz, nh):
    _, z, x, c = coords()
    head = lax.axis_index("head")
    barrier = pltpu.get_barrier_semaphore()

    def greet(target):
        pl.semaphore_signal(barrier, inc=1, device_id=target, device_id_type=MESH)

    for p in range(1, nh):
        greet({"head": lax.rem(head + p, nh)})
    greet({"ctx": slot_of(z, 1 - x, c)})
    greet({"ctx": slot_of(z, x, 1 - c)})

    @pl.when(z > 0)
    def _():
        greet({"ctx": slot_of(z - 1, x, c)})

    @pl.when(z < nz - 1)
    def _():
        greet({"ctx": slot_of(z + 1, x, c)})

    @pl.when((z > 0) & (z < nz - 1))
    def _():
        pl.semaphore_wait(barrier, nh + 3)

    @pl.when((z == 0) | (z == nz - 1))
    def _():
        pl.semaphore_wait(barrier, nh + 2)


def front_kernel(nz, nh, order_ref, lengths_ref, x_ref, dy_ref, gain_ref,
                 wq_ref, wk_ref, wv_ref, wo_ref,
                 q_out, do_out, kv_out, stat_ref, pq_ref, pk_ref,
                 q_ref, do_ref, kv_ref, wq, wk, wv, wo, xall, dyall, normed,
                 wsem, lsem, osem, ssem, xs, xr, dys, dyr, ks, kr):
    me, z, x, c = coords()
    head = lax.axis_index("head")
    rows, share = x_ref.shape
    dim = nh * share
    hq = q_ref.shape[1]
    width = wk_ref.shape[1]
    loads = [
        pltpu.make_async_copy(a, b, wsem.at[i])
        for i, (a, b) in enumerate(((wk_ref, wk), (wv_ref, wv), (wq_ref, wq), (wo_ref, wo)))
    ]
    for load in loads:
        load.start()
    own = [
        pltpu.make_async_copy(x_ref, xall.at[head], lsem.at[0]),
        pltpu.make_async_copy(dy_ref, dyall.at[head], lsem.at[1]),
    ]
    for copy in own:
        copy.start()
    enter(nz, nh)

    def head_copies(src, dst, send, recv):
        return [
            pltpu.make_async_remote_copy(
                src_ref=src, dst_ref=dst.at[head], send_sem=send.at[p - 1], recv_sem=recv.at[p - 1],
                device_id={"head": lax.rem(head + p, nh)}, device_id_type=MESH)
            for p in range(1, nh)
        ]

    xc = head_copies(x_ref, xall, xs, xr)
    dyc = head_copies(dy_ref, dyall, dys, dyr)
    for copy in xc + dyc:
        copy.start()
    length = kv_ref.shape[0]
    pk_ref[0:1, :], pk_ref[1:2, :] = timeline_place(
        lax.broadcasted_iota(jnp.int32, (1, length), 1), order_ref, lengths_ref)
    pq_ref[:, 0:1], pq_ref[:, 1:2] = timeline_place(
        lax.broadcasted_iota(jnp.int32, (rows, 1), 0) + me * rows, order_ref, lengths_ref)
    own[0].wait()
    for copy in xc:
        copy.wait()
    total = jnp.zeros((rows, 1), F32)
    for j in range(nh):
        v = xall[j].astype(F32)
        total = total + jnp.sum(v * v, axis=1, keepdims=True)
    root = jnp.sqrt(total / dim + 1e-05)
    inv = 1.0 / root
    for j in range(nh):
        cols = slice(j * share, (j + 1) * share)
        normed[:, cols] = (xall[j].astype(F32) * inv * gain_ref[:, cols]).astype(BF16)

    def block(slot):
        return kv_ref.at[pl.ds(pl.multiple_of(slot * rows, rows), rows), :]

    def send(direction, slot, target):
        return pltpu.make_async_remote_copy(
            src_ref=block(slot), dst_ref=block(slot), send_sem=ks.at[direction, slot],
            recv_sem=kr.at[slot], device_id={"ctx": target}, device_id_type=MESH)

    def store(slot):
        return pltpu.make_async_copy(
            block(slot), kv_out.at[pl.ds(pl.multiple_of(slot * rows, rows), rows), :],
            ssem.at[slot])

    def arrived(slot):
        send(0, slot, me).wait_recv()
        store(slot).start()

    mine = pl.ds(pl.multiple_of(me * rows, rows), rows)
    loads[0].wait()
    kv_ref[mine, :width] = jnp.dot(normed[...], wk[...], preferred_element_type=F32).astype(BF16)
    loads[1].wait()
    kv_ref[mine, width:] = jnp.dot(normed[...], wv[...], preferred_element_type=F32).astype(BF16)

    right = slot_of(z + 1, x, c)
    left = slot_of(z - 1, x, c)
    across = slot_of(z, 1 - x, c)
    beside = slot_of(z, x, 1 - c)

    def spread(s, act):
        if s == 0:
            pl.when(z < nz - 1)(lambda: act(send(0, me, right)))
            pl.when(z > 0)(lambda: act(send(1, me, left)))
            act(send(2, me, across))
            act(send(3, me, beside))
            return
        low, high = slot_of(z - s, x, c), slot_of(z + s, x, c)

        @pl.when(z - s >= 0)
        def _():
            if act is start:
                arrived(low)
            pl.when(z < nz - 1)(lambda: act(send(0, low, right)))
            act(send(2, low, across))
            act(send(3, low, beside))

        @pl.when(z + s < nz)
        def _():
            if act is start:
                arrived(high)
            pl.when(z > 0)(lambda: act(send(1, high, left)))
            act(send(2, high, across))
            act(send(3, high, beside))

    def hand_over(s, act):
        def one(slot):
            if act is start:
                arrived(slot)
            act(send(3, slot, beside))

        if s == 0:
            one(slot_of(z, 1 - x, c))
            return
        pl.when(z - s >= 0)(lambda: one(slot_of(z - s, 1 - x, c)))
        pl.when(z + s < nz)(lambda: one(slot_of(z + s, 1 - x, c)))

    def start(copy):
        copy.start()

    def sent(copy):
        copy.wait_send()

    spread(0, start)
    store(me).start()

    loads[2].wait()
    tq = min(512, hq)

    def q_tile(t, carry):
        cols = pl.ds(pl.multiple_of(t * tq, tq), tq)
        q_ref[:, cols] = jnp.dot(normed[...], wq[:, cols], preferred_element_type=F32).astype(BF16)
        return carry

    lax.fori_loop(0, hq // tq, q_tile, 0)
    q_store = pltpu.make_async_copy(q_ref, q_out, osem.at[0])
    q_store.start()
    spread(1, start)

    own[1].wait()
    for copy in dyc:
        copy.wait()
    loads[3].wait()

    def do_tile(t, carry):
        cols = pl.ds(pl.multiple_of(t * tq, tq), tq)
        acc = jnp.zeros((rows, tq), F32)
        for j in range(nh):
            acc = acc + lax.dot_general(
                dyall[j], wo[cols, j * share:(j + 1) * share], NT, preferred_element_type=F32)
        do_ref[:, cols] = acc.astype(BF16)
        return carry

    tiles = hq // tq
    gaps = nz - 2
    for s in range(2, nz):
        lax.fori_loop(tiles * (s - 2) // gaps, tiles * (s - 1) // gaps, do_tile, 0)
        if s == nz - 1:
            do_store = pltpu.make_async_copy(do_ref, do_out, osem.at[1])
            do_store.start()
        spread(s, start)
        hand_over(s - 2, start)

    product = jnp.zeros((rows, 1), F32)
    for j in range(nh):
        product = product + jnp.sum(
            xall[j].astype(F32) * dyall[j].astype(F32), axis=1, keepdims=True)
    stat_ref[:, 0:128] = jnp.broadcast_to(inv, (rows, 128))
    stat_ref[:, 128:256] = jnp.broadcast_to(product, (rows, 128))
    stat_ref[:, 256:384] = jnp.broadcast_to(total * inv * inv, (rows, 128))

    for s in range(nz - 2, nz):
        hand_over(s, start)
    for zz in range(nz):
        for xx in range(2):
            arrived(slot_of(zz, xx, 1 - c))
    for s in range(nz):
        spread(s, sent)
        hand_over(s, sent)
    for slot in range(4 * nz):
        store(slot).wait()
    q_store.wait()
    do_store.wait()


def front(nz, nh, order, lengths, x, dy, gain, wq, wk, wv, wo):
    rows, share = x.shape
    hq, width = wq.shape[1], wk.shape[1]
    n = 4 * nz
    dma = pltpu.SemaphoreType.DMA
    return pl.pallas_call(
        functools.partial(front_kernel, nz, nh),
        out_shape=(
            jax.ShapeDtypeStruct((rows, hq), BF16),
            jax.ShapeDtypeStruct((rows, hq), BF16),
            jax.ShapeDtypeStruct((n * rows, 2 * width), BF16),
            jax.ShapeDtypeStruct((rows, 384), F32),
            jax.ShapeDtypeStruct((rows, 2), jnp.int32),
            jax.ShapeDtypeStruct((2, n * rows), jnp.int32),
        ),
        in_specs=[SM, SM, VM, VM, VM, ANY, ANY, ANY, ANY],
        out_specs=(ANY, ANY, ANY, VM, VM, VM),
        scratch_shapes=[
            pltpu.VMEM((rows, hq), BF16), pltpu.VMEM((rows, hq), BF16),
            pltpu.VMEM((n * rows, 2 * width), BF16),
            pltpu.VMEM(wq.shape, BF16), pltpu.VMEM(wk.shape, BF16),
            pltpu.VMEM(wv.shape, BF16), pltpu.VMEM(wo.shape, BF16),
            pltpu.VMEM((nh, rows, share), BF16), pltpu.VMEM((nh, rows, share), BF16),
            pltpu.VMEM((rows, nh * share), BF16),
            dma((4,)), dma((2,)), dma((2,)), dma((n,)), dma((nh,)), dma((nh,)), dma((nh,)), dma((nh,)),
            dma((4, n)), dma((n,)),
        ],
        compiler_params=pltpu.CompilerParams(
            collective_id=0, has_side_effects=True, vmem_limit_bytes=VMEM_LIMIT),
        name="front",
    )(order, lengths, x, dy, gain, wq, wk, wv, wo)


def back_kernel(nz, nh, chunk, pq_ref, pk_ref, q_ref, do_ref, kv_hbm, x_ref, dy_ref, gain_ref,
                stat_ref, wq_ref, wk_ref, wv_ref, out_ref, sal_ref,
                kv_ref, wq, wk, wv, bias, ds_all, p_all, dq, dkv, hidden,
                core_in, x_out, x_in, low_out, low_in, high_out, high_in,
                grads, h_out, h_in, part_out, part_in,
                gsem, wsem, cs, cr, xs, xr, ls, lr, us, ur, hs, hr, ps, pr):
    me, z, x, c = coords()
    head = lax.axis_index("head")
    rows, share = x_ref.shape
    dim = nh * share
    hq = q_ref.shape[1]
    width = wk_ref.shape[1]
    kvh = width // HEAD_DIM
    per_group = hq // width
    scale = HEAD_DIM ** (-0.5)

    def kv_load(g, kind):
        at = pl.ds(pl.multiple_of(kind * width + g * HEAD_DIM, HEAD_DIM), HEAD_DIM)
        return pltpu.make_async_copy(kv_hbm.at[:, at], kv_ref.at[:, at], gsem.at[kind, g])

    for g in range(kvh):
        kv_load(g, 0).start()
        kv_load(g, 1).start()
    loads = [
        pltpu.make_async_copy(a, b, wsem.at[i])
        for i, (a, b) in enumerate(((wq_ref, wq), (wk_ref, wk), (wv_ref, wv)))
    ]
    for load in loads:
        load.start()
    enter(nz, nh)
    place, owner = pq_ref[:, 0:1], pq_ref[:, 1:2]
    allowed = (owner == pk_ref[1:2, :]) & (pk_ref[0:1, :] <= place)
    bias[...] = jnp.where(allowed, 0.0, -1e30)

    def lanes(start, size):
        return pl.ds(pl.multiple_of(start, HEAD_DIM), size)

    def part(g, slot):
        return (g, slice(None), pl.ds(pl.multiple_of(slot * rows, rows), rows), slice(None))

    def remote(src, dst, ss, rs, target):
        return pltpu.make_async_remote_copy(
            src_ref=src, dst_ref=dst, send_sem=ss, recv_sem=rs, device_id=target,
            device_id_type=MESH)

    beside = {"ctx": slot_of(z, x, 1 - c)}
    across = {"ctx": slot_of(z, 1 - x, c)}
    right = {"ctx": slot_of(z + 1, x, c)}
    left = {"ctx": slot_of(z - 1, x, c)}

    def core_copy(g, k, zz):
        xx = 1 - x if k == 0 else x
        return remote(dkv.at[part(g, slot_of(zz, xx, 1 - c))], core_in.at[g, k, zz],
                      cs.at[g, k, zz], cr.at[g, k, zz], beside)

    def x_copy(g, zz):
        return remote(x_out.at[g, zz], x_in.at[g, zz], xs.at[g, zz], xr.at[g, zz], across)

    def up_copy(g, zz):
        return remote(high_out.at[g, zz], high_in.at[g, zz], us.at[g, zz], ur.at[g, zz], right)

    def down_copy(g, zz):
        return remote(low_out.at[g, zz], low_in.at[g, zz], ls.at[g, zz], lr.at[g, zz], left)

    def target_of(i):
        if i == nz - 1:
            return z
        high = nz - 1 - i - jnp.where(i >= nz - 1 - z, 1, 0)
        low = i + jnp.where(i >= z, 1, 0)
        return jnp.where(z < nz // 2, high, low)

    def cross(g):
        for i in range(nz):
            zz = target_of(i)
            core_copy(g, 0, zz).wait_recv()
            x_out[g, zz] = (dkv[part(g, slot_of(zz, 1 - x, c))].astype(F32)
                            + core_in[g, 0, zz].astype(F32)).astype(BF16)
            x_copy(g, zz).start()

    def local_sum(g, zz):
        core_copy(g, 1, zz).wait_recv()
        x_copy(g, zz).wait_recv()
        return (dkv[part(g, slot_of(zz, x, c))].astype(F32) + core_in[g, 1, zz].astype(F32)
                + x_in[g, zz].astype(F32))

    def tick(g, tau):
        @pl.when(z <= tau)
        def _():
            zz = nz - 1 - tau + z
            high_out[g, zz] = local_sum(g, zz).astype(BF16)

            @pl.when(z > 0)
            def _():
                up_copy(g, zz).wait_recv()
                high_out[g, zz] = (high_out[g, zz].astype(F32)
                                   + high_in[g, zz].astype(F32)).astype(BF16)

            up_copy(g, zz).start()

        @pl.when(nz - 1 - z <= tau)
        def _():
            zz = tau - (nz - 1 - z)
            low_out[g, zz] = local_sum(g, zz).astype(BF16)

            @pl.when(z < nz - 1)
            def _():
                down_copy(g, zz).wait_recv()
                low_out[g, zz] = (low_out[g, zz].astype(F32)
                                  + low_in[g, zz].astype(F32)).astype(BF16)

            down_copy(g, zz).start()

    def settle(g):
        at = lanes(g * HEAD_DIM, HEAD_DIM)
        grads[:, :, at] = local_sum(g, z)

        @pl.when(z > 0)
        def _():
            up_copy(g, z).wait_recv()
            grads[:, :, at] = grads[:, :, at] + high_in[g, z].astype(F32)

        @pl.when(z < nz - 1)
        def _():
            down_copy(g, z).wait_recv()
            grads[:, :, at] = grads[:, :, at] + low_in[g, z].astype(F32)

    def attend(g, h):
        k = kv_ref[:, lanes(g * HEAD_DIM, HEAD_DIM)]
        v = kv_ref[:, lanes(width + g * HEAD_DIM, HEAD_DIM)]
        cols = lanes((g * per_group + h) * HEAD_DIM, HEAD_DIM)
        band = slice(h * rows, (h + 1) * rows)
        q, do = q_ref[:, cols], do_ref[:, cols]
        s = lax.dot_general(q, k, NT, preferred_element_type=F32) * scale + bias[...]
        e = jnp.exp(s - jnp.max(s, axis=1, keepdims=True))
        p = e * (1.0 / jnp.sum(e, axis=1, keepdims=True))
        half = p.astype(BF16)
        p_all[band, :] = half
        attended = jnp.dot(half, v, preferred_element_type=F32).astype(BF16)
        delta = jnp.sum(do.astype(F32) * attended.astype(F32), axis=1, keepdims=True)
        dp = lax.dot_general(do, v, NT, preferred_element_type=F32)
        ds = (p * (dp - delta) * scale).astype(BF16)
        ds_all[band, :] = ds
        dq[:, cols] = jnp.dot(ds, k, preferred_element_type=F32).astype(BF16)

    def group_grads(g):
        heads = [lanes((g * per_group + h) * HEAD_DIM, HEAD_DIM) for h in range(per_group)]
        qs = jnp.concatenate([q_ref[:, at] for at in heads], axis=0)
        dos = jnp.concatenate([do_ref[:, at] for at in heads], axis=0)
        dk = lax.dot_general(qs, ds_all[...], TN, preferred_element_type=F32)
        dkv[g, 0] = dk.astype(BF16).T
        dv = lax.dot_general(dos, p_all[...], TN, preferred_element_type=F32)
        dkv[g, 1] = dv.astype(BF16).T
        for kind in range(2):
            for i in range(nz):
                core_copy(g, kind, target_of(i)).start()

    tile = 512
    tiles = dim // tile

    def h_tile(t, carry):
        at = pl.ds(pl.multiple_of(t * tile, tile), tile)
        hidden[:, at] = lax.dot_general(dq[...], wq[at, :], NT, preferred_element_type=F32)
        return carry

    def step(t, carry):
        @pl.when(t < kvh)
        def _():
            kv_load(t, 0).wait()
            kv_load(t, 1).wait()
            for h in range(per_group // 2):
                attend(t, h)

        @pl.when(t == kvh)
        def _():
            loads[0].wait()

        @pl.when(t >= kvh)
        def _():
            e = t - kvh
            lax.fori_loop(tiles * e // (nz + 1), tiles * (e + 1) // (nz + 1), h_tile, 0)

        for stage in range(1, nz + 2):
            g = t - stage

            @pl.when((g >= 0) & (g < kvh))
            def _():
                if stage == 1:
                    cross(g)
                elif stage <= nz:
                    tick(g, stage - 2)
                else:
                    settle(g)

        @pl.when(t < kvh)
        def _():
            for h in range(per_group // 2, per_group):
                attend(t, h)
            group_grads(t)

        return carry

    lax.fori_loop(0, kvh + nz + 1, step, 0)
    loads[1].wait()
    loads[2].wait()

    def finish(start):
        at = pl.ds(pl.multiple_of(start, chunk), chunk)
        return (hidden[:, at]
                + lax.dot_general(grads[0].astype(BF16), wk[at, :], NT, preferred_element_type=F32)
                + lax.dot_general(grads[1].astype(BF16), wv[at, :], NT, preferred_element_type=F32))

    per = share // chunk

    def h_copy(p, k):
        return remote(h_out.at[p - 1, k], h_in.at[p - 1, k], hs.at[p - 1, k], hr.at[p - 1, k],
                      {"head": lax.rem(head + p, nh)})

    for p in range(1, nh):
        for k in range(per):
            h_out[p - 1, k] = finish(lax.rem(head + p, nh) * share + k * chunk).astype(BF16)
            h_copy(p, k).start()
    inv = stat_ref[:, 0:1]
    product = stat_ref[:, 128:129]
    squares = stat_ref[:, 256:257]
    for k in range(per):
        hidden[:, k * chunk:(k + 1) * chunk] = finish(head * share + k * chunk)
    inner = jnp.zeros((rows, 1), F32)
    for k in range(per):
        cols = slice(k * chunk, (k + 1) * chunk)
        grad = hidden[:, cols]
        for p in range(1, nh):
            h_copy(p, k).wait_recv()
            grad = grad + h_in[p - 1, k].astype(F32)
        scaled = grad * gain_ref[:, pl.ds(pl.multiple_of(head * share + k * chunk, chunk), chunk)]
        hidden[:, cols] = scaled
        inner = inner + jnp.sum(scaled * (x_ref[:, cols].astype(F32) * inv), axis=1, keepdims=True)
    part_out[...] = jnp.broadcast_to(inner, part_out.shape)

    def p_copy(p):
        return remote(part_out, part_in.at[p - 1], ps.at[p - 1], pr.at[p - 1],
                      {"head": lax.rem(head + p, nh)})

    for p in range(1, nh):
        p_copy(p).start()
    for p in range(1, nh):
        p_copy(p).wait_recv()
        inner = inner + part_in[p - 1][:, 0:1]
    saliency = product + inner - (inner / dim) * squares
    sal_ref[...] = jnp.broadcast_to(saliency, (rows, 128)).T[0:1, :]
    inner = inner / dim
    for k in range(per):
        cols = slice(k * chunk, (k + 1) * chunk)
        unit = x_ref[:, cols].astype(F32) * inv
        out_ref[:, cols] = (dy_ref[:, cols].astype(F32)
                            + (hidden[:, cols] - unit * inner) * inv).astype(BF16)

    def drain(g, carry):
        for zz in range(nz):
            core_copy(g, 0, zz).wait_send()
            core_copy(g, 1, zz).wait_send()
            x_copy(g, zz).wait_send()
            pl.when(z < zz)(lambda zz=zz: up_copy(g, zz).wait_send())
            pl.when(z > zz)(lambda zz=zz: down_copy(g, zz).wait_send())
        return carry

    lax.fori_loop(0, kvh, drain, 0)
    for p in range(1, nh):
        for k in range(per):
            h_copy(p, k).wait_send()
        p_copy(p).wait_send()


def back(nz, nh, pq, pk, q, do, kv, x, dy, gain, stat, wq, wk, wv):
    rows, share = x.shape
    width = wk.shape[1]
    kvh = width // HEAD_DIM
    length = kv.shape[0]
    wide = q.shape[1] // kvh
    dim = nh * share
    chunk = min(512, share)
    per = share // chunk
    piece = (kvh, nz, 2, rows, HEAD_DIM)
    dma = pltpu.SemaphoreType.DMA
    peers = max(1, nh - 1)
    hops = dma((kvh, nz))
    return pl.pallas_call(
        functools.partial(back_kernel, nz, nh, chunk),
        out_shape=(
            jax.ShapeDtypeStruct((rows, share), BF16),
            jax.ShapeDtypeStruct((1, rows), F32),
        ),
        in_specs=[VM] * 4 + [ANY] + [VM] * 4 + [ANY] * 3,
        out_specs=(VM, VM),
        scratch_shapes=[
            pltpu.VMEM(kv.shape, BF16),
            pltpu.VMEM(wq.shape, BF16), pltpu.VMEM(wk.shape, BF16), pltpu.VMEM(wv.shape, BF16),
            pltpu.VMEM((rows, length), F32),
            pltpu.VMEM((wide // HEAD_DIM * rows, length), BF16),
            pltpu.VMEM((wide // HEAD_DIM * rows, length), BF16),
            pltpu.VMEM(q.shape, BF16),
            pltpu.VMEM((kvh, 2, length, HEAD_DIM), BF16),
            pltpu.VMEM((rows, dim), F32),
            pltpu.VMEM((kvh, 2, nz, 2, rows, HEAD_DIM), BF16),
            pltpu.VMEM(piece, BF16), pltpu.VMEM(piece, BF16),
            pltpu.VMEM(piece, BF16), pltpu.VMEM(piece, BF16),
            pltpu.VMEM(piece, BF16), pltpu.VMEM(piece, BF16),
            pltpu.VMEM((2, rows, width), F32),
            pltpu.VMEM((peers, per, rows, chunk), BF16),
            pltpu.VMEM((peers, per, rows, chunk), BF16),
            pltpu.VMEM((rows, 128), F32), pltpu.VMEM((peers, rows, 128), F32),
            dma((2, kvh)), dma((3,)), dma((kvh, 2, nz)), dma((kvh, 2, nz)),
            hops, hops, hops, hops, hops, hops,
            dma((peers, per)), dma((peers, per)), dma((peers,)), dma((peers,)),
        ],
        compiler_params=pltpu.CompilerParams(
            collective_id=1, has_side_effects=True, vmem_limit_bytes=VMEM_LIMIT),
        name="back",
    )(pq, pk, q, do, kv, x, dy, gain, stat, wq, wk, wv)


def fused_kernel(nz, order_hbm, lengths_hbm, x_ref, dy_ref, gain_hbm,
                 wq_ref, wk_ref, wv_ref, wo_ref, out_ref, sal_ref,
                 wq, wk, wv, wo, xall, dyall, xg, acc_kv, acc2, inv_ref, vx,
                 kv_own, kvs, q_out, do_out, qs, dos, qt, dot_, bias, ee, acc_o, m_run, stat,
                 dq_own, part, up_in, down_in, dkvr,
                 h_in, part_out, part_in, gain_ref, order_ref, lengths_ref,
                 isem, wsem, lsem, xs, xr, dys, dyr, ks, kr, zus, zds, zr, qsem, qr, dsem, dr,
                 us, ur, ls, lr, gs, gr, fs, fr, hs, hr, ps, pr):
    me, z, x, c = coords()
    head = lax.axis_index("head")
    rows, share = x_ref.shape
    dim = 2 * share
    width = wk_ref.shape[1]
    slab = SLAB * rows
    wide = wq_ref.shape[1] // SLAB
    per_group = wide // HEAD_DIM
    rc = rows // HALVES
    block = SLAB * rc
    kv = 2 * HEAD_DIM
    scale = HEAD_DIM ** (-0.5)
    j = x * 2 + c
    gg = wo.at[:, 0:block]
    dq_slab = wo.at[0:slab, block:block + wide]
    peer = 1 - head
    mine = pl.ds(pl.multiple_of(head * share, share), share)
    theirs = pl.ds(pl.multiple_of(peer * share, share), share)

    own = [
        pltpu.make_async_copy(x_ref, xall.at[head], lsem.at[0]),
        pltpu.make_async_copy(dy_ref, dyall.at[head], lsem.at[1]),
    ]
    small = [pltpu.make_async_copy(a, b, isem.at[i]) for i, (a, b) in enumerate(
        ((order_hbm, order_ref), (lengths_hbm, lengths_ref), (gain_hbm, gain_ref)))]
    for copy in small:
        copy.start()
    own[0].start()
    load_k = pltpu.make_async_copy(wk_ref, wk, wsem.at[0])
    load_v = pltpu.make_async_copy(wv_ref, wv, wsem.at[1])
    load_q = [pltpu.make_async_copy(wq_ref.at[at, :], wq.at[at, :], wsem.at[2 + i])
              for i, at in enumerate((mine, theirs))]
    load_o = [pltpu.make_async_copy(wo_ref.at[:, at], wo, wsem.at[4 + i])
              for i, at in enumerate((mine, theirs))]
    load_k.start()
    load_v.start()
    own[1].start()

    def member(p):
        xx = x if p < 2 else 1 - x
        cc = c if p % 2 == 0 else 1 - c
        return xx, cc, xx * 2 + cc

    barrier = pltpu.get_barrier_semaphore()

    def greet(target):
        pl.semaphore_signal(barrier, inc=1, device_id=target, device_id_type=MESH)

    greet({"head": peer})
    for p in range(1, SLAB):
        greet({"ctx": slot_of(z, *member(p)[:2])})
    pl.when(z > 0)(lambda: greet({"ctx": slot_of(z - 1, x, c)}))
    pl.when(z < nz - 1)(lambda: greet({"ctx": slot_of(z + 1, x, c)}))

    @pl.when((z > 0) & (z < nz - 1))
    def _():
        pl.semaphore_wait(barrier, SLAB + 2)

    @pl.when((z == 0) | (z == nz - 1))
    def _():
        pl.semaphore_wait(barrier, SLAB + 1)

    def remote(src, dst, ss, rs, target):
        return pltpu.make_async_remote_copy(
            src_ref=src, dst_ref=dst, send_sem=ss, recv_sem=rs, device_id=target,
            device_id_type=MESH)

    def to_member(p, src, dst, ss, rs):
        xx, cc, _ = member(p)
        return remote(src, dst, ss, rs, {"ctx": slot_of(z, xx, cc)})

    right = {"ctx": slot_of(z + 1, x, c)}
    left = {"ctx": slot_of(z - 1, x, c)}

    def span(start, size):
        return pl.ds(pl.multiple_of(start, size), size)

    def x_copy(a):
        at = slice(a * rc, (a + 1) * rc)
        return remote(xall.at[head, at, :], xall.at[head, at, :], xs.at[a], xr.at[a], {"head": peer})

    tile = wide
    fd = min(1024, share)
    feats = share // fd

    def dy_copy(f):
        at = slice(f * fd, (f + 1) * fd)
        return remote(dyall.at[head, :, at], dyall.at[head, :, at], dys.at[f], dyr.at[f], {"head": peer})

    own[0].wait()
    for a in range(HALVES):
        x_copy(a).start()
    own[1].wait()
    for f in range(feats):
        dy_copy(f).start()
    for copy in small:
        copy.wait()
    load_q[0].start()
    load_o[0].start()
    load_q[1].start()

    def make_bias():
        vx[:, HEAD_DIM:kv] = jnp.ones((slab, HEAD_DIM), BF16)
        place_q, owner_q = timeline_place(
            lax.broadcasted_iota(jnp.int32, (slab, 1), 0) + z * slab, order_ref, lengths_ref)
        lane = lax.broadcasted_iota(jnp.int32, (1, nz * slab), 1)
        chunk_bits = rc.bit_length() - 1
        row_in = lane & (rc - 1)
        member_in = jnp.right_shift(lane, chunk_bits) & (SLAB - 1)
        half_in = jnp.right_shift(lane, chunk_bits + 2) & (HALVES - 1)
        slab_in = jnp.right_shift(lane, slab.bit_length() - 1)
        place_k, owner_k = timeline_place(
            slab_in * slab + member_in * rows + half_in * rc + row_in, order_ref, lengths_ref)
        for zz in range(nz):
            for a in range(HALVES):
                at = slice(zz * slab + a * block, zz * slab + (a + 1) * block)
                allowed = (owner_q == owner_k[:, at]) & (place_k[:, at] <= place_q)
                bias[zz, :, a * block:(a + 1) * block] = jnp.where(allowed, 0.0, -1e30).astype(BF16)

    def squares(v):
        return jnp.sum(v * v, axis=1, keepdims=True)

    def kv_own_half():
        v = xall[head].astype(F32)
        inv_ref[:, 2:3] = squares(v)
        xg[head] = (v * gain_ref[:, mine]).astype(BF16)
        load_k.wait()
        acc_kv[0] = jnp.dot(xg[head], wk[mine, :], preferred_element_type=F32)
        load_v.wait()
        acc_kv[1] = jnp.dot(xg[head], wv[mine, :], preferred_element_type=F32)

    def q_half(t, carry):
        at = span(t * tile, tile)
        acc2[0, :, at] = jnp.dot(xg[head], wq[mine, at], preferred_element_type=F32)
        return carry

    def do_half(t, carry):
        at = span(t * tile, tile)
        acc2[1, :, at] = lax.dot_general(dyall[head], wo[at, :], NT, preferred_element_type=F32)
        return carry

    def q_own():
        load_q[0].wait()
        lax.fori_loop(0, SLAB, q_half, 0)

    def do_own(first, last):
        if first == 0:
            load_o[0].wait()
        lax.fori_loop(first, last, do_half, 0)
        if last == SLAB:
            load_o[1].start()

    def kv_copy(p, a):
        jt = member(p)[2]
        dst = kvs.at[z, a, span(j * rc, rc), :]
        return to_member(p, kv_own.at[a, jt], dst, ks.at[a, p], kr.at[a, j])

    def kv_arrived(p, a):
        jt = member(p)[2]
        to_member(p, kv_own.at[a, jt], kvs.at[z, a, span(jt * rc, rc), :],
                  ks.at[a, p], kr.at[a, jt]).wait_recv()

    def make_kv(a):
        x_copy(a).wait_recv()
        at = slice(a * rc, (a + 1) * rc)
        v = xall[peer, at, :].astype(F32)
        total = inv_ref[at, 2:3] + squares(v)
        inv = 1.0 / jnp.sqrt(total / dim + 1e-05)
        inv_ref[at, 0:1] = inv
        inv_ref[at, 1:2] = total * inv * inv
        xg[peer, at, :] = (v * gain_ref[:, theirs]).astype(BF16)
        lhs = xg[peer, at, :]
        for i, w in enumerate((wk, wv)):
            got = (acc_kv[i, at, :] + jnp.dot(lhs, w[theirs, :], preferred_element_type=F32)) * inv
            got = got.astype(BF16)
            for jj in range(SLAB):
                kv_own[a, jj, :, i * HEAD_DIM:(i + 1) * HEAD_DIM] = (
                    got[:, jj * HEAD_DIM:(jj + 1) * HEAD_DIM])
        for p in (2, 3, 1):
            kv_copy(p, a).start()
        kvs[z, a, span(j * rc, rc), :] = kv_own[a, j]

    def piece(zz, a, s):
        return kvs.at[zz, a, span(s * 2 * rc, 2 * rc), :]

    def z_up(zz, a, s):
        return remote(piece(zz, a, s), piece(zz, a, s), zus.at[zz, a, s], zr.at[zz, a, s], right)

    def z_down(zz, a, s):
        return remote(piece(zz, a, s), piece(zz, a, s), zds.at[zz, a, s], zr.at[zz, a, s], left)

    def gather_own(a):
        kv_arrived(1, a)
        for s, peers in ((x, ()), (1 - x, (2, 3))):
            for p in peers:
                kv_arrived(p, a)
            pl.when(z < nz - 1)(lambda s=s: z_up(z, a, s).start())
            pl.when(z > 0)(lambda s=s: z_down(z, a, s).start())

    def order(t):
        near = jnp.where(z < nz // 2, z, nz - 1 - z)
        d = (t + 1) // 2
        o = jnp.where(t <= 2 * near, near + d if t % 2 else near - d, t)
        return jnp.where(z < nz // 2, o, nz - 1 - o)

    def travels(zz):
        return ((zz < z) & (z < nz - 1)) | ((zz > z) & (z > 0))

    def take(t, a):
        zz = order(t)

        @pl.when(travels(zz))
        def _():
            for s in range(2):
                z_up(zz, a, s).wait_recv()
                pl.when(zz < z)(lambda s=s: z_up(zz, a, s).start())
                pl.when(zz > z)(lambda s=s: z_down(zz, a, s).start())

    def keep(t):
        zz = order(t)

        @pl.when(jnp.logical_not(travels(zz)))
        def _():
            for a in range(HALVES):
                for s in range(2):
                    z_up(zz, a, s).wait_recv()

    def shared(p, src, dst, ss, rs):
        jt = member(p)[2]
        return to_member(p, src.at[jt], dst.at[span(j * rows, rows), :], ss.at[p], rs.at[j])

    def shared_arrived(p, src, dst, ss, rs):
        jt = member(p)[2]
        to_member(p, src.at[jt], dst.at[span(jt * rows, rows), :], ss.at[p], rs.at[jt]).wait_recv()

    def q_tile(p):
        jt = member(p)[2]
        at = span(jt * tile, tile)
        got = acc2[0, :, at] + jnp.dot(
            xg[peer], wq[theirs, at], preferred_element_type=F32)
        q_out[jt] = (got * (inv_ref[:, 0:1] * (scale * LOG2E))).astype(BF16)
        if p:
            shared(p, q_out, qs, qsem, qr).start()
        else:
            qs[span(j * rows, rows), :] = q_out[jt]

    def do_part(f, first=0, last=SLAB):
        if f == 0 and first == 0:
            load_o[1].wait()
        if first == 0:
            dy_copy(f).wait_recv()
        at = slice(f * fd, (f + 1) * fd)
        if f < feats - 1:
            def body(t, carry):
                cols = span(t * tile, tile)
                acc2[1, :, cols] = acc2[1, :, cols] + lax.dot_general(
                    dyall[peer, :, at], wo[cols, at], NT, preferred_element_type=F32)
                return carry

            lax.fori_loop(first, last, body, 0)
            return
        for p in (3, 2, 1, 0):
            jt = member(p)[2]
            cols = span(jt * tile, tile)
            do_out[jt] = (acc2[1, :, cols] + lax.dot_general(
                dyall[peer, :, at], wo[cols, at], NT, preferred_element_type=F32)).astype(BF16)
            if p:
                shared(p, do_out, dos, dsem, dr).start()
            else:
                dos[span(j * rows, rows), :] = do_out[jt]

    lane_at = lax.broadcasted_iota(jnp.int32, (slab, HEAD_DIM), 1)

    def forward(t, hook=None):
        zz = order(t)
        vx[:, 0:HEAD_DIM] = kvs[zz, :, :, HEAD_DIM:kv].reshape(slab, HEAD_DIM)
        def one(hh):
            cols = span(hh * HEAD_DIM, HEAD_DIM)
            k = kvs[zz, :, :, 0:HEAD_DIM].reshape(slab, HEAD_DIM)
            s = lax.dot_general(qs[:, cols], k, NT, preferred_element_type=F32)
            s = s + bias[zz].astype(F32)
            m = jnp.broadcast_to(jnp.max(s, axis=1, keepdims=True), (slab, HEAD_DIM))
            if t:
                old = m_run[hh]
                m = jnp.maximum(m, old)
            half = jnp.exp2(s - jnp.concatenate([m] * SLAB, axis=1)).astype(BF16)
            ee[t, span(hh * slab, slab), :] = half
            o = jnp.dot(half, vx[...], preferred_element_type=F32)
            if t:
                alpha = jnp.exp2(old - m)
                o = o + acc_o[hh] * jnp.concatenate([alpha, alpha], axis=1)
            stat[hh] = jnp.where(lane_at == t, m, stat[hh]) if t else m
            m_run[hh] = m
            acc_o[hh] = o

        def pair(i, carry):
            one(2 * i)
            one(2 * i + 1)
            if hook is not None:
                pl.when(i == 0)(hook)
            return carry

        lax.fori_loop(0, per_group // 2, pair, 0)

    def settle():
        def one(hh, carry):
            cols = span(hh * HEAD_DIM, HEAD_DIM)
            do = dos[:, cols]
            inv_l = 1.0 / acc_o[hh, :, HEAD_DIM:kv]
            attended = (acc_o[hh, :, 0:HEAD_DIM] * inv_l).astype(BF16)
            delta = jnp.sum(do.astype(F32) * attended.astype(F32), axis=1, keepdims=True)
            stat[hh] = jnp.where(lane_at == HEAD_DIM - 1, delta, jnp.exp2(stat[hh] - m_run[hh]) * inv_l)
            acc_o[hh, :, 0:HEAD_DIM] = jnp.zeros((slab, HEAD_DIM), F32)
            dot_[:, span(hh * slab, slab)] = do.T
            return carry

        lax.fori_loop(0, per_group, one, 0)

    def turn_q():
        def one(hh, carry):
            qt[:, span(hh * slab, slab)] = qs[:, span(hh * HEAD_DIM, HEAD_DIM)].T
            return carry

        lax.fori_loop(0, per_group, one, 0)

    def backward(t, a):
        zz = order(t)
        half = slice(a * block, (a + 1) * block)

        def one(hh):
            k = kvs[zz, a, :, 0:HEAD_DIM]
            v = kvs[zz, a, :, HEAD_DIM:kv]
            cols = span(hh * HEAD_DIM, HEAD_DIM)
            at = span(hh * slab, slab)
            dp = lax.dot_general(dos[:, cols], v, NT, preferred_element_type=F32)
            p = ee[t, at, half].astype(F32) * stat[hh, :, t:t + 1]
            ee[t, at, half] = p.astype(BF16)
            g = (p * (dp - stat[hh, :, 127:128])).astype(BF16)
            gg[at, :] = g
            acc_o[hh, :, 0:HEAD_DIM] = (acc_o[hh, :, 0:HEAD_DIM]
                                        + jnp.dot(g, k, preferred_element_type=F32))

        def pair(i, carry):
            one(2 * i)
            one(2 * i + 1)
            return carry

        lax.fori_loop(0, per_group // 2, pair, 0)
        dk = jnp.dot(qt[...], gg[...], preferred_element_type=F32) * LN2
        dv = jnp.dot(dot_[...], ee[t, :, half], preferred_element_type=F32)
        part[zz, a, :, 0:HEAD_DIM] = dk.astype(BF16).T
        part[zz, a, :, HEAD_DIM:kv] = dv.astype(BF16).T

    def up_copy(zz, a):
        return remote(part.at[zz, a], up_in.at[zz, a], us.at[zz, a], ur.at[zz, a], right)

    def down_copy(zz, a):
        return remote(part.at[zz, a], down_in.at[zz, a], ls.at[zz, a], lr.at[zz, a], left)

    def send_part(t, a):
        zz = order(t)
        pl.when((zz > z) & (z == 0))(lambda: up_copy(zz, a).start())
        pl.when((zz < z) & (z == nz - 1))(lambda: down_copy(zz, a).start())

    def pass_part(t, a):
        zz = order(t)

        @pl.when((zz > z) & (z > 0))
        def _():
            up_copy(zz, a).wait_recv()
            part[zz, a] = (part[zz, a].astype(F32) + up_in[zz, a].astype(F32)).astype(BF16)
            up_copy(zz, a).start()

        @pl.when((zz < z) & (z < nz - 1))
        def _():
            down_copy(zz, a).wait_recv()
            part[zz, a] = (part[zz, a].astype(F32) + down_in[zz, a].astype(F32)).astype(BF16)
            down_copy(zz, a).start()

    def fin_copy(p, a):
        jt = member(p)[2]
        return to_member(p, kv_own.at[a, jt], dkvr.at[a, j], fs.at[a, p], fr.at[a, j])

    def fin_arrived(p, a):
        jt = member(p)[2]
        to_member(p, kv_own.at[a, jt], dkvr.at[a, jt], fs.at[a, p],
                  fr.at[a, jt]).wait_recv()

    def finish_part(a):
        kv_own[a] = part[z, a].reshape(SLAB, rc, kv)

        @pl.when(z > 0)
        def _():
            up_copy(z, a).wait_recv()
            got = up_in[z, a].reshape(SLAB, rc, kv)
            kv_own[a] = (kv_own[a].astype(F32) + got.astype(F32)).astype(BF16)

        @pl.when(z < nz - 1)
        def _():
            down_copy(z, a).wait_recv()
            got = down_in[z, a].reshape(SLAB, rc, kv)
            kv_own[a] = (kv_own[a].astype(F32) + got.astype(F32)).astype(BF16)

        for p in (3, 2, 1):
            fin_copy(p, a).start()
        dkvr[a, j] = kv_own[a, j]

    def dq_copy(p):
        jt = member(p)[2]
        return to_member(p, wo.at[span(jt * rows, rows), block:block + wide], dq_own.at[:, span(j * tile, tile)],
                         gs.at[p], gr.at[j])

    def dq_arrived(p):
        jt = member(p)[2]
        to_member(p, wo.at[span(jt * rows, rows), block:block + wide], dq_own.at[:, span(jt * tile, tile)],
                  gs.at[p], gr.at[jt]).wait_recv()

    make_bias()
    kv_own_half()
    q_own()
    make_kv(0)
    do_own(0, 2)
    gather_own(0)
    do_own(2, SLAB)
    make_kv(1)
    load_q[1].wait()
    q_tile(3)
    q_tile(2)
    q_tile(1)
    q_tile(0)
    take(1, 0)
    gather_own(1)
    do_part(0, 0, 2)
    for t in range(2, min(3, nz)):
        take(t, 0)
    do_part(0, 2, SLAB)
    take(1, 1)
    for p in (1, 2, 3):
        shared_arrived(p, q_out, qs, qsem, qr)

    def far():
        for t in range(2, min(3, nz)):
            take(t, 1)
        for t in range(3, nz):
            take(t, 0)

    def last():
        for t in range(3, nz):
            take(t, 1)

    forward(0, far)
    for f in range(1, feats):
        do_part(f)
    keep(1)
    forward(1, last)
    turn_q()
    for t in range(2, nz):
        keep(t)
        forward(t)
    for p in (1, 2, 3):
        shared_arrived(p, do_out, dos, dsem, dr)
    settle()
    steps = [(nz - 1, a) for a in range(HALVES)]
    steps += [(t, a) for a in range(HALVES) for t in range(nz - 2, 0, -1)]
    steps += [(0, a) for a in range(HALVES)]
    lag = 3
    for i, (t, a) in enumerate(steps):
        backward(t, a)
        if t:
            send_part(t, a)
        if i >= lag and steps[i - lag][0]:
            pass_part(*steps[i - lag])
    for hh in range(per_group):
        dq_slab[:, hh * HEAD_DIM:(hh + 1) * HEAD_DIM] = (acc_o[hh, :, 0:HEAD_DIM] * scale).astype(BF16)
    for p in (3, 2, 1):
        dq_copy(p).start()
    dq_own[:, span(j * tile, tile)] = dq_slab[span(j * rows, rows), :]
    for step in steps[len(steps) - lag:]:
        if step[0]:
            pass_part(*step)
    for p in (1, 2, 3):
        shared(p, q_out, qs, qsem, qr).wait_send()
        for a in range(HALVES):
            kv_copy(p, a).wait_send()
    product = jnp.zeros((rows, 1), F32)
    for h in range(2):
        product = product + jnp.sum(
            xall[h].astype(F32) * dyall[h].astype(F32), axis=1, keepdims=True)
    dq_arrived(1)
    hidden = acc2
    h_out = q_out
    chunk = min(512, share)
    per = share // chunk

    def h_tile(half, start, size, add):
        heads_at = pl.ds(pl.multiple_of(start * tile, tile), size * tile)

        def body(k, carry):
            at = span(half * share + k * chunk, chunk)
            cols = span(k * chunk, chunk)
            got = lax.dot_general(dq_own[:, heads_at], wq[at, heads_at], NT,
                                  preferred_element_type=F32)
            hidden[half, :, cols] = hidden[half, :, cols] + got if add else got
            return carry

        lax.fori_loop(0, per, body, 0)

    h_tile(peer, 2 * x, 2, False)
    finish_part(0)
    finish_part(1)
    dq_arrived(3)
    h_tile(peer, member(3)[2], 1, True)
    dq_arrived(2)
    h_tile(peer, member(2)[2], 1, True)
    for a in range(HALVES):
        for p in (1, 2, 3):
            fin_arrived(p, a)
    grads = [
        jnp.concatenate(
            [jnp.concatenate([dkvr[a, jj, :, i * HEAD_DIM:(i + 1) * HEAD_DIM] for jj in range(SLAB)],
                             axis=1) for a in range(HALVES)], axis=0)
        for i in range(2)
    ]

    def finish(half, k):
        at = span(half * share + k * chunk, chunk)
        return (hidden[half, :, k * chunk:(k + 1) * chunk]
                + lax.dot_general(grads[0], wk[at, :], NT, preferred_element_type=F32)
                + lax.dot_general(grads[1], wv[at, :], NT, preferred_element_type=F32))

    def h_copy(k):
        return remote(h_out.at[k], h_in.at[k], hs.at[k], hr.at[k], {"head": peer})

    inv = inv_ref[:, 0:1]
    inner = jnp.zeros((rows, 1), F32)

    def weighed(half, k, grad):
        scaled = grad * gain_ref[:, span(half * share + k * chunk, chunk)]
        unit = xall[half, :, k * chunk:(k + 1) * chunk].astype(F32) * inv
        return jnp.sum(scaled * unit, axis=1, keepdims=True)

    for k in range(per):
        grad = finish(peer, k)
        h_out[k] = grad.astype(BF16)
        h_copy(k).start()
        inner = inner + weighed(peer, k, grad)
    h_tile(head, 2 * x, 2, False)
    h_tile(head, 2 * (1 - x), 2, True)
    for k in range(per):
        grad = finish(head, k)
        hidden[head, :, k * chunk:(k + 1) * chunk] = grad
        inner = inner + weighed(head, k, grad)
    part_out[...] = jnp.broadcast_to(inner, (rows, 128)).T[0:8, :]
    p_copy = remote(part_out, part_in, ps, pr, {"head": peer})
    p_copy.start()
    p_copy.wait_recv()
    inner = inner + jnp.broadcast_to(part_in[0:1, :], (128, rows)).T[:, 0:1]
    saliency = product + inner - (inner / dim) * inv_ref[:, 1:2]
    sal_ref[...] = jnp.broadcast_to(saliency, (rows, 128)).T[0:1, :]
    inner = inner / dim
    for k in range(per):
        cols = slice(k * chunk, (k + 1) * chunk)
        unit = xall[head, :, cols].astype(F32) * inv
        h_copy(k).wait_recv()
        grad = hidden[head, :, cols] + h_in[k].astype(F32)
        scaled = grad * gain_ref[:, span(head * share + k * chunk, chunk)]
        out_ref[:, cols] = (dyall[head, :, cols].astype(F32)
                            + (scaled - unit * inner) * inv).astype(BF16)

    for a in range(HALVES):
        x_copy(a).wait_send()
        for p in (1, 2, 3):
            fin_copy(p, a).wait_send()
        for zz in range(nz):
            pl.when(z < zz)(lambda zz=zz, a=a: up_copy(zz, a).wait_send())
            pl.when(z > zz)(lambda zz=zz, a=a: down_copy(zz, a).wait_send())
            for s in range(2):
                pl.when((zz <= z) & (z < nz - 1))(lambda zz=zz, a=a, s=s: z_up(zz, a, s).wait_send())
                pl.when((zz >= z) & (z > 0))(lambda zz=zz, a=a, s=s: z_down(zz, a, s).wait_send())
    for f in range(feats):
        dy_copy(f).wait_send()
    for p in (1, 2, 3):
        shared(p, do_out, dos, dsem, dr).wait_send()
        dq_copy(p).wait_send()
    for k in range(per):
        h_copy(k).wait_send()
    p_copy.wait_send()


def fused(nz, order, lengths, x, dy, gain, wq, wk, wv, wo):
    rows, share = x.shape
    dim = 2 * share
    hq, width = wq.shape[1], wk.shape[1]
    wide = hq // SLAB
    heads = wide // HEAD_DIM
    rc = rows // HALVES
    slab = SLAB * rows
    block = SLAB * rc
    kv = 2 * HEAD_DIM
    fd = min(1024, share)
    chunk = min(512, share)
    per = share // chunk
    feats = share // fd
    dma = pltpu.SemaphoreType.DMA
    vm = pltpu.VMEM
    return pl.pallas_call(
        functools.partial(fused_kernel, nz),
        out_shape=(
            jax.ShapeDtypeStruct((rows, share), BF16),
            jax.ShapeDtypeStruct((1, rows), F32),
        ),
        in_specs=[ANY] * 9,
        out_specs=(VM, VM),
        scratch_shapes=[
            vm(wq.shape, BF16), vm(wk.shape, BF16), vm(wv.shape, BF16), vm((hq, share), BF16),
            vm((2, rows, share), BF16), vm((2, rows, share), BF16), vm((2, rows, share), BF16),
            vm((2, rows, width), F32), vm((2, rows, share), F32), vm((rows, 128), F32),
            vm((slab, kv), BF16),
            vm((HALVES, SLAB, rc, kv), BF16), vm((nz, HALVES, block, kv), BF16),
            vm((SLAB, rows, wide), BF16), vm((SLAB, rows, wide), BF16),
            vm((slab, wide), BF16), vm((slab, wide), BF16),
            vm((HEAD_DIM, heads * slab), BF16), vm((HEAD_DIM, heads * slab), BF16),
            vm((nz, slab, slab), BF16),
            vm((nz, heads * slab, slab), BF16),
            vm((heads, slab, kv), F32), vm((heads, slab, HEAD_DIM), F32), vm((heads, slab, 128), F32),
            vm((rows, hq), BF16),
            vm((nz, HALVES, block, kv), BF16), vm((nz, HALVES, block, kv), BF16),
            vm((nz, HALVES, block, kv), BF16),
            vm((HALVES, SLAB, rc, kv), BF16),
            vm((per, rows, chunk), BF16),
            vm((8, rows), F32), vm((8, rows), F32),
            vm((1, dim), F32), pltpu.SMEM(order.shape, jnp.int32), pltpu.SMEM(lengths.shape, jnp.int32),
            dma((3,)), dma((6,)), dma((2,)), dma((HALVES,)), dma((HALVES,)), dma((feats,)), dma((feats,)),
            dma((HALVES, SLAB)), dma((HALVES, SLAB)),
            dma((nz, HALVES, 2)), dma((nz, HALVES, 2)), dma((nz, HALVES, 2)),
            dma((SLAB,)), dma((SLAB,)), dma((SLAB,)), dma((SLAB,)),
            dma((nz, HALVES)), dma((nz, HALVES)), dma((nz, HALVES)), dma((nz, HALVES)),
            dma((SLAB,)), dma((SLAB,)), dma((HALVES, SLAB)), dma((HALVES, SLAB)),
            dma((per,)), dma((per,)), dma(()), dma(()),
        ],
        compiler_params=pltpu.CompilerParams(
            collective_id=2, has_side_effects=True, vmem_limit_bytes=VMEM_LIMIT),
        name="fused",
    )(order, lengths, x, dy, gain, wq, wk, wv, wo)


def local(inputs, out_grad, norm_gain, w_query, w_key, w_value, w_out, record_lengths, block_order):
    rows, share = inputs.shape
    n = lax.axis_size("ctx")
    nh = lax.axis_size("head")
    nz = n // 4
    gain = norm_gain[None, :]
    if nh == 2 and w_key.shape[1] == SLAB * HEAD_DIM and inputs.shape[1] == w_query.shape[1]:
        input_grad, saliency = fused(
            nz, block_order, record_lengths, inputs, out_grad, gain, w_query, w_key, w_value, w_out)
        return (input_grad, saliency.reshape(rows))
    q, do, kv, stat, pq, pk = front(
        nz, nh, block_order, record_lengths, inputs, out_grad, gain,
        w_query, w_key, w_value, w_out)
    input_grad, saliency = back(
        nz, nh, pq, pk, q, do, kv, inputs, out_grad, gain, stat, w_query, w_key, w_value)
    return (input_grad, saliency.reshape(rows))


def solution(mesh):
    placed = (
        P("ctx", "head"),
        P("ctx", "head"),
        P(),
        P(None, "head"),
        P(None, "head"),
        P(None, "head"),
        P("head", None),
        P(),
        P(),
    )
    return jax.shard_map(
        local, mesh=mesh, in_specs=placed, out_specs=(P("ctx", "head"), P("ctx")), check_vma=False
    )
```

```python
import functools

import jax
import jax.numpy as jnp
from jax import lax
from jax.experimental import pallas as pl
from jax.experimental.pallas import tpu as pltpu
from jax.sharding import PartitionSpec as P

HEAD_DIM = 128
BLOCK = 64
SLAB = 4
HALVES = 2
LOG2E = 1.4426950408889634
LN2 = 0.6931471805599453
NT = (((1,), (1,)), ((), ()))
TN = (((0,), (0,)), ((), ()))
F32 = jnp.float32
BF16 = jnp.bfloat16
MESH = pl.DeviceIdType.MESH
VM = pl.BlockSpec(memory_space=pltpu.VMEM)
ANY = pl.BlockSpec(memory_space=pl.ANY)
SM = pl.BlockSpec(memory_space=pltpu.SMEM)
VMEM_LIMIT = 67043328


def timeline_place(stored, order_ref, lengths_ref):
    block = jnp.right_shift(stored, 6)
    position = jnp.zeros(stored.shape, jnp.int32)
    for b in range(order_ref.shape[0]):
        position = jnp.where(block == b, order_ref[b], position)
    position = position * BLOCK + (stored & (BLOCK - 1))
    record = jnp.zeros(stored.shape, jnp.int32)
    start = 0
    for r in range(lengths_ref.shape[0]):
        record = record + jnp.where(position >= start, 1, 0)
        start = start + lengths_ref[r]
    return position, record


def coords():
    me = lax.axis_index("ctx")
    return me, me // 4, lax.rem(me // 2, 2), lax.rem(me, 2)


def slot_of(z, x, c):
    return (z * 2 + x) * 2 + c


def enter(nz, nh):
    _, z, x, c = coords()
    head = lax.axis_index("head")
    barrier = pltpu.get_barrier_semaphore()

    def greet(target):
        pl.semaphore_signal(barrier, inc=1, device_id=target, device_id_type=MESH)

    for p in range(1, nh):
        greet({"head": lax.rem(head + p, nh)})
    greet({"ctx": slot_of(z, 1 - x, c)})
    greet({"ctx": slot_of(z, x, 1 - c)})

    @pl.when(z > 0)
    def _():
        greet({"ctx": slot_of(z - 1, x, c)})

    @pl.when(z < nz - 1)
    def _():
        greet({"ctx": slot_of(z + 1, x, c)})

    @pl.when((z > 0) & (z < nz - 1))
    def _():
        pl.semaphore_wait(barrier, nh + 3)

    @pl.when((z == 0) | (z == nz - 1))
    def _():
        pl.semaphore_wait(barrier, nh + 2)


def front_kernel(nz, nh, order_ref, lengths_ref, x_ref, dy_ref, gain_ref,
                 wq_ref, wk_ref, wv_ref, wo_ref,
                 q_out, do_out, kv_out, stat_ref, pq_ref, pk_ref,
                 q_ref, do_ref, kv_ref, wq, wk, wv, wo, xall, dyall, normed,
                 wsem, lsem, osem, ssem, xs, xr, dys, dyr, ks, kr):
    me, z, x, c = coords()
    head = lax.axis_index("head")
    rows, share = x_ref.shape
    dim = nh * share
    hq = q_ref.shape[1]
    width = wk_ref.shape[1]
    loads = [
        pltpu.make_async_copy(a, b, wsem.at[i])
        for i, (a, b) in enumerate(((wk_ref, wk), (wv_ref, wv), (wq_ref, wq), (wo_ref, wo)))
    ]
    for load in loads:
        load.start()
    own = [
        pltpu.make_async_copy(x_ref, xall.at[head], lsem.at[0]),
        pltpu.make_async_copy(dy_ref, dyall.at[head], lsem.at[1]),
    ]
    for copy in own:
        copy.start()
    enter(nz, nh)

    def head_copies(src, dst, send, recv):
        return [
            pltpu.make_async_remote_copy(
                src_ref=src, dst_ref=dst.at[head], send_sem=send.at[p - 1], recv_sem=recv.at[p - 1],
                device_id={"head": lax.rem(head + p, nh)}, device_id_type=MESH)
            for p in range(1, nh)
        ]

    xc = head_copies(x_ref, xall, xs, xr)
    dyc = head_copies(dy_ref, dyall, dys, dyr)
    for copy in xc + dyc:
        copy.start()
    length = kv_ref.shape[0]
    pk_ref[0:1, :], pk_ref[1:2, :] = timeline_place(
        lax.broadcasted_iota(jnp.int32, (1, length), 1), order_ref, lengths_ref)
    pq_ref[:, 0:1], pq_ref[:, 1:2] = timeline_place(
        lax.broadcasted_iota(jnp.int32, (rows, 1), 0) + me * rows, order_ref, lengths_ref)
    own[0].wait()
    for copy in xc:
        copy.wait()
    total = jnp.zeros((rows, 1), F32)
    for j in range(nh):
        v = xall[j].astype(F32)
        total = total + jnp.sum(v * v, axis=1, keepdims=True)
    root = jnp.sqrt(total / dim + 1e-05)
    inv = 1.0 / root
    for j in range(nh):
        cols = slice(j * share, (j + 1) * share)
        normed[:, cols] = (xall[j].astype(F32) * inv * gain_ref[:, cols]).astype(BF16)

    def block(slot):
        return kv_ref.at[pl.ds(pl.multiple_of(slot * rows, rows), rows), :]

    def send(direction, slot, target):
        return pltpu.make_async_remote_copy(
            src_ref=block(slot), dst_ref=block(slot), send_sem=ks.at[direction, slot],
            recv_sem=kr.at[slot], device_id={"ctx": target}, device_id_type=MESH)

    def store(slot):
        return pltpu.make_async_copy(
            block(slot), kv_out.at[pl.ds(pl.multiple_of(slot * rows, rows), rows), :],
            ssem.at[slot])

    def arrived(slot):
        send(0, slot, me).wait_recv()
        store(slot).start()

    mine = pl.ds(pl.multiple_of(me * rows, rows), rows)
    loads[0].wait()
    kv_ref[mine, :width] = jnp.dot(normed[...], wk[...], preferred_element_type=F32).astype(BF16)
    loads[1].wait()
    kv_ref[mine, width:] = jnp.dot(normed[...], wv[...], preferred_element_type=F32).astype(BF16)

    right = slot_of(z + 1, x, c)
    left = slot_of(z - 1, x, c)
    across = slot_of(z, 1 - x, c)
    beside = slot_of(z, x, 1 - c)

    def spread(s, act):
        if s == 0:
            pl.when(z < nz - 1)(lambda: act(send(0, me, right)))
            pl.when(z > 0)(lambda: act(send(1, me, left)))
            act(send(2, me, across))
            act(send(3, me, beside))
            return
        low, high = slot_of(z - s, x, c), slot_of(z + s, x, c)

        @pl.when(z - s >= 0)
        def _():
            if act is start:
                arrived(low)
            pl.when(z < nz - 1)(lambda: act(send(0, low, right)))
            act(send(2, low, across))
            act(send(3, low, beside))

        @pl.when(z + s < nz)
        def _():
            if act is start:
                arrived(high)
            pl.when(z > 0)(lambda: act(send(1, high, left)))
            act(send(2, high, across))
            act(send(3, high, beside))

    def hand_over(s, act):
        def one(slot):
            if act is start:
                arrived(slot)
            act(send(3, slot, beside))

        if s == 0:
            one(slot_of(z, 1 - x, c))
            return
        pl.when(z - s >= 0)(lambda: one(slot_of(z - s, 1 - x, c)))
        pl.when(z + s < nz)(lambda: one(slot_of(z + s, 1 - x, c)))

    def start(copy):
        copy.start()

    def sent(copy):
        copy.wait_send()

    spread(0, start)
    store(me).start()

    loads[2].wait()
    tq = min(512, hq)

    def q_tile(t, carry):
        cols = pl.ds(pl.multiple_of(t * tq, tq), tq)
        q_ref[:, cols] = jnp.dot(normed[...], wq[:, cols], preferred_element_type=F32).astype(BF16)
        return carry

    lax.fori_loop(0, hq // tq, q_tile, 0)
    q_store = pltpu.make_async_copy(q_ref, q_out, osem.at[0])
    q_store.start()
    spread(1, start)

    own[1].wait()
    for copy in dyc:
        copy.wait()
    loads[3].wait()

    def do_tile(t, carry):
        cols = pl.ds(pl.multiple_of(t * tq, tq), tq)
        acc = jnp.zeros((rows, tq), F32)
        for j in range(nh):
            acc = acc + lax.dot_general(
                dyall[j], wo[cols, j * share:(j + 1) * share], NT, preferred_element_type=F32)
        do_ref[:, cols] = acc.astype(BF16)
        return carry

    tiles = hq // tq
    gaps = nz - 2
    for s in range(2, nz):
        lax.fori_loop(tiles * (s - 2) // gaps, tiles * (s - 1) // gaps, do_tile, 0)
        if s == nz - 1:
            do_store = pltpu.make_async_copy(do_ref, do_out, osem.at[1])
            do_store.start()
        spread(s, start)
        hand_over(s - 2, start)

    product = jnp.zeros((rows, 1), F32)
    for j in range(nh):
        product = product + jnp.sum(
            xall[j].astype(F32) * dyall[j].astype(F32), axis=1, keepdims=True)
    stat_ref[:, 0:128] = jnp.broadcast_to(inv, (rows, 128))
    stat_ref[:, 128:256] = jnp.broadcast_to(product, (rows, 128))
    stat_ref[:, 256:384] = jnp.broadcast_to(total * inv * inv, (rows, 128))

    for s in range(nz - 2, nz):
        hand_over(s, start)
    for zz in range(nz):
        for xx in range(2):
            arrived(slot_of(zz, xx, 1 - c))
    for s in range(nz):
        spread(s, sent)
        hand_over(s, sent)
    for slot in range(4 * nz):
        store(slot).wait()
    q_store.wait()
    do_store.wait()


def front(nz, nh, order, lengths, x, dy, gain, wq, wk, wv, wo):
    rows, share = x.shape
    hq, width = wq.shape[1], wk.shape[1]
    n = 4 * nz
    dma = pltpu.SemaphoreType.DMA
    return pl.pallas_call(
        functools.partial(front_kernel, nz, nh),
        out_shape=(
            jax.ShapeDtypeStruct((rows, hq), BF16),
            jax.ShapeDtypeStruct((rows, hq), BF16),
            jax.ShapeDtypeStruct((n * rows, 2 * width), BF16),
            jax.ShapeDtypeStruct((rows, 384), F32),
            jax.ShapeDtypeStruct((rows, 2), jnp.int32),
            jax.ShapeDtypeStruct((2, n * rows), jnp.int32),
        ),
        in_specs=[SM, SM, VM, VM, VM, ANY, ANY, ANY, ANY],
        out_specs=(ANY, ANY, ANY, VM, VM, VM),
        scratch_shapes=[
            pltpu.VMEM((rows, hq), BF16), pltpu.VMEM((rows, hq), BF16),
            pltpu.VMEM((n * rows, 2 * width), BF16),
            pltpu.VMEM(wq.shape, BF16), pltpu.VMEM(wk.shape, BF16),
            pltpu.VMEM(wv.shape, BF16), pltpu.VMEM(wo.shape, BF16),
            pltpu.VMEM((nh, rows, share), BF16), pltpu.VMEM((nh, rows, share), BF16),
            pltpu.VMEM((rows, nh * share), BF16),
            dma((4,)), dma((2,)), dma((2,)), dma((n,)), dma((nh,)), dma((nh,)), dma((nh,)), dma((nh,)),
            dma((4, n)), dma((n,)),
        ],
        compiler_params=pltpu.CompilerParams(
            collective_id=0, has_side_effects=True, vmem_limit_bytes=VMEM_LIMIT),
        name="front",
    )(order, lengths, x, dy, gain, wq, wk, wv, wo)


def back_kernel(nz, nh, chunk, pq_ref, pk_ref, q_ref, do_ref, kv_hbm, x_ref, dy_ref, gain_ref,
                stat_ref, wq_ref, wk_ref, wv_ref, out_ref, sal_ref,
                kv_ref, wq, wk, wv, bias, ds_all, p_all, dq, dkv, hidden,
                core_in, x_out, x_in, low_out, low_in, high_out, high_in,
                grads, h_out, h_in, part_out, part_in,
                gsem, wsem, cs, cr, xs, xr, ls, lr, us, ur, hs, hr, ps, pr):
    me, z, x, c = coords()
    head = lax.axis_index("head")
    rows, share = x_ref.shape
    dim = nh * share
    hq = q_ref.shape[1]
    width = wk_ref.shape[1]
    kvh = width // HEAD_DIM
    per_group = hq // width
    scale = HEAD_DIM ** (-0.5)

    def kv_load(g, kind):
        at = pl.ds(pl.multiple_of(kind * width + g * HEAD_DIM, HEAD_DIM), HEAD_DIM)
        return pltpu.make_async_copy(kv_hbm.at[:, at], kv_ref.at[:, at], gsem.at[kind, g])

    for g in range(kvh):
        kv_load(g, 0).start()
        kv_load(g, 1).start()
    loads = [
        pltpu.make_async_copy(a, b, wsem.at[i])
        for i, (a, b) in enumerate(((wq_ref, wq), (wk_ref, wk), (wv_ref, wv)))
    ]
    for load in loads:
        load.start()
    enter(nz, nh)
    place, owner = pq_ref[:, 0:1], pq_ref[:, 1:2]
    allowed = (owner == pk_ref[1:2, :]) & (pk_ref[0:1, :] <= place)
    bias[...] = jnp.where(allowed, 0.0, -1e30)

    def lanes(start, size):
        return pl.ds(pl.multiple_of(start, HEAD_DIM), size)

    def part(g, slot):
        return (g, slice(None), pl.ds(pl.multiple_of(slot * rows, rows), rows), slice(None))

    def remote(src, dst, ss, rs, target):
        return pltpu.make_async_remote_copy(
            src_ref=src, dst_ref=dst, send_sem=ss, recv_sem=rs, device_id=target,
            device_id_type=MESH)

    beside = {"ctx": slot_of(z, x, 1 - c)}
    across = {"ctx": slot_of(z, 1 - x, c)}
    right = {"ctx": slot_of(z + 1, x, c)}
    left = {"ctx": slot_of(z - 1, x, c)}

    def core_copy(g, k, zz):
        xx = 1 - x if k == 0 else x
        return remote(dkv.at[part(g, slot_of(zz, xx, 1 - c))], core_in.at[g, k, zz],
                      cs.at[g, k, zz], cr.at[g, k, zz], beside)

    def x_copy(g, zz):
        return remote(x_out.at[g, zz], x_in.at[g, zz], xs.at[g, zz], xr.at[g, zz], across)

    def up_copy(g, zz):
        return remote(high_out.at[g, zz], high_in.at[g, zz], us.at[g, zz], ur.at[g, zz], right)

    def down_copy(g, zz):
        return remote(low_out.at[g, zz], low_in.at[g, zz], ls.at[g, zz], lr.at[g, zz], left)

    def target_of(i):
        if i == nz - 1:
            return z
        high = nz - 1 - i - jnp.where(i >= nz - 1 - z, 1, 0)
        low = i + jnp.where(i >= z, 1, 0)
        return jnp.where(z < nz // 2, high, low)

    def cross(g):
        for i in range(nz):
            zz = target_of(i)
            core_copy(g, 0, zz).wait_recv()
            x_out[g, zz] = (dkv[part(g, slot_of(zz, 1 - x, c))].astype(F32)
                            + core_in[g, 0, zz].astype(F32)).astype(BF16)
            x_copy(g, zz).start()

    def local_sum(g, zz):
        core_copy(g, 1, zz).wait_recv()
        x_copy(g, zz).wait_recv()
        return (dkv[part(g, slot_of(zz, x, c))].astype(F32) + core_in[g, 1, zz].astype(F32)
                + x_in[g, zz].astype(F32))

    def tick(g, tau):
        @pl.when(z <= tau)
        def _():
            zz = nz - 1 - tau + z
            high_out[g, zz] = local_sum(g, zz).astype(BF16)

            @pl.when(z > 0)
            def _():
                up_copy(g, zz).wait_recv()
                high_out[g, zz] = (high_out[g, zz].astype(F32)
                                   + high_in[g, zz].astype(F32)).astype(BF16)

            up_copy(g, zz).start()

        @pl.when(nz - 1 - z <= tau)
        def _():
            zz = tau - (nz - 1 - z)
            low_out[g, zz] = local_sum(g, zz).astype(BF16)

            @pl.when(z < nz - 1)
            def _():
                down_copy(g, zz).wait_recv()
                low_out[g, zz] = (low_out[g, zz].astype(F32)
                                  + low_in[g, zz].astype(F32)).astype(BF16)

            down_copy(g, zz).start()

    def settle(g):
        at = lanes(g * HEAD_DIM, HEAD_DIM)
        grads[:, :, at] = local_sum(g, z)

        @pl.when(z > 0)
        def _():
            up_copy(g, z).wait_recv()
            grads[:, :, at] = grads[:, :, at] + high_in[g, z].astype(F32)

        @pl.when(z < nz - 1)
        def _():
            down_copy(g, z).wait_recv()
            grads[:, :, at] = grads[:, :, at] + low_in[g, z].astype(F32)

    def attend(g, h):
        k = kv_ref[:, lanes(g * HEAD_DIM, HEAD_DIM)]
        v = kv_ref[:, lanes(width + g * HEAD_DIM, HEAD_DIM)]
        cols = lanes((g * per_group + h) * HEAD_DIM, HEAD_DIM)
        band = slice(h * rows, (h + 1) * rows)
        q, do = q_ref[:, cols], do_ref[:, cols]
        s = lax.dot_general(q, k, NT, preferred_element_type=F32) * scale + bias[...]
        e = jnp.exp(s - jnp.max(s, axis=1, keepdims=True))
        p = e * (1.0 / jnp.sum(e, axis=1, keepdims=True))
        half = p.astype(BF16)
        p_all[band, :] = half
        attended = jnp.dot(half, v, preferred_element_type=F32).astype(BF16)
        delta = jnp.sum(do.astype(F32) * attended.astype(F32), axis=1, keepdims=True)
        dp = lax.dot_general(do, v, NT, preferred_element_type=F32)
        ds = (p * (dp - delta) * scale).astype(BF16)
        ds_all[band, :] = ds
        dq[:, cols] = jnp.dot(ds, k, preferred_element_type=F32).astype(BF16)

    def group_grads(g):
        heads = [lanes((g * per_group + h) * HEAD_DIM, HEAD_DIM) for h in range(per_group)]
        qs = jnp.concatenate([q_ref[:, at] for at in heads], axis=0)
        dos = jnp.concatenate([do_ref[:, at] for at in heads], axis=0)
        dk = lax.dot_general(qs, ds_all[...], TN, preferred_element_type=F32)
        dkv[g, 0] = dk.astype(BF16).T
        dv = lax.dot_general(dos, p_all[...], TN, preferred_element_type=F32)
        dkv[g, 1] = dv.astype(BF16).T
        for kind in range(2):
            for i in range(nz):
                core_copy(g, kind, target_of(i)).start()

    tile = 512
    tiles = dim // tile

    def h_tile(t, carry):
        at = pl.ds(pl.multiple_of(t * tile, tile), tile)
        hidden[:, at] = lax.dot_general(dq[...], wq[at, :], NT, preferred_element_type=F32)
        return carry

    def step(t, carry):
        @pl.when(t < kvh)
        def _():
            kv_load(t, 0).wait()
            kv_load(t, 1).wait()
            for h in range(per_group // 2):
                attend(t, h)

        @pl.when(t == kvh)
        def _():
            loads[0].wait()

        @pl.when(t >= kvh)
        def _():
            e = t - kvh
            lax.fori_loop(tiles * e // (nz + 1), tiles * (e + 1) // (nz + 1), h_tile, 0)

        for stage in range(1, nz + 2):
            g = t - stage

            @pl.when((g >= 0) & (g < kvh))
            def _():
                if stage == 1:
                    cross(g)
                elif stage <= nz:
                    tick(g, stage - 2)
                else:
                    settle(g)

        @pl.when(t < kvh)
        def _():
            for h in range(per_group // 2, per_group):
                attend(t, h)
            group_grads(t)

        return carry

    lax.fori_loop(0, kvh + nz + 1, step, 0)
    loads[1].wait()
    loads[2].wait()

    def finish(start):
        at = pl.ds(pl.multiple_of(start, chunk), chunk)
        return (hidden[:, at]
                + lax.dot_general(grads[0].astype(BF16), wk[at, :], NT, preferred_element_type=F32)
                + lax.dot_general(grads[1].astype(BF16), wv[at, :], NT, preferred_element_type=F32))

    per = share // chunk

    def h_copy(p, k):
        return remote(h_out.at[p - 1, k], h_in.at[p - 1, k], hs.at[p - 1, k], hr.at[p - 1, k],
                      {"head": lax.rem(head + p, nh)})

    for p in range(1, nh):
        for k in range(per):
            h_out[p - 1, k] = finish(lax.rem(head + p, nh) * share + k * chunk).astype(BF16)
            h_copy(p, k).start()
    inv = stat_ref[:, 0:1]
    product = stat_ref[:, 128:129]
    squares = stat_ref[:, 256:257]
    for k in range(per):
        hidden[:, k * chunk:(k + 1) * chunk] = finish(head * share + k * chunk)
    inner = jnp.zeros((rows, 1), F32)
    for k in range(per):
        cols = slice(k * chunk, (k + 1) * chunk)
        grad = hidden[:, cols]
        for p in range(1, nh):
            h_copy(p, k).wait_recv()
            grad = grad + h_in[p - 1, k].astype(F32)
        scaled = grad * gain_ref[:, pl.ds(pl.multiple_of(head * share + k * chunk, chunk), chunk)]
        hidden[:, cols] = scaled
        inner = inner + jnp.sum(scaled * (x_ref[:, cols].astype(F32) * inv), axis=1, keepdims=True)
    part_out[...] = jnp.broadcast_to(inner, part_out.shape)

    def p_copy(p):
        return remote(part_out, part_in.at[p - 1], ps.at[p - 1], pr.at[p - 1],
                      {"head": lax.rem(head + p, nh)})

    for p in range(1, nh):
        p_copy(p).start()
    for p in range(1, nh):
        p_copy(p).wait_recv()
        inner = inner + part_in[p - 1][:, 0:1]
    saliency = product + inner - (inner / dim) * squares
    sal_ref[...] = jnp.broadcast_to(saliency, (rows, 128)).T[0:1, :]
    inner = inner / dim
    for k in range(per):
        cols = slice(k * chunk, (k + 1) * chunk)
        unit = x_ref[:, cols].astype(F32) * inv
        out_ref[:, cols] = (dy_ref[:, cols].astype(F32)
                            + (hidden[:, cols] - unit * inner) * inv).astype(BF16)

    def drain(g, carry):
        for zz in range(nz):
            core_copy(g, 0, zz).wait_send()
            core_copy(g, 1, zz).wait_send()
            x_copy(g, zz).wait_send()
            pl.when(z < zz)(lambda zz=zz: up_copy(g, zz).wait_send())
            pl.when(z > zz)(lambda zz=zz: down_copy(g, zz).wait_send())
        return carry

    lax.fori_loop(0, kvh, drain, 0)
    for p in range(1, nh):
        for k in range(per):
            h_copy(p, k).wait_send()
        p_copy(p).wait_send()


def back(nz, nh, pq, pk, q, do, kv, x, dy, gain, stat, wq, wk, wv):
    rows, share = x.shape
    width = wk.shape[1]
    kvh = width // HEAD_DIM
    length = kv.shape[0]
    wide = q.shape[1] // kvh
    dim = nh * share
    chunk = min(512, share)
    per = share // chunk
    piece = (kvh, nz, 2, rows, HEAD_DIM)
    dma = pltpu.SemaphoreType.DMA
    peers = max(1, nh - 1)
    hops = dma((kvh, nz))
    return pl.pallas_call(
        functools.partial(back_kernel, nz, nh, chunk),
        out_shape=(
            jax.ShapeDtypeStruct((rows, share), BF16),
            jax.ShapeDtypeStruct((1, rows), F32),
        ),
        in_specs=[VM] * 4 + [ANY] + [VM] * 4 + [ANY] * 3,
        out_specs=(VM, VM),
        scratch_shapes=[
            pltpu.VMEM(kv.shape, BF16),
            pltpu.VMEM(wq.shape, BF16), pltpu.VMEM(wk.shape, BF16), pltpu.VMEM(wv.shape, BF16),
            pltpu.VMEM((rows, length), F32),
            pltpu.VMEM((wide // HEAD_DIM * rows, length), BF16),
            pltpu.VMEM((wide // HEAD_DIM * rows, length), BF16),
            pltpu.VMEM(q.shape, BF16),
            pltpu.VMEM((kvh, 2, length, HEAD_DIM), BF16),
            pltpu.VMEM((rows, dim), F32),
            pltpu.VMEM((kvh, 2, nz, 2, rows, HEAD_DIM), BF16),
            pltpu.VMEM(piece, BF16), pltpu.VMEM(piece, BF16),
            pltpu.VMEM(piece, BF16), pltpu.VMEM(piece, BF16),
            pltpu.VMEM(piece, BF16), pltpu.VMEM(piece, BF16),
            pltpu.VMEM((2, rows, width), F32),
            pltpu.VMEM((peers, per, rows, chunk), BF16),
            pltpu.VMEM((peers, per, rows, chunk), BF16),
            pltpu.VMEM((rows, 128), F32), pltpu.VMEM((peers, rows, 128), F32),
            dma((2, kvh)), dma((3,)), dma((kvh, 2, nz)), dma((kvh, 2, nz)),
            hops, hops, hops, hops, hops, hops,
            dma((peers, per)), dma((peers, per)), dma((peers,)), dma((peers,)),
        ],
        compiler_params=pltpu.CompilerParams(
            collective_id=1, has_side_effects=True, vmem_limit_bytes=VMEM_LIMIT),
        name="back",
    )(pq, pk, q, do, kv, x, dy, gain, stat, wq, wk, wv)


def fused_kernel(nz, order_hbm, lengths_hbm, x_ref, dy_ref, gain_hbm,
                 wq_ref, wk_ref, wv_ref, wo_ref, out_ref, sal_ref,
                 wq, wk, wv, wo, xall, dyall, xg, acc_kv, acc2, inv_ref, vx,
                 kv_own, kvs, q_out, do_out, qs, dos, qt, dot_, bias, ee, acc_o, m_run, stat,
                 dq_own, part, up_in, down_in, dkvr,
                 h_in, part_out, part_in, gain_ref, order_ref, lengths_ref,
                 isem, wsem, lsem, xs, xr, dys, dyr, ks, kr, zus, zds, zr, qsem, qr, dsem, dr,
                 us, ur, ls, lr, gs, gr, fs, fr, hs, hr, ps, pr):
    me, z, x, c = coords()
    head = lax.axis_index("head")
    rows, share = x_ref.shape
    dim = 2 * share
    width = wk_ref.shape[1]
    slab = SLAB * rows
    wide = wq_ref.shape[1] // SLAB
    per_group = wide // HEAD_DIM
    rc = rows // HALVES
    block = SLAB * rc
    kv = 2 * HEAD_DIM
    scale = HEAD_DIM ** (-0.5)
    j = x * 2 + c
    gg = wo.at[:, 0:block]
    dq_slab = wo.at[0:slab, block:block + wide]
    peer = 1 - head
    mine = pl.ds(pl.multiple_of(head * share, share), share)
    theirs = pl.ds(pl.multiple_of(peer * share, share), share)

    own = [
        pltpu.make_async_copy(x_ref, xall.at[head], lsem.at[0]),
        pltpu.make_async_copy(dy_ref, dyall.at[head], lsem.at[1]),
    ]
    small = [pltpu.make_async_copy(a, b, isem.at[i]) for i, (a, b) in enumerate(
        ((order_hbm, order_ref), (lengths_hbm, lengths_ref), (gain_hbm, gain_ref)))]
    for copy in small:
        copy.start()
    own[0].start()
    load_k = pltpu.make_async_copy(wk_ref, wk, wsem.at[0])
    load_v = pltpu.make_async_copy(wv_ref, wv, wsem.at[1])
    load_q = [pltpu.make_async_copy(wq_ref.at[at, :], wq.at[at, :], wsem.at[2 + i])
              for i, at in enumerate((mine, theirs))]
    load_o = [pltpu.make_async_copy(wo_ref.at[:, at], wo, wsem.at[4 + i])
              for i, at in enumerate((mine, theirs))]
    load_k.start()
    load_v.start()
    own[1].start()

    def member(p):
        xx = x if p < 2 else 1 - x
        cc = c if p % 2 == 0 else 1 - c
        return xx, cc, xx * 2 + cc

    barrier = pltpu.get_barrier_semaphore()

    def greet(target):
        pl.semaphore_signal(barrier, inc=1, device_id=target, device_id_type=MESH)

    greet({"head": peer})
    for p in range(1, SLAB):
        greet({"ctx": slot_of(z, *member(p)[:2])})
    pl.when(z > 0)(lambda: greet({"ctx": slot_of(z - 1, x, c)}))
    pl.when(z < nz - 1)(lambda: greet({"ctx": slot_of(z + 1, x, c)}))

    @pl.when((z > 0) & (z < nz - 1))
    def _():
        pl.semaphore_wait(barrier, SLAB + 2)

    @pl.when((z == 0) | (z == nz - 1))
    def _():
        pl.semaphore_wait(barrier, SLAB + 1)

    def remote(src, dst, ss, rs, target):
        return pltpu.make_async_remote_copy(
            src_ref=src, dst_ref=dst, send_sem=ss, recv_sem=rs, device_id=target,
            device_id_type=MESH)

    def to_member(p, src, dst, ss, rs):
        xx, cc, _ = member(p)
        return remote(src, dst, ss, rs, {"ctx": slot_of(z, xx, cc)})

    right = {"ctx": slot_of(z + 1, x, c)}
    left = {"ctx": slot_of(z - 1, x, c)}

    def span(start, size):
        return pl.ds(pl.multiple_of(start, size), size)

    def x_copy(a):
        at = slice(a * rc, (a + 1) * rc)
        return remote(xall.at[head, at, :], xall.at[head, at, :], xs.at[a], xr.at[a], {"head": peer})

    tile = wide
    fd = min(1024, share)
    feats = share // fd

    def dy_copy(f):
        at = slice(f * fd, (f + 1) * fd)
        return remote(dyall.at[head, :, at], dyall.at[head, :, at], dys.at[f], dyr.at[f], {"head": peer})

    own[0].wait()
    for a in range(HALVES):
        x_copy(a).start()
    own[1].wait()
    for f in range(feats):
        dy_copy(f).start()
    for copy in small:
        copy.wait()
    load_q[0].start()
    load_o[0].start()
    load_q[1].start()

    def make_bias():
        vx[:, HEAD_DIM:kv] = jnp.ones((slab, HEAD_DIM), BF16)
        place_q, owner_q = timeline_place(
            lax.broadcasted_iota(jnp.int32, (slab, 1), 0) + z * slab, order_ref, lengths_ref)
        lane = lax.broadcasted_iota(jnp.int32, (1, nz * slab), 1)
        chunk_bits = rc.bit_length() - 1
        row_in = lane & (rc - 1)
        member_in = jnp.right_shift(lane, chunk_bits) & (SLAB - 1)
        half_in = jnp.right_shift(lane, chunk_bits + 2) & (HALVES - 1)
        slab_in = jnp.right_shift(lane, slab.bit_length() - 1)
        place_k, owner_k = timeline_place(
            slab_in * slab + member_in * rows + half_in * rc + row_in, order_ref, lengths_ref)
        for zz in range(nz):
            for a in range(HALVES):
                at = slice(zz * slab + a * block, zz * slab + (a + 1) * block)
                allowed = (owner_q == owner_k[:, at]) & (place_k[:, at] <= place_q)
                bias[zz, :, a * block:(a + 1) * block] = jnp.where(allowed, 0.0, -1e30).astype(BF16)

    def squares(v):
        return jnp.sum(v * v, axis=1, keepdims=True)

    def kv_own_half():
        v = xall[head].astype(F32)
        inv_ref[:, 2:3] = squares(v)
        xg[head] = (v * gain_ref[:, mine]).astype(BF16)
        load_k.wait()
        acc_kv[0] = jnp.dot(xg[head], wk[mine, :], preferred_element_type=F32)
        load_v.wait()
        acc_kv[1] = jnp.dot(xg[head], wv[mine, :], preferred_element_type=F32)

    def q_half(t, carry):
        at = span(t * tile, tile)
        acc2[0, :, at] = jnp.dot(xg[head], wq[mine, at], preferred_element_type=F32)
        return carry

    def do_half(t, carry):
        at = span(t * tile, tile)
        acc2[1, :, at] = lax.dot_general(dyall[head], wo[at, :], NT, preferred_element_type=F32)
        return carry

    def q_own():
        load_q[0].wait()
        lax.fori_loop(0, SLAB, q_half, 0)

    def do_own(first, last):
        if first == 0:
            load_o[0].wait()
        lax.fori_loop(first, last, do_half, 0)
        if last == SLAB:
            load_o[1].start()

    def kv_copy(p, a):
        jt = member(p)[2]
        dst = kvs.at[z, a, span(j * rc, rc), :]
        return to_member(p, kv_own.at[a, jt], dst, ks.at[a, p], kr.at[a, j])

    def kv_arrived(p, a):
        jt = member(p)[2]
        to_member(p, kv_own.at[a, jt], kvs.at[z, a, span(jt * rc, rc), :],
                  ks.at[a, p], kr.at[a, jt]).wait_recv()

    def make_kv(a):
        x_copy(a).wait_recv()
        at = slice(a * rc, (a + 1) * rc)
        v = xall[peer, at, :].astype(F32)
        total = inv_ref[at, 2:3] + squares(v)
        inv = 1.0 / jnp.sqrt(total / dim + 1e-05)
        inv_ref[at, 0:1] = inv
        inv_ref[at, 1:2] = total * inv * inv
        xg[peer, at, :] = (v * gain_ref[:, theirs]).astype(BF16)
        lhs = xg[peer, at, :]
        for i, w in enumerate((wk, wv)):
            got = (acc_kv[i, at, :] + jnp.dot(lhs, w[theirs, :], preferred_element_type=F32)) * inv
            got = got.astype(BF16)
            for jj in range(SLAB):
                kv_own[a, jj, :, i * HEAD_DIM:(i + 1) * HEAD_DIM] = (
                    got[:, jj * HEAD_DIM:(jj + 1) * HEAD_DIM])
        for p in (2, 3, 1):
            kv_copy(p, a).start()
        kvs[z, a, span(j * rc, rc), :] = kv_own[a, j]

    def piece(zz, a, s):
        return kvs.at[zz, a, span(s * 2 * rc, 2 * rc), :]

    def z_up(zz, a, s):
        return remote(piece(zz, a, s), piece(zz, a, s), zus.at[zz, a, s], zr.at[zz, a, s], right)

    def z_down(zz, a, s):
        return remote(piece(zz, a, s), piece(zz, a, s), zds.at[zz, a, s], zr.at[zz, a, s], left)

    def gather_own(a):
        kv_arrived(1, a)
        for s, peers in ((x, ()), (1 - x, (2, 3))):
            for p in peers:
                kv_arrived(p, a)
            pl.when(z < nz - 1)(lambda s=s: z_up(z, a, s).start())
            pl.when(z > 0)(lambda s=s: z_down(z, a, s).start())

    def order(t):
        near = jnp.where(z < nz // 2, z, nz - 1 - z)
        d = (t + 1) // 2
        o = jnp.where(t <= 2 * near, near + d if t % 2 else near - d, t)
        return jnp.where(z < nz // 2, o, nz - 1 - o)

    def travels(zz):
        return ((zz < z) & (z < nz - 1)) | ((zz > z) & (z > 0))

    def take(t, a):
        zz = order(t)

        @pl.when(travels(zz))
        def _():
            for s in range(2):
                z_up(zz, a, s).wait_recv()
                pl.when(zz < z)(lambda s=s: z_up(zz, a, s).start())
                pl.when(zz > z)(lambda s=s: z_down(zz, a, s).start())

    def keep(t):
        zz = order(t)

        @pl.when(jnp.logical_not(travels(zz)))
        def _():
            for a in range(HALVES):
                for s in range(2):
                    z_up(zz, a, s).wait_recv()

    def shared(p, src, dst, ss, rs):
        jt = member(p)[2]
        return to_member(p, src.at[jt], dst.at[span(j * rows, rows), :], ss.at[p], rs.at[j])

    def shared_arrived(p, src, dst, ss, rs):
        jt = member(p)[2]
        to_member(p, src.at[jt], dst.at[span(jt * rows, rows), :], ss.at[p], rs.at[jt]).wait_recv()

    def q_tile(p):
        jt = member(p)[2]
        at = span(jt * tile, tile)
        got = acc2[0, :, at] + jnp.dot(
            xg[peer], wq[theirs, at], preferred_element_type=F32)
        q_out[jt] = (got * (inv_ref[:, 0:1] * (scale * LOG2E))).astype(BF16)
        if p:
            shared(p, q_out, qs, qsem, qr).start()
        else:
            qs[span(j * rows, rows), :] = q_out[jt]

    def do_part(f, first=0, last=SLAB):
        if f == 0 and first == 0:
            load_o[1].wait()
        if first == 0:
            dy_copy(f).wait_recv()
        at = slice(f * fd, (f + 1) * fd)
        if f < feats - 1:
            def body(t, carry):
                cols = span(t * tile, tile)
                acc2[1, :, cols] = acc2[1, :, cols] + lax.dot_general(
                    dyall[peer, :, at], wo[cols, at], NT, preferred_element_type=F32)
                return carry

            lax.fori_loop(first, last, body, 0)
            return
        for p in (3, 2, 1, 0):
            jt = member(p)[2]
            cols = span(jt * tile, tile)
            do_out[jt] = (acc2[1, :, cols] + lax.dot_general(
                dyall[peer, :, at], wo[cols, at], NT, preferred_element_type=F32)).astype(BF16)
            if p:
                shared(p, do_out, dos, dsem, dr).start()
            else:
                dos[span(j * rows, rows), :] = do_out[jt]

    lane_at = lax.broadcasted_iota(jnp.int32, (slab, HEAD_DIM), 1)

    def forward(t, hook=None):
        zz = order(t)
        vx[:, 0:HEAD_DIM] = kvs[zz, :, :, HEAD_DIM:kv].reshape(slab, HEAD_DIM)
        def one(hh):
            cols = span(hh * HEAD_DIM, HEAD_DIM)
            k = kvs[zz, :, :, 0:HEAD_DIM].reshape(slab, HEAD_DIM)
            s = lax.dot_general(qs[:, cols], k, NT, preferred_element_type=F32)
            s = s + bias[zz].astype(F32)
            m = jnp.broadcast_to(jnp.max(s, axis=1, keepdims=True), (slab, HEAD_DIM))
            if t:
                old = m_run[hh]
                m = jnp.maximum(m, old)
            half = jnp.exp2(s - jnp.concatenate([m] * SLAB, axis=1)).astype(BF16)
            ee[t, span(hh * slab, slab), :] = half
            o = jnp.dot(half, vx[...], preferred_element_type=F32)
            if t:
                alpha = jnp.exp2(old - m)
                o = o + acc_o[hh] * jnp.concatenate([alpha, alpha], axis=1)
            stat[hh] = jnp.where(lane_at == t, m, stat[hh]) if t else m
            m_run[hh] = m
            acc_o[hh] = o

        def pair(i, carry):
            one(2 * i)
            one(2 * i + 1)
            if hook is not None:
                pl.when(i == 0)(hook)
            return carry

        lax.fori_loop(0, per_group // 2, pair, 0)

    def settle():
        def one(hh, carry):
            cols = span(hh * HEAD_DIM, HEAD_DIM)
            do = dos[:, cols]
            inv_l = 1.0 / acc_o[hh, :, HEAD_DIM:kv]
            attended = (acc_o[hh, :, 0:HEAD_DIM] * inv_l).astype(BF16)
            delta = jnp.sum(do.astype(F32) * attended.astype(F32), axis=1, keepdims=True)
            stat[hh] = jnp.where(lane_at == HEAD_DIM - 1, delta, jnp.exp2(stat[hh] - m_run[hh]) * inv_l)
            acc_o[hh, :, 0:HEAD_DIM] = jnp.zeros((slab, HEAD_DIM), F32)
            dot_[:, span(hh * slab, slab)] = do.T
            return carry

        lax.fori_loop(0, per_group, one, 0)

    def turn_q():
        def one(hh, carry):
            qt[:, span(hh * slab, slab)] = qs[:, span(hh * HEAD_DIM, HEAD_DIM)].T
            return carry

        lax.fori_loop(0, per_group, one, 0)

    def backward(t, a):
        zz = order(t)
        half = slice(a * block, (a + 1) * block)

        def one(hh):
            k = kvs[zz, a, :, 0:HEAD_DIM]
            v = kvs[zz, a, :, HEAD_DIM:kv]
            cols = span(hh * HEAD_DIM, HEAD_DIM)
            at = span(hh * slab, slab)
            dp = lax.dot_general(dos[:, cols], v, NT, preferred_element_type=F32)
            p = ee[t, at, half].astype(F32) * stat[hh, :, t:t + 1]
            ee[t, at, half] = p.astype(BF16)
            g = (p * (dp - stat[hh, :, 127:128])).astype(BF16)
            gg[at, :] = g
            acc_o[hh, :, 0:HEAD_DIM] = (acc_o[hh, :, 0:HEAD_DIM]
                                        + jnp.dot(g, k, preferred_element_type=F32))

        def pair(i, carry):
            one(2 * i)
            one(2 * i + 1)
            return carry

        lax.fori_loop(0, per_group // 2, pair, 0)
        dk = jnp.dot(qt[...], gg[...], preferred_element_type=F32) * LN2
        dv = jnp.dot(dot_[...], ee[t, :, half], preferred_element_type=F32)
        part[zz, a, :, 0:HEAD_DIM] = dk.astype(BF16).T
        part[zz, a, :, HEAD_DIM:kv] = dv.astype(BF16).T

    def up_copy(zz, a):
        return remote(part.at[zz, a], up_in.at[zz, a], us.at[zz, a], ur.at[zz, a], right)

    def down_copy(zz, a):
        return remote(part.at[zz, a], down_in.at[zz, a], ls.at[zz, a], lr.at[zz, a], left)

    def send_part(t, a):
        zz = order(t)
        pl.when((zz > z) & (z == 0))(lambda: up_copy(zz, a).start())
        pl.when((zz < z) & (z == nz - 1))(lambda: down_copy(zz, a).start())

    def pass_part(t, a):
        zz = order(t)

        @pl.when((zz > z) & (z > 0))
        def _():
            up_copy(zz, a).wait_recv()
            part[zz, a] = (part[zz, a].astype(F32) + up_in[zz, a].astype(F32)).astype(BF16)
            up_copy(zz, a).start()

        @pl.when((zz < z) & (z < nz - 1))
        def _():
            down_copy(zz, a).wait_recv()
            part[zz, a] = (part[zz, a].astype(F32) + down_in[zz, a].astype(F32)).astype(BF16)
            down_copy(zz, a).start()

    def fin_copy(p, a):
        jt = member(p)[2]
        return to_member(p, kv_own.at[a, jt], dkvr.at[a, j], fs.at[a, p], fr.at[a, j])

    def fin_arrived(p, a):
        jt = member(p)[2]
        to_member(p, kv_own.at[a, jt], dkvr.at[a, jt], fs.at[a, p],
                  fr.at[a, jt]).wait_recv()

    def finish_part(a):
        kv_own[a] = part[z, a].reshape(SLAB, rc, kv)

        @pl.when(z > 0)
        def _():
            up_copy(z, a).wait_recv()
            got = up_in[z, a].reshape(SLAB, rc, kv)
            kv_own[a] = (kv_own[a].astype(F32) + got.astype(F32)).astype(BF16)

        @pl.when(z < nz - 1)
        def _():
            down_copy(z, a).wait_recv()
            got = down_in[z, a].reshape(SLAB, rc, kv)
            kv_own[a] = (kv_own[a].astype(F32) + got.astype(F32)).astype(BF16)

        for p in (3, 2, 1):
            fin_copy(p, a).start()
        dkvr[a, j] = kv_own[a, j]

    def dq_copy(p):
        jt = member(p)[2]
        return to_member(p, wo.at[span(jt * rows, rows), block:block + wide], dq_own.at[:, span(j * tile, tile)],
                         gs.at[p], gr.at[j])

    def dq_arrived(p):
        jt = member(p)[2]
        to_member(p, wo.at[span(jt * rows, rows), block:block + wide], dq_own.at[:, span(jt * tile, tile)],
                  gs.at[p], gr.at[jt]).wait_recv()

    make_bias()
    kv_own_half()
    q_own()
    make_kv(0)
    do_own(0, 2)
    gather_own(0)
    do_own(2, SLAB)
    make_kv(1)
    load_q[1].wait()
    q_tile(3)
    q_tile(2)
    q_tile(1)
    q_tile(0)
    take(1, 0)
    gather_own(1)
    do_part(0, 0, 2)
    for t in range(2, min(3, nz)):
        take(t, 0)
    do_part(0, 2, SLAB)
    for t in range(1, min(3, nz)):
        take(t, 1)
    for p in (1, 2, 3):
        shared_arrived(p, q_out, qs, qsem, qr)

    def far():
        for t in range(3, nz):
            take(t, 0)

    def last():
        for t in range(3, nz):
            take(t, 1)

    forward(0, far)
    for f in range(1, feats):
        do_part(f)
    last()
    keep(1)
    forward(1)
    turn_q()
    for t in range(2, nz):
        keep(t)
        forward(t)
    for p in (1, 2, 3):
        shared_arrived(p, do_out, dos, dsem, dr)
    settle()
    steps = [(nz - 1, a) for a in range(HALVES)]
    steps += [(t, a) for a in range(HALVES) for t in range(nz - 2, 0, -1)]
    steps += [(0, a) for a in range(HALVES)]
    lag = 3
    for i, (t, a) in enumerate(steps):
        backward(t, a)
        if t:
            send_part(t, a)
        if i >= lag and steps[i - lag][0]:
            pass_part(*steps[i - lag])
    for hh in range(per_group):
        dq_slab[:, hh * HEAD_DIM:(hh + 1) * HEAD_DIM] = (acc_o[hh, :, 0:HEAD_DIM] * scale).astype(BF16)
    for p in (3, 2, 1):
        dq_copy(p).start()
    dq_own[:, span(j * tile, tile)] = dq_slab[span(j * rows, rows), :]
    for step in steps[len(steps) - lag:]:
        if step[0]:
            pass_part(*step)
    for p in (1, 2, 3):
        shared(p, q_out, qs, qsem, qr).wait_send()
        for a in range(HALVES):
            kv_copy(p, a).wait_send()
    product = jnp.zeros((rows, 1), F32)
    for h in range(2):
        product = product + jnp.sum(
            xall[h].astype(F32) * dyall[h].astype(F32), axis=1, keepdims=True)
    dq_arrived(1)
    hidden = acc2
    h_out = q_out
    chunk = min(512, share)
    per = share // chunk

    def h_tile(half, start, size, add):
        heads_at = pl.ds(pl.multiple_of(start * tile, tile), size * tile)

        def body(k, carry):
            at = span(half * share + k * chunk, chunk)
            cols = span(k * chunk, chunk)
            got = lax.dot_general(dq_own[:, heads_at], wq[at, heads_at], NT,
                                  preferred_element_type=F32)
            hidden[half, :, cols] = hidden[half, :, cols] + got if add else got
            return carry

        lax.fori_loop(0, per, body, 0)

    h_tile(peer, 2 * x, 2, False)
    finish_part(0)
    finish_part(1)
    dq_arrived(3)
    h_tile(peer, member(3)[2], 1, True)
    dq_arrived(2)
    h_tile(peer, member(2)[2], 1, True)
    for a in range(HALVES):
        for p in (1, 2, 3):
            fin_arrived(p, a)
    grads = [
        jnp.concatenate(
            [jnp.concatenate([dkvr[a, jj, :, i * HEAD_DIM:(i + 1) * HEAD_DIM] for jj in range(SLAB)],
                             axis=1) for a in range(HALVES)], axis=0)
        for i in range(2)
    ]

    def finish(half, k):
        at = span(half * share + k * chunk, chunk)
        return (hidden[half, :, k * chunk:(k + 1) * chunk]
                + lax.dot_general(grads[0], wk[at, :], NT, preferred_element_type=F32)
                + lax.dot_general(grads[1], wv[at, :], NT, preferred_element_type=F32))

    def h_copy(k):
        return remote(h_out.at[k], h_in.at[k], hs.at[k], hr.at[k], {"head": peer})

    inv = inv_ref[:, 0:1]
    inner = jnp.zeros((rows, 1), F32)

    def weighed(half, k, grad):
        scaled = grad * gain_ref[:, span(half * share + k * chunk, chunk)]
        unit = xall[half, :, k * chunk:(k + 1) * chunk].astype(F32) * inv
        return jnp.sum(scaled * unit, axis=1, keepdims=True)

    for k in range(per):
        grad = finish(peer, k)
        h_out[k] = grad.astype(BF16)
        h_copy(k).start()
        inner = inner + weighed(peer, k, grad)
    h_tile(head, 2 * x, 2, False)
    h_tile(head, 2 * (1 - x), 2, True)
    for k in range(per):
        grad = finish(head, k)
        hidden[head, :, k * chunk:(k + 1) * chunk] = grad
        inner = inner + weighed(head, k, grad)
    part_out[...] = jnp.broadcast_to(inner, (rows, 128)).T[0:8, :]
    p_copy = remote(part_out, part_in, ps, pr, {"head": peer})
    p_copy.start()
    p_copy.wait_recv()
    inner = inner + jnp.broadcast_to(part_in[0:1, :], (128, rows)).T[:, 0:1]
    saliency = product + inner - (inner / dim) * inv_ref[:, 1:2]
    sal_ref[...] = jnp.broadcast_to(saliency, (rows, 128)).T[0:1, :]
    inner = inner / dim
    for k in range(per):
        cols = slice(k * chunk, (k + 1) * chunk)
        unit = xall[head, :, cols].astype(F32) * inv
        h_copy(k).wait_recv()
        grad = hidden[head, :, cols] + h_in[k].astype(F32)
        scaled = grad * gain_ref[:, span(head * share + k * chunk, chunk)]
        out_ref[:, cols] = (dyall[head, :, cols].astype(F32)
                            + (scaled - unit * inner) * inv).astype(BF16)

    for a in range(HALVES):
        x_copy(a).wait_send()
        for p in (1, 2, 3):
            fin_copy(p, a).wait_send()
        for zz in range(nz):
            pl.when(z < zz)(lambda zz=zz, a=a: up_copy(zz, a).wait_send())
            pl.when(z > zz)(lambda zz=zz, a=a: down_copy(zz, a).wait_send())
            for s in range(2):
                pl.when((zz <= z) & (z < nz - 1))(lambda zz=zz, a=a, s=s: z_up(zz, a, s).wait_send())
                pl.when((zz >= z) & (z > 0))(lambda zz=zz, a=a, s=s: z_down(zz, a, s).wait_send())
    for f in range(feats):
        dy_copy(f).wait_send()
    for p in (1, 2, 3):
        shared(p, do_out, dos, dsem, dr).wait_send()
        dq_copy(p).wait_send()
    for k in range(per):
        h_copy(k).wait_send()
    p_copy.wait_send()


def fused(nz, order, lengths, x, dy, gain, wq, wk, wv, wo):
    rows, share = x.shape
    dim = 2 * share
    hq, width = wq.shape[1], wk.shape[1]
    wide = hq // SLAB
    heads = wide // HEAD_DIM
    rc = rows // HALVES
    slab = SLAB * rows
    block = SLAB * rc
    kv = 2 * HEAD_DIM
    fd = min(1024, share)
    chunk = min(512, share)
    per = share // chunk
    feats = share // fd
    dma = pltpu.SemaphoreType.DMA
    vm = pltpu.VMEM
    return pl.pallas_call(
        functools.partial(fused_kernel, nz),
        out_shape=(
            jax.ShapeDtypeStruct((rows, share), BF16),
            jax.ShapeDtypeStruct((1, rows), F32),
        ),
        in_specs=[ANY] * 9,
        out_specs=(VM, VM),
        scratch_shapes=[
            vm(wq.shape, BF16), vm(wk.shape, BF16), vm(wv.shape, BF16), vm((hq, share), BF16),
            vm((2, rows, share), BF16), vm((2, rows, share), BF16), vm((2, rows, share), BF16),
            vm((2, rows, width), F32), vm((2, rows, share), F32), vm((rows, 128), F32),
            vm((slab, kv), BF16),
            vm((HALVES, SLAB, rc, kv), BF16), vm((nz, HALVES, block, kv), BF16),
            vm((SLAB, rows, wide), BF16), vm((SLAB, rows, wide), BF16),
            vm((slab, wide), BF16), vm((slab, wide), BF16),
            vm((HEAD_DIM, heads * slab), BF16), vm((HEAD_DIM, heads * slab), BF16),
            vm((nz, slab, slab), BF16),
            vm((nz, heads * slab, slab), BF16),
            vm((heads, slab, kv), F32), vm((heads, slab, HEAD_DIM), F32), vm((heads, slab, 128), F32),
            vm((rows, hq), BF16),
            vm((nz, HALVES, block, kv), BF16), vm((nz, HALVES, block, kv), BF16),
            vm((nz, HALVES, block, kv), BF16),
            vm((HALVES, SLAB, rc, kv), BF16),
            vm((per, rows, chunk), BF16),
            vm((8, rows), F32), vm((8, rows), F32),
            vm((1, dim), F32), pltpu.SMEM(order.shape, jnp.int32), pltpu.SMEM(lengths.shape, jnp.int32),
            dma((3,)), dma((6,)), dma((2,)), dma((HALVES,)), dma((HALVES,)), dma((feats,)), dma((feats,)),
            dma((HALVES, SLAB)), dma((HALVES, SLAB)),
            dma((nz, HALVES, 2)), dma((nz, HALVES, 2)), dma((nz, HALVES, 2)),
            dma((SLAB,)), dma((SLAB,)), dma((SLAB,)), dma((SLAB,)),
            dma((nz, HALVES)), dma((nz, HALVES)), dma((nz, HALVES)), dma((nz, HALVES)),
            dma((SLAB,)), dma((SLAB,)), dma((HALVES, SLAB)), dma((HALVES, SLAB)),
            dma((per,)), dma((per,)), dma(()), dma(()),
        ],
        compiler_params=pltpu.CompilerParams(
            collective_id=2, has_side_effects=True, vmem_limit_bytes=VMEM_LIMIT),
        name="fused",
    )(order, lengths, x, dy, gain, wq, wk, wv, wo)


def local(inputs, out_grad, norm_gain, w_query, w_key, w_value, w_out, record_lengths, block_order):
    rows, share = inputs.shape
    n = lax.axis_size("ctx")
    nh = lax.axis_size("head")
    nz = n // 4
    gain = norm_gain[None, :]
    if nh == 2 and w_key.shape[1] == SLAB * HEAD_DIM and inputs.shape[1] == w_query.shape[1]:
        input_grad, saliency = fused(
            nz, block_order, record_lengths, inputs, out_grad, gain, w_query, w_key, w_value, w_out)
        return (input_grad, saliency.reshape(rows))
    q, do, kv, stat, pq, pk = front(
        nz, nh, block_order, record_lengths, inputs, out_grad, gain,
        w_query, w_key, w_value, w_out)
    input_grad, saliency = back(
        nz, nh, pq, pk, q, do, kv, inputs, out_grad, gain, stat, w_query, w_key, w_value)
    return (input_grad, saliency.reshape(rows))


def solution(mesh):
    placed = (
        P("ctx", "head"),
        P("ctx", "head"),
        P(),
        P(None, "head"),
        P(None, "head"),
        P(None, "head"),
        P("head", None),
        P(),
        P(),
    )
    return jax.shard_map(
        local, mesh=mesh, in_specs=placed, out_specs=(P("ctx", "head"), P("ctx")), check_vma=False
    )
```
